32 devices in a mesh: blk: 8 (over y, x, core), grp: 4 (over z).
Axes of the slice: x: 2, y: 2, z: 4, core: 2. Of those that a mesh axis runs over, the one named last changes fastest.
Arguments:
- depth: float32 [256, 128, 128], P(('blk', 'grp')), may hold values from 0.2 to 1
- cell_dx: float32 [256, 128, 128], P(('blk', 'grp')), may hold values from 0.6 to 1.5
- cell_dy: float32 [256, 128, 128], P(('blk', 'grp')), may hold values from 0.6 to 1.5
- forcing: float32 [256, 128, 128], P(('blk', 'grp')), may hold values from -6 to 6
- land_mask: int32 [256, 128, 128], P(('blk', 'grp')), may hold values 0 or 1
- dest_block: int32 [256], P(('blk', 'grp')), may hold values from -1 to 127, as said below
- source_slot: int32 [128], P(('blk', 'grp')), may hold values from 0 to 255, as said below
- neighbours: int32 [128, 8], P(('blk', 'grp')), may hold values from -1 to 127, as said below
Outputs:
- solution: float32 [128, 128, 128], P(('blk', 'grp'))
- residual: float32 [128, 128, 128], P(('blk', 'grp'))
The draws below stay inside these ranges and needn't reach their ends.
Inputs may be any that keep to these rules, and one draw needn't show every extreme that they name: `dest_block`: every ocean block is held by exactly one old slot; a block's old and new owners share their index on grp and lie in the same aligned group of four indices on blk. One device's live slots send at most 4 blocks to any one device; in every band some devices hold no block and some have all 8 slots live. `source_slot`: the inverse of dest_block. North and south neighbours lie on devices with the same index on grp; east, north-east and south-east neighbours on the device with the same index on blk and the next index on grp, cyclically; west, north-west and south-west ones on the previous index on grp.
All inputs are finite; a program needn't handle non-finite values. No bound on the sum of `land_mask` on one device may be relied on, other than what follows from the above.
Results may differ from the reference program's by a relative error of at most 0.000034.
Values sent between devices are 32-bit elements; how exact they have to be, the bound alone decides.
A program may use at most 64 MiB of HBM per device.

```python
import math
import jax
import jax.numpy as jnp

SIDE = 128
BX = 128
BLK_DEV = 4
SWEEPS = 4
CAP = 8
NB = 128
SLOTS = 256
N_BLK = 8
N_GRP = 4


def move_plan(count):
    new_list = []
    old_list = []
    rank_list = []
    within_list = []
    taken = [0, 0, 0, 0]
    for target in range(4):
        for within in range(count):
            if target == 1:
                anchor = 0
            elif target == 0:
                anchor = 3 if within == 0 else 0
            elif target == 2:
                anchor = 3 if within == 0 else 2
            else:
                anchor = 0 if within == 0 else 2 if within == 1 else 3
            new_list.append(target)
            old_list.append(anchor)
            rank_list.append(taken[anchor])
            within_list.append(within)
            taken[anchor] = taken[anchor] + 1
    return (new_list, old_list, rank_list, within_list)


def block_layout(key):
    base = jax.random.fold_in(key, 11)
    windows = N_BLK // 4
    new_list, old_list, rank_list, within_list = move_plan(BLK_DEV)
    new_pos = jnp.array(new_list, dtype=jnp.int32)[None, None, :]
    old_pos = jnp.array(old_list, dtype=jnp.int32)[None, None, :]
    ranks = jnp.array(rank_list, dtype=jnp.int32)[None, None, :]
    within = jnp.array(within_list, dtype=jnp.int32)[None, None, :]
    masks = jax.random.randint(jax.random.fold_in(base, 1), (N_GRP, windows, 1), 0, 4, dtype=jnp.int32)
    window_base = 4 * jnp.arange(windows, dtype=jnp.int32)[None, :, None]
    new_owner = window_base + jnp.bitwise_xor(new_pos, masks)
    old_owner = window_base + jnp.bitwise_xor(old_pos, masks)
    slot_keys = jax.random.split(jax.random.fold_in(base, 3), N_BLK * N_GRP)
    orders = jax.vmap(lambda one_key: jax.random.permutation(one_key, CAP))(slot_keys).astype(jnp.int32).reshape(N_BLK, N_GRP, CAP)
    shape = (N_GRP, windows, 4 * BLK_DEV)
    band_full = jnp.broadcast_to(jnp.arange(N_GRP, dtype=jnp.int32)[:, None, None], shape)
    within_full = jnp.broadcast_to(within, shape)
    rank_full = jnp.broadcast_to(ranks, shape)
    slot_old = orders[old_owner, band_full, rank_full]
    new_id = ((new_owner * N_GRP + band_full) * BLK_DEV + within_full).reshape(-1).astype(jnp.int32)
    old_id = ((old_owner * N_GRP + band_full) * CAP + slot_old).reshape(-1).astype(jnp.int32)
    source = jnp.zeros((NB,), jnp.int32).at[new_id].set(old_id)
    dest = jnp.full((SLOTS,), -1, jnp.int32).at[old_id].set(new_id)
    return (source, dest)


def draw_source_slot(key, part):
    return block_layout(key)[0]


def draw_dest_block(key, part):
    return block_layout(key)[1]


def draw_neighbours(key, part):
    base = jax.random.fold_in(key, 23)
    owner_new = jnp.arange(N_BLK, dtype=jnp.int32)[:, None, None, None]
    band = jnp.arange(N_GRP, dtype=jnp.int32)[None, :, None, None]
    shape = (N_BLK, N_GRP, BLK_DEV, 8)
    far_owner = jax.random.randint(jax.random.fold_in(base, 1), shape, 0, N_BLK, dtype=jnp.int32)
    far_slot = jax.random.randint(jax.random.fold_in(base, 2), shape, 0, BLK_DEV, dtype=jnp.int32)
    gaps = jax.random.randint(jax.random.fold_in(base, 3), shape, 0, 5, dtype=jnp.int32)
    east_band = (band + 1) % N_GRP
    west_band = (band + N_GRP - 1) % N_GRP
    polar = (far_owner * N_GRP + band) * BLK_DEV + far_slot
    eastern = (owner_new * N_GRP + east_band) * BLK_DEV + far_slot
    western = (owner_new * N_GRP + west_band) * BLK_DEV + far_slot
    ids = jnp.stack((polar[..., 0], polar[..., 1], eastern[..., 2], western[..., 3], eastern[..., 4], western[..., 5], eastern[..., 6], western[..., 7]), axis=-1)
    ids = jnp.where(gaps == 0, -1, ids)
    return ids.reshape(NB, 8).astype(jnp.int32)


def plant(values, key, smallest, high):
    longest = values.shape.index(max(values.shape))
    spots = []
    for shift in (0, 1):
        where = [jax.random.randint(jax.random.fold_in(key, axis), (), 0, length) for axis, length in enumerate(values.shape)]
        where[longest] = (where[longest] + shift) % values.shape[longest]
        spots.append(tuple(where))
    return values.at[spots[0]].set(smallest).at[spots[1]].set(high)


def steps_of(own_key, dims, cuts, smallest, top_value):
    level, own = 1.0, jax.random.fold_in(own_key, 6)
    for axis_at, blocks in cuts:
        heights = jnp.exp(jax.random.uniform(jax.random.fold_in(own, axis_at), (blocks,), jnp.float32, smallest / len(cuts), top_value / len(cuts)))
        level = level * jnp.repeat(heights, dims[axis_at] // blocks).reshape([-1 if axis == axis_at else 1 for axis in range(len(dims))])
    return level


def gaussian(stream_key, shape, spread, bound, cuts=(), kind=jnp.bfloat16):
    factor_of = steps_of(stream_key, shape, cuts, -0.22, 0.18) if cuts else 1.0
    drawn = jax.random.normal(stream_key, shape, jnp.float32) * spread * factor_of
    return jnp.minimum(jnp.maximum(drawn, -bound), bound).astype(kind)


def setup_inputs(seed: int = 0) -> dict:
    keys = jax.random.split(jax.random.key(seed), 9)
    depth = jnp.clip(0.2 + 0.8 * jax.random.uniform(keys[0], (SLOTS, BX, SIDE), jnp.float32) ** steps_of(keys[0], (SLOTS, BX, SIDE), ((0, 32),), -0.2, 0.2), 0.2, 1.0)
    cell_dx = jnp.clip(jnp.exp(math.log(1.5) - 0.9162907 * jax.random.uniform(keys[1], (SLOTS, BX, SIDE), jnp.float32) ** steps_of(keys[1], (SLOTS, BX, SIDE), ((0, 32),), -0.2, 0.2)), 0.6, 1.5)
    cell_dy = jnp.clip(jnp.exp(math.log(1.5) - 0.9162907 * jax.random.uniform(keys[2], (SLOTS, BX, SIDE), jnp.float32) ** steps_of(keys[2], (SLOTS, BX, SIDE), ((0, 32),), -0.2, 0.2)), 0.6, 1.5)
    forcing = gaussian(keys[3], (SLOTS, BX, SIDE), 1.0, 6.0, ((0, 32),), jnp.float32)
    land_mask = plant((jax.random.randint(keys[4], (SLOTS, BX, SIDE), 0, 5) < 4).astype(jnp.int32), jax.random.fold_in(keys[4], 1), 0, 1)
    dest_block = draw_dest_block(jax.random.fold_in(keys[8], 71), 0)
    source_slot = draw_source_slot(jax.random.fold_in(keys[8], 71), 0)
    neighbours = draw_neighbours(jax.random.fold_in(keys[8], 71), 0)
    return {"depth": depth, "cell_dx": cell_dx, "cell_dy": cell_dy, "forcing": forcing, "land_mask": land_mask, "dest_block": dest_block, "source_slot": source_slot, "neighbours": neighbours}


tau_mass = 6.0
low_bound = 0.2
high_bound = 1.9


def coefficients(ocean_depth, cell_dx, cell_dy):
    ratio_x = cell_dy / cell_dx
    ratio_y = cell_dx / cell_dy
    coef_x = ocean_depth * ratio_x
    coef_y = ocean_depth * ratio_y
    coef_c = 0.125 * ocean_depth * (ratio_x + ratio_y)
    coef_d = 2.0 * coef_x + 2.0 * coef_y + 4.0 * coef_c + tau_mass * cell_dx * cell_dy
    return coef_x, coef_y, coef_c, coef_d


def combine(iterate, coefs, north_row, south_row, west_col, east_col, north_west, north_east, south_west, south_east):
    coef_x, coef_y, coef_c, coef_d = coefs
    top_pad = jnp.concatenate((north_west[:, None], north_row, north_east[:, None]), axis=1)
    bottom_pad = jnp.concatenate((south_west[:, None], south_row, south_east[:, None]), axis=1)
    middle = jnp.concatenate((west_col[:, :, None], iterate, east_col[:, :, None]), axis=2)
    padded = jnp.concatenate((top_pad[:, None, :], middle, bottom_pad[:, None, :]), axis=1)
    from_north = padded[:, :-2, 1:-1]
    from_south = padded[:, 2:, 1:-1]
    from_west = padded[:, 1:-1, :-2]
    from_east = padded[:, 1:-1, 2:]
    diagonal = padded[:, :-2, :-2] + padded[:, :-2, 2:] + padded[:, 2:, :-2] + padded[:, 2:, 2:]
    return coef_d * iterate - coef_x * (from_east + from_west) - coef_y * (from_north + from_south) - coef_c * diagonal


def apply_operator(iterate, coefs, neighbours):
    present = neighbours >= 0
    safe_ids = jnp.where(present, neighbours, 0).astype(jnp.int32)
    top_rows = iterate[:, 0, :]
    bottom_rows = iterate[:, -1, :]
    left_cols = iterate[:, :, 0]
    right_cols = iterate[:, :, -1]
    north_row = jnp.where(present[:, 0, None], bottom_rows[safe_ids[:, 0]], 0.0)
    south_row = jnp.where(present[:, 1, None], top_rows[safe_ids[:, 1]], 0.0)
    east_col = jnp.where(present[:, 2, None], left_cols[safe_ids[:, 2]], 0.0)
    west_col = jnp.where(present[:, 3, None], right_cols[safe_ids[:, 3]], 0.0)
    north_east = jnp.where(present[:, 4], bottom_rows[safe_ids[:, 4], 0], 0.0)
    north_west = jnp.where(present[:, 5], bottom_rows[safe_ids[:, 5], -1], 0.0)
    south_east = jnp.where(present[:, 6], top_rows[safe_ids[:, 6], 0], 0.0)
    south_west = jnp.where(present[:, 7], top_rows[safe_ids[:, 7], -1], 0.0)
    return combine(iterate, coefs, north_row, south_row, west_col, east_col, north_west, north_east, south_west, south_east)


def reference(depth, cell_dx, cell_dy, forcing, land_mask, dest_block, source_slot, neighbours):
    ocean_mask = land_mask.astype(depth.dtype)
    ocean_depth = depth * ocean_mask
    source_old = forcing * ocean_mask
    old_coefs = coefficients(ocean_depth, cell_dx, cell_dy)
    coefs = tuple(field[source_slot] for field in old_coefs)
    target = jnp.where(dest_block >= 0, dest_block, NB).astype(jnp.int32)
    source = jnp.zeros((NB, BX, SIDE), depth.dtype).at[target].set(source_old, mode="drop")
    coef_d = coefs[3]
    scale_alpha = 2.0 / (high_bound - low_bound)
    scale_beta = (high_bound + low_bound) / (high_bound - low_bound)
    scale_gamma = scale_beta / scale_alpha
    relax_weight = 2.0 / scale_gamma
    update = source / (scale_gamma * coef_d)
    solution = update
    residual = source - apply_operator(solution, coefs, neighbours)
    for sweep in range(SWEEPS - 1):
        relax_weight = 1.0 / (scale_gamma - relax_weight / (4.0 * scale_alpha ** 2))
        update = relax_weight * residual / coef_d + (scale_gamma * relax_weight - 1.0) * update
        solution = solution + update
        residual = source - apply_operator(solution, coefs, neighbours)
    return solution, residual
```

```python
import functools

import jax
import jax.numpy as jnp
from jax import lax
from jax.experimental import pallas as pl
from jax.experimental.pallas import tpu as pltpu
from jax.sharding import PartitionSpec as P

SWEEPS = 4
TAU_MASS = 6.0
LOW_BOUND = 0.2
HIGH_BOUND = 1.9
CHUNK = 32
PAD = 8
MESH = pl.DeviceIdType.MESH
EXACT = lax.Precision.HIGHEST


def relax_weights():
    alpha = 2.0 / (HIGH_BOUND - LOW_BOUND)
    beta = (HIGH_BOUND + LOW_BOUND) / (HIGH_BOUND - LOW_BOUND)
    gamma = beta / alpha
    weight = 2.0 / gamma
    weights = []
    for _ in range(SWEEPS - 1):
        weight = 1.0 / (gamma - weight / (4.0 * alpha**2))
        weights.append((weight, gamma * weight - 1.0))
    return gamma, weights


def kernel(
    owners,
    bands,
    depth_hbm,
    dx_hbm,
    dy_hbm,
    forcing_hbm,
    mask_hbm,
    dest_smem,
    dest_row,
    neigh,
    sol_out,
    res_out,
    depth_v,
    dx_v,
    dy_v,
    forcing_v,
    mask_v,
    coef_x,
    coef_y,
    coef_d,
    inv_d,
    source,
    update,
    field,
    resid,
    table,
    band_tables,
    side_tables,
    pick_rows,
    pick_cols,
    edge_rows,
    edge_cols,
    band_rows,
    side_cols,
    col_tile,
    row_coefs,
    col_coefs,
    inner_cols,
    filled,
    halo_cols,
    find,
    have,
    half_out,
    half_in,
    pair_out,
    pair_in,
    cross_out,
    cross_in,
    load_sems,
    row_send,
    row_recv,
    col_send,
    col_recv,
    move_send,
    move_recv,
):
    slots, height, width = depth_v.shape
    blocks = neigh.shape[0]
    me = lax.axis_index("blk")
    band = lax.axis_index("grp")
    core = me % 2
    sibling = me + 1 - 2 * core
    base = me - me % 4
    inner = me % 4
    east_band = (band + 1) % bands
    west_band = (band + bands - 1) % bands
    half = height // 2

    loads = [
        pltpu.make_async_copy(src, dst, load_sems.at[i])
        for i, (src, dst) in enumerate(
            (
                (dx_hbm, dx_v),
                (dy_hbm, dy_v),
                (depth_hbm, depth_v),
                (mask_hbm, mask_v),
                (forcing_hbm, forcing_v),
            )
        )
    ]
    for load in loads:
        load.start()

    barrier = pltpu.get_barrier_semaphore()
    for step in range(4):
        for side in (east_band, west_band):
            pl.semaphore_signal(
                barrier,
                inc=1,
                device_id=(base + (inner + step) % 4, side),
                device_id_type=MESH,
            )
    for step in range(1, owners):
        pl.semaphore_signal(
            barrier, inc=1, device_id=((me + step) % owners, band), device_id_type=MESH
        )

    table[...] = jnp.zeros_like(table)
    table[0:blocks, 0:8] = (neigh[...] + 1).astype(jnp.float32)
    table[blocks : blocks + 1, 0:slots] = (dest_row[...] + 1).astype(jnp.float32)
    band_tables[0] = table[...]

    targets = (me, sibling, (base + (inner + 2) % 4), (base + (sibling % 4 + 2) % 4))
    for t, target in enumerate(targets):
        for j in range(blocks):
            wanted = (target * bands + band) * blocks + j
            place = jnp.int32(0)
            count = jnp.int32(0)
            for s in range(slots):
                hit = dest_smem[s] == wanted
                place = jnp.where(hit, s, place)
                count = jnp.where(hit, 1, count)
            find[t * blocks + j] = place
            have[t * blocks + j] = count.astype(jnp.float32)

    gamma, weights = relax_weights()
    lane = lax.broadcasted_iota(jnp.int32, (CHUNK, width), 1)
    first_lane = lane == 0
    last_lane = lane == width - 1

    def put_columns(at, s, r0, value, deep):
        rows = pl.ds(r0, CHUNK)
        right = pltpu.roll(value, at + 1 + deep + s, 1)
        left = pltpu.roll(value, at + slots - deep + s, 1)
        tile = jnp.where(lane == at + s, right, col_tile[rows, :])
        col_tile[rows, :] = jnp.where(lane == at + slots + s, left, tile)

    col_tile[...] = jnp.zeros_like(col_tile)
    for load in loads:
        load.wait()

    def prepare(s, carry):
        for r0 in range(0, height, CHUNK):
            rows = pl.ds(r0, CHUNK)
            ocean = mask_v[s, rows, :].astype(jnp.float32)
            dx = dx_v[s, rows, :]
            dy = dy_v[s, rows, :]
            area = dx * dy
            scaled = depth_v[s, rows, :] * ocean / area
            cx = scaled * (dy * dy)
            cy = scaled * (dx * dx)
            cd = 2.5 * (cx + cy) + TAU_MASS * area
            inv = 1.0 / cd
            src = forcing_v[s, rows, :] * ocean
            start = src * (inv * (1.0 / gamma))
            coef_x[s, rows, :] = cx
            coef_y[s, rows, :] = cy
            coef_d[s, rows, :] = cd
            inv_d[s, rows, :] = inv
            source[s, rows, :] = src
            update[s, rows, :] = start
            field[0, s, pl.ds(PAD + r0, CHUNK), :] = start
            parts = (cx, cy, cd, inv, src, start, start)
            for i, part in enumerate(parts):
                put_columns(2 * slots * i, s, r0, part, 1 if i == 6 else 0)
        return carry

    lax.fori_loop(0, slots, prepare, 0)
    col_coefs[...] = col_tile[...].T
    inner_cols[...] = col_coefs[12 * slots : 14 * slots, :]
    filled[...] = jnp.zeros_like(filled)
    for i, ref in enumerate((coef_x, coef_y, coef_d, inv_d, source, update)):
        for s in range(slots):
            row_coefs[i, s : s + 1, :] = ref[s, 0:1, :]
            row_coefs[i, slots + s : slots + s + 1, :] = ref[s, height - 1 : height, :]
    edge_rows[0] = row_coefs[5]
    edge_cols[0] = col_coefs[10 * slots : 12 * slots, :]

    def send_tables():
        for step in range(4):
            for slot, side in ((step, west_band), (4 + step, east_band)):
                pltpu.make_async_remote_copy(
                    src_ref=table,
                    dst_ref=side_tables.at[slot],
                    send_sem=col_send.at[SWEEPS],
                    recv_sem=col_recv.at[SWEEPS],
                    device_id=(base + (inner + step) % 4, side),
                    device_id_type=MESH,
                ).start()
        for step in range(1, owners):
            pltpu.make_async_remote_copy(
                src_ref=table,
                dst_ref=band_tables.at[owners - step],
                send_sem=row_send.at[SWEEPS],
                recv_sem=row_recv.at[SWEEPS],
                device_id=((me + step) % owners, band),
                device_id_type=MESH,
            ).start()

    def send_cols(k):
        for step in range(4):
            for slot, part, side in ((step, slots, west_band), (4 + step, 0, east_band)):
                pltpu.make_async_remote_copy(
                    src_ref=edge_cols.at[k, pl.ds(part, slots)],
                    dst_ref=side_cols.at[k, slot],
                    send_sem=col_send.at[k],
                    recv_sem=col_recv.at[k],
                    device_id=(base + (inner + step) % 4, side),
                    device_id_type=MESH,
                ).start()

    def send_rows(k):
        for step in range(1, owners):
            pltpu.make_async_remote_copy(
                src_ref=edge_rows.at[k],
                dst_ref=band_rows.at[k, owners - step],
                send_sem=row_send.at[k],
                recv_sem=row_recv.at[k],
                device_id=((me + step) % owners, band),
                device_id_type=MESH,
            ).start()
        band_rows[k, 0] = edge_rows[k]

    def take(ref, sem):
        pltpu.make_async_copy(ref, ref, sem).wait()

    def build_picks():
        take(band_tables.at[pl.ds(1, owners - 1)], row_recv.at[SWEEPS])
        take(side_tables, col_recv.at[SWEEPS])
        lanes = lax.broadcasted_iota(jnp.int32, (2 * slots, width), 1)
        rows = lax.broadcasted_iota(jnp.int32, (2 * slots, width), 0)
        lower = rows >= slots
        mine = jnp.broadcast_to(table[blocks : blocks + 1, :], (2 * slots, width))
        own = jnp.sum(jnp.where(lanes == rows % slots, mine, 0.0), axis=1, keepdims=True)
        group_ids = ((base + lanes // 8) * bands + band) * blocks + lanes % 8 + 1
        known = (lanes % 8 < blocks) & (lanes < 32)
        match = jnp.where(known & (own == group_ids.astype(jnp.float32)), 1.0, 0.0)
        listed = jnp.concatenate(
            [band_tables[(base + g - me + owners) % owners] for g in range(4)], axis=0
        )
        need = jnp.dot(
            match[:, :32], listed, precision=EXACT, preferred_element_type=jnp.float32
        )
        low = lax.broadcasted_iota(jnp.int32, (8, width), 1) < slots
        per_tile = width // (2 * slots)
        wanted = jnp.where(lower, need[:, 1:2], need[:, 0:1])
        for q in range(owners // per_tile):
            ids = jnp.zeros((8, width), jnp.float32)
            for d in range(per_tile):
                tile = jnp.where(low, band_tables[q * per_tile + d], 0.0)
                twice = tile + pltpu.roll(tile, slots, 1)
                ids = ids + (pltpu.roll(twice, 2 * slots * d, 1) if d else twice)
            id_row = jnp.broadcast_to(ids[blocks : blocks + 1, :], (2 * slots, width))
            bottom = (lanes % (2 * slots)) // slots == 1
            good = (wanted == id_row) & (id_row > 0.0) & (bottom != lower)
            pick_rows[:, q * width : (q + 1) * width] = jnp.where(good, 1.0, 0.0)
        ids = jnp.zeros((8, width), jnp.float32)
        for d in range(8):
            tile = jnp.where(low, side_tables[d], 0.0)
            ids = ids + (pltpu.roll(tile, slots * d, 1) if d else tile)
        id_row = jnp.broadcast_to(ids[blocks : blocks + 1, :], (2 * slots, width))
        western = lanes >= 4 * slots
        for i, (east_of, west_of) in enumerate(((2, 3), (4, 5), (6, 7))):
            wanted = jnp.where(
                lower, need[:, west_of : west_of + 1], need[:, east_of : east_of + 1]
            )
            good = (wanted == id_row) & (id_row > 0.0) & (western == lower)
            pick_cols[2 * slots * i : 2 * slots * (i + 1), :] = jnp.where(good, 1.0, 0.0)

    def take_edges(k):
        take(band_rows.at[k, pl.ds(1, owners - 1)], row_recv.at[k])
        per_tile = width // (2 * slots)
        got = jnp.zeros((2 * slots, width), jnp.float32)
        for q in range(owners // per_tile):
            got = got + jnp.dot(
                pick_rows[:, q * width : (q + 1) * width],
                band_rows[k, q * per_tile : (q + 1) * per_tile].reshape(width, width),
                precision=EXACT,
                preferred_element_type=jnp.float32,
            )
        take(side_cols.at[k], col_recv.at[k])
        count = 8 * slots
        cols = jnp.dot(
            pick_cols[:, 0:count],
            side_cols[k].reshape(count, width),
            precision=EXACT,
            preferred_element_type=jnp.float32,
        )
        lanes = lax.broadcasted_iota(jnp.int32, (2 * slots, width), 1)
        straight = cols[0 : 2 * slots]
        above = jnp.where(lanes == width - 1, cols[2 * slots : 4 * slots], straight)
        below = jnp.where(lanes == 0, cols[4 * slots : 6 * slots], straight)
        slanted = pltpu.roll(above, 1, 1) + pltpu.roll(below, width - 1, 1)
        return got, straight, slanted

    def put_halo(k, got, straight, slanted):
        now = k % 2
        for s in range(slots):
            field[now, s, PAD - 1 : PAD, :] = got[s : s + 1, :]
            field[now, s, PAD + height : PAD + height + 1, :] = got[slots + s : slots + s + 1, :]
        for i, tile in enumerate((straight, slanted)):
            for h in range(2):
                filled[pl.ds(2 * slots * i + h, slots, stride=2), :] = tile[
                    slots * h : slots * (h + 1)
                ]
        halo_cols[...] = filled[...].T

    def stencil(coefs, center, level, vertical, slant):
        cx, cy, cd, inv, src = (coefs[i] for i in range(5))
        slant = 0.125 * slant
        return (src - cd * center + cx * (level + slant) + cy * (vertical + slant)) * inv

    def ring(k, got, straight, slanted):
        now = k % 2
        weight, keep = weights[k]
        lanes = lax.broadcasted_iota(jnp.int32, (2 * slots, width), 1)
        start = lanes == 0
        end = lanes == width - 1

        def spread(value, before, after):
            left = jnp.where(start, before, pltpu.roll(value, 1, 1))
            return left + jnp.where(end, after, pltpu.roll(value, width - 1, 1))

        def ends(tile, at):
            part = tile[at : at + slots]
            return jnp.concatenate([part[:, 0:1], part[:, width - 1 : width]], axis=0)

        def sides(at, deep):
            part = got[at : at + slots]
            last = width - 1 - deep
            return jnp.concatenate([part[:, last : last + 1], part[:, deep : deep + 1]], axis=0)

        center = edge_cols[k]
        inside = inner_cols[...]
        level = inside + straight
        vertical = spread(center, sides(0, 0), sides(slots, 0))
        slant = slanted + spread(inside, sides(0, 1), sides(slots, 1))
        tall = 2 * slots
        coefs = [col_coefs[i * tall : (i + 1) * tall, :] for i in range(5)]
        left = stencil(coefs, center, level, vertical, slant)
        change = weight * left + keep * col_coefs[5 * tall : 6 * tall, :]
        col_coefs[5 * tall : 6 * tall, :] = change
        edge_cols[k + 1] = center + change
        send_cols(k + 1)

        center = edge_rows[k]
        inside = jnp.concatenate(
            [field[now, s, PAD + 1 : PAD + 2, :] for s in range(slots)]
            + [field[now, s, PAD + height - 2 : PAD + height - 1, :] for s in range(slots)],
            axis=0,
        )
        vertical = inside + got
        level = spread(center, ends(straight, slots), ends(straight, 0))
        slant = spread(vertical, ends(slanted, slots), ends(slanted, 0))
        left = stencil([row_coefs[i] for i in range(5)], center, level, vertical, slant)
        change = weight * left + keep * row_coefs[5]
        row_coefs[5] = change
        edge_rows[k + 1] = center + change
        send_rows(k + 1)

    def around(value, halo):
        left = jnp.where(first_lane, halo, pltpu.roll(value, 1, 1))
        right = jnp.where(last_lane, halo, pltpu.roll(value, width - 1, 1))
        return left + right

    def sweep(k, first, stop):
        now = k % 2

        def one(s, carry):
            for r0 in range(0, height, CHUNK):
                rows = pl.ds(r0, CHUNK)
                center = field[now, s, pl.ds(PAD + r0, CHUNK), :]
                north = field[now, s, pl.ds(PAD + r0 - 1, CHUNK), :]
                south = field[now, s, pl.ds(PAD + r0 + 1, CHUNK), :]
                vertical = north + south
                cols = halo_cols[rows, :]
                level = around(center, pltpu.roll(cols, width - 1 - 2 * s, 1))
                slant = around(vertical, pltpu.roll(cols, width - 1 - 2 * slots - 2 * s, 1))
                slant = 0.125 * slant
                left = (
                    source[s, rows, :]
                    - coef_d[s, rows, :] * center
                    + coef_x[s, rows, :] * (level + slant)
                    + coef_y[s, rows, :] * (vertical + slant)
                )
                if k == SWEEPS - 1:
                    resid[s, rows, :] = left
                else:
                    weight, keep = weights[k]
                    change = weight * left * inv_d[s, rows, :] + keep * update[s, rows, :]
                    update[s, rows, :] = change
                    fresh = center + change
                    field[1 - now, s, pl.ds(PAD + r0, CHUNK), :] = fresh
                    put_columns(0, s, r0, fresh, 1)
            return carry

        lax.fori_loop(first, stop, one, 0)
        if k < SWEEPS - 1:
            inner_cols[...] = col_tile[...].T[0 : 2 * slots]

    last = (SWEEPS - 1) % 2

    def rows_of(f, slot, r0, count):
        if f == 0:
            return field[last, slot, pl.ds(PAD + r0, count), :]
        return resid[slot, pl.ds(r0, count), :]

    def start_move(f):
        away = (1 - core) * half

        def fill_half(i, carry):
            slot = find[2 * blocks + i]
            half_out[f, i] = rows_of(f, slot, away, half) * have[2 * blocks + i]
            return carry

        lax.fori_loop(0, 2 * blocks, fill_half, 0)
        pltpu.make_async_remote_copy(
            src_ref=half_out.at[f],
            dst_ref=half_in.at[f],
            send_sem=move_send.at[f, 0],
            recv_sem=move_recv.at[f, 0],
            device_id=(sibling, band),
            device_id_type=MESH,
        ).start()

        def fill_pair(i, carry):
            slot = find[blocks + i]
            pair_out[f, i] = rows_of(f, slot, 0, height) * have[blocks + i]
            return carry

        lax.fori_loop(0, blocks, fill_pair, 0)
        pltpu.make_async_remote_copy(
            src_ref=pair_out.at[f],
            dst_ref=pair_in.at[f],
            send_sem=move_send.at[f, 1],
            recv_sem=move_recv.at[f, 1],
            device_id=(sibling, band),
            device_id_type=MESH,
        ).start()

    def cross_move(f):
        kept = core * half
        take(half_in.at[f], move_recv.at[f, 0])
        for t in range(2):

            def fill(i, carry, t=t):
                slot = find[(2 + t) * blocks + i]
                cross_out[f, t, i] = (
                    rows_of(f, slot, kept, half) * have[(2 + t) * blocks + i]
                    + half_in[f, (1 - t) * blocks + i]
                )
                return carry

            lax.fori_loop(0, blocks, fill, 0)
            pltpu.make_async_remote_copy(
                src_ref=cross_out.at[f, t],
                dst_ref=cross_in.at[f, core],
                send_sem=move_send.at[f, 2 + t],
                recv_sem=move_recv.at[f, 2],
                device_id=(targets[2 + t], band),
                device_id_type=MESH,
            ).start()

    def finish_move(f, out):
        take(pair_in.at[f], move_recv.at[f, 1])

        def near(i, carry):
            out[i] = rows_of(f, find[i], 0, height) * have[i] + pair_in[f, i]
            return carry

        lax.fori_loop(0, blocks, near, 0)
        take(cross_in.at[f], move_recv.at[f, 2])

        def far(i, carry):
            for h in range(2):
                rows = pl.ds(h * half, half)
                out[i, rows, :] = out[i, rows, :] + cross_in[f, h, i]
            return carry

        lax.fori_loop(0, blocks, far, 0)

    pl.semaphore_wait(barrier, owners - 1 + 8)
    send_tables()
    send_cols(0)
    send_rows(0)
    build_picks()
    for k in range(SWEEPS - 1):
        halo = take_edges(k)
        ring(k, *halo)
        put_halo(k, *halo)
        sweep(k, 0, slots)
    start_move(0)
    cross_move(0)
    put_halo(SWEEPS - 1, *take_edges(SWEEPS - 1))
    sweep(SWEEPS - 1, 0, slots)
    start_move(1)
    cross_move(1)
    finish_move(0, sol_out)
    finish_move(1, res_out)

    take(band_tables.at[pl.ds(1, owners - 1)], row_send.at[SWEEPS])
    take(side_tables, col_send.at[SWEEPS])
    for k in range(SWEEPS):
        take(band_rows.at[k, pl.ds(1, owners - 1)], row_send.at[k])
        take(side_cols.at[k], col_send.at[k])
    for f in range(2):
        take(half_out.at[f], move_send.at[f, 0])
        take(pair_out.at[f], move_send.at[f, 1])
        take(cross_out.at[f, 0], move_send.at[f, 2])
        take(cross_out.at[f, 1], move_send.at[f, 3])


def per_device(
    owners, bands, depth, cell_dx, cell_dy, forcing, land_mask, dest_block, source_slot, neighbours
):
    slots, height, width = depth.shape
    blocks = source_slot.shape[0]
    half = height // 2
    f32 = jnp.float32
    any_spec = pl.BlockSpec(memory_space=pl.ANY)
    vmem = pl.BlockSpec(memory_space=pltpu.VMEM)
    whole = pltpu.VMEM((slots, height, width), f32)
    dma = pltpu.SemaphoreType.DMA
    out = pltpu.VMEM((blocks, height, width), f32)
    return pl.pallas_call(
        functools.partial(kernel, owners, bands),
        out_shape=(out, out),
        in_specs=[any_spec] * 5 + [pl.BlockSpec(memory_space=pltpu.SMEM), vmem, vmem],
        out_specs=(vmem, vmem),
        scratch_shapes=[
            whole,
            whole,
            whole,
            whole,
            pltpu.VMEM((slots, height, width), jnp.int32),
            whole,
            whole,
            whole,
            whole,
            whole,
            whole,
            pltpu.VMEM((2, slots, height + 2 * PAD, width), f32),
            whole,
            pltpu.VMEM((8, width), f32),
            pltpu.VMEM((owners, 8, width), f32),
            pltpu.VMEM((8, 8, width), f32),
            pltpu.VMEM((2 * slots, owners * 2 * slots), f32),
            pltpu.VMEM((6 * slots, width), f32),
            pltpu.VMEM((SWEEPS, 2 * slots, width), f32),
            pltpu.VMEM((SWEEPS, 2 * slots, width), f32),
            pltpu.VMEM((SWEEPS, owners, 2 * slots, width), f32),
            pltpu.VMEM((SWEEPS, 8, slots, width), f32),
            pltpu.VMEM((height, width), f32),
            pltpu.VMEM((6, 2 * slots, width), f32),
            pltpu.VMEM((width, height), f32),
            pltpu.VMEM((2 * slots, width), f32),
            pltpu.VMEM((width, height), f32),
            pltpu.VMEM((height, width), f32),
            pltpu.SMEM((4 * blocks,), jnp.int32),
            pltpu.SMEM((4 * blocks,), f32),
            pltpu.VMEM((2, 2 * blocks, half, width), f32),
            pltpu.VMEM((2, 2 * blocks, half, width), f32),
            pltpu.VMEM((2, blocks, height, width), f32),
            pltpu.VMEM((2, blocks, height, width), f32),
            pltpu.VMEM((2, 2, blocks, half, width), f32),
            pltpu.VMEM((2, 2, blocks, half, width), f32),
            dma((5,)),
            dma((SWEEPS + 1,)),
            dma((SWEEPS + 1,)),
            dma((SWEEPS + 1,)),
            dma((SWEEPS + 1,)),
            dma((2, 4)),
            dma((2, 3)),
        ],
        compiler_params=pltpu.CompilerParams(
            collective_id=0, has_side_effects=True, vmem_limit_bytes=56 * 1024 * 1024
        ),
        name="barotropic_solve",
    )(
        depth,
        cell_dx,
        cell_dy,
        forcing,
        land_mask,
        dest_block,
        dest_block.reshape(1, slots),
        neighbours,
    )


def solution(mesh):
    blocks3 = P(("blk", "grp"), None, None)
    flat = P(("blk", "grp"))
    in_specs = (blocks3,) * 5 + (flat, flat, P(("blk", "grp"), None))
    return jax.shard_map(
        functools.partial(per_device, mesh.shape["blk"], mesh.shape["grp"]),
        mesh=mesh,
        in_specs=in_specs,
        out_specs=(blocks3, blocks3),
        check_vma=False,
    )
```

```python
import functools

import jax
import jax.numpy as jnp
from jax import lax
from jax.experimental import pallas as pl
from jax.experimental.pallas import tpu as pltpu
from jax.sharding import PartitionSpec as P

SWEEPS = 4
TAU_MASS = 6.0
LOW_BOUND = 0.2
HIGH_BOUND = 1.9
CHUNK = 32
PAD = 8
TOP = 40
DEEP = TOP + 8
WINDOWS = 3
PART = DEEP // WINDOWS
LATE = ((40, 24), (64, 32), (96, 32))
MESH = pl.DeviceIdType.MESH
EXACT = lax.Precision.HIGHEST


def relax_weights():
    alpha = 2.0 / (HIGH_BOUND - LOW_BOUND)
    beta = (HIGH_BOUND + LOW_BOUND) / (HIGH_BOUND - LOW_BOUND)
    gamma = beta / alpha
    weight = 2.0 / gamma
    weights = []
    for _ in range(SWEEPS - 1):
        weight = 1.0 / (gamma - weight / (4.0 * alpha**2))
        weights.append((weight, gamma * weight - 1.0))
    return gamma, weights


def kernel(
    owners,
    bands,
    depth_hbm,
    dx_hbm,
    dy_hbm,
    forcing_hbm,
    mask_hbm,
    dest_smem,
    dest_row,
    neigh,
    sol_out,
    res_out,
    depth_v,
    dx_v,
    dy_v,
    forcing_v,
    mask_v,
    coef_x,
    coef_y,
    coef_d,
    inv_d,
    source,
    update,
    field,
    resid,
    pick_rows,
    pick_cols,
    first_rows,
    first_cols,
    band_first,
    side_first,
    edge_rows,
    edge_cols,
    band_rows,
    side_cols,
    col_tile,
    row_coefs,
    col_coefs,
    inner_cols,
    filled,
    halo_cols,
    new_top,
    new_coefs,
    new_inv,
    new_update,
    new_field,
    fix_source,
    fix_out,
    fix_in,
    find,
    have,
    near_out,
    near_in,
    far_out,
    far_in,
    late_out,
    late_in,
    cross_out,
    cross_in,
    load_sems,
    row_send,
    row_recv,
    col_send,
    col_recv,
    early_send,
    early_recv,
    late_send,
    late_recv,
    fix_send,
    fix_recv,
):
    slots, height, width = depth_v.shape
    blocks = neigh.shape[0]
    tall = 2 * slots
    me = lax.axis_index("blk")
    band = lax.axis_index("grp")
    core = me % 2
    sibling = me + 1 - 2 * core
    base = me - me % 4
    inner = me % 4
    across = base + (inner + 2) % 4
    east_band = (band + 1) % bands
    west_band = (band + bands - 1) % bands

    loads = [
        pltpu.make_async_copy(src, dst, load_sems.at[i])
        for i, (src, dst) in enumerate(
            (
                (dx_hbm, dx_v),
                (dy_hbm, dy_v),
                (depth_hbm, depth_v),
                (mask_hbm, mask_v),
                (forcing_hbm, forcing_v),
            )
        )
    ]
    for load in loads:
        load.start()

    barrier = pltpu.get_barrier_semaphore()
    for step in range(4):
        for side in (east_band, west_band):
            pl.semaphore_signal(
                barrier,
                inc=1,
                device_id=(base + (inner + step) % 4, side),
                device_id_type=MESH,
            )
    for step in range(1, owners):
        pl.semaphore_signal(
            barrier, inc=1, device_id=((me + step) % owners, band), device_id_type=MESH
        )

    first_rows[tall:, :] = jnp.zeros((8, width), jnp.float32)
    first_rows[tall : tall + blocks, 0:8] = (neigh[...] + 1).astype(jnp.float32)
    first_rows[tall + blocks : tall + blocks + 1, 0:slots] = (dest_row[...] + 1).astype(
        jnp.float32
    )
    table = first_rows[tall:, :]
    first_cols[0, slots:, :] = table
    first_cols[1, slots:, :] = table

    targets = (me, sibling, across, base + (sibling % 4 + 2) % 4)
    for t, target in enumerate(targets):
        for j in range(blocks):
            wanted = (target * bands + band) * blocks + j
            place = jnp.int32(0)
            count = jnp.int32(0)
            for s in range(slots):
                hit = dest_smem[s] == wanted
                place = jnp.where(hit, s, place)
                count = jnp.where(hit, 1, count)
            find[t * blocks + j] = place
            have[t * blocks + j] = count.astype(jnp.float32)

    gamma, weights = relax_weights()
    lane = lax.broadcasted_iota(jnp.int32, (CHUNK, width), 1)

    def put_columns(at, s, r0, value, deep):
        rows = pl.ds(r0, CHUNK)
        right = pltpu.roll(value, at + 1 + deep + s, 1)
        left = pltpu.roll(value, at + slots - deep + s, 1)
        tile = jnp.where(lane == at + s, right, col_tile[rows, :])
        col_tile[rows, :] = jnp.where(lane == at + slots + s, left, tile)

    col_tile[...] = jnp.zeros_like(col_tile)
    for load in loads:
        load.wait()

    def prepare(s, carry):
        for r0 in range(0, height, CHUNK):
            rows = pl.ds(r0, CHUNK)
            ocean = mask_v[s, rows, :].astype(jnp.float32)
            dx = dx_v[s, rows, :]
            dy = dy_v[s, rows, :]
            area = dx * dy
            scaled = depth_v[s, rows, :] * ocean / area
            cx = scaled * (dy * dy)
            cy = scaled * (dx * dx)
            cd = 2.5 * (cx + cy) + TAU_MASS * area
            inv = 1.0 / cd
            src = forcing_v[s, rows, :] * ocean
            start = src * (inv * (1.0 / gamma))
            coef_x[s, rows, :] = cx
            coef_y[s, rows, :] = cy
            coef_d[s, rows, :] = cd
            inv_d[s, rows, :] = inv
            source[s, rows, :] = src
            update[s, rows, :] = start
            field[0, s, pl.ds(PAD + r0, CHUNK), :] = start
            parts = (cx, cy, cd, inv, src, start, start)
            for i, part in enumerate(parts):
                put_columns(tall * i, s, r0, part, 1 if i == 6 else 0)
        return carry

    lax.fori_loop(0, slots, prepare, 0)
    col_coefs[...] = col_tile[...].T
    inner_cols[...] = col_coefs[6 * tall : 7 * tall, :]
    filled[...] = jnp.zeros_like(filled)
    for i, ref in enumerate((coef_x, coef_y, coef_d, inv_d, source, update)):
        for s in range(slots):
            row_coefs[i, s : s + 1, :] = ref[s, 0:1, :]
            row_coefs[i, slots + s : slots + s + 1, :] = ref[s, height - 1 : height, :]
    edge_rows[0] = row_coefs[5]
    edge_cols[0] = col_coefs[5 * tall : 6 * tall, :]
    first_rows[0:tall, :] = row_coefs[5]
    first_cols[0, 0:slots, :] = col_coefs[5 * tall + slots : 6 * tall, :]
    first_cols[1, 0:slots, :] = col_coefs[5 * tall : 5 * tall + slots, :]

    def send_cols(k):
        for step in range(4):
            for slot, part, side in ((step, 0, west_band), (4 + step, 1, east_band)):
                if k == 0:
                    src, dst = first_cols.at[part], side_first.at[slot]
                else:
                    src = edge_cols.at[k, pl.ds((1 - part) * slots, slots)]
                    dst = side_cols.at[k - 1, slot]
                pltpu.make_async_remote_copy(
                    src_ref=src,
                    dst_ref=dst,
                    send_sem=col_send.at[k],
                    recv_sem=col_recv.at[k],
                    device_id=(base + (inner + step) % 4, side),
                    device_id_type=MESH,
                ).start()

    def send_rows(k):
        for step in range(1, owners):
            if k == 0:
                src, dst = first_rows, band_first.at[owners - step]
            else:
                src, dst = edge_rows.at[k], band_rows.at[k - 1, owners - step]
            pltpu.make_async_remote_copy(
                src_ref=src,
                dst_ref=dst,
                send_sem=row_send.at[k],
                recv_sem=row_recv.at[k],
                device_id=((me + step) % owners, band),
                device_id_type=MESH,
            ).start()
        if k == 0:
            band_first[0] = first_rows[...]
        else:
            band_rows[k - 1, 0] = edge_rows[k]

    def take(ref, sem):
        pltpu.make_async_copy(ref, ref, sem).wait()

    def rows_landed(k):
        return (band_first if k == 0 else band_rows.at[k - 1]).at[pl.ds(1, owners - 1)]

    def cols_landed(k):
        return side_first if k == 0 else side_cols.at[k - 1]

    def build_picks():
        lanes = lax.broadcasted_iota(jnp.int32, (tall, width), 1)
        rows = lax.broadcasted_iota(jnp.int32, (tall, width), 0)
        ids_here = first_rows[tall:, :]
        mine = jnp.broadcast_to(ids_here[blocks : blocks + 1, :], (tall, width))
        own = jnp.sum(jnp.where(lanes == rows % slots, mine, 0.0), axis=1, keepdims=True)
        group_ids = ((base + lanes // 8) * bands + band) * blocks + lanes % 8 + 1
        known = (lanes % 8 < blocks) & (lanes < 32)
        match = jnp.where(known & (own == group_ids.astype(jnp.float32)), 1.0, 0.0)
        listed = jnp.concatenate(
            [band_first[(base + g - me + owners) % owners, tall:, :] for g in range(4)], axis=0
        )
        need = jnp.dot(
            match[:, :32], listed, precision=EXACT, preferred_element_type=jnp.float32
        )
        all_rows = tall + 2 * blocks
        lanes = lax.broadcasted_iota(jnp.int32, (all_rows, width), 1)
        rows = lax.broadcasted_iota(jnp.int32, (all_rows, width), 0)
        second = ((rows >= slots) & (rows < tall)) | (rows >= tall + blocks)
        lower = rows[0:tall] >= slots
        low = lax.broadcasted_iota(jnp.int32, (8, width), 1) < slots
        per_tile = width // tall
        wanted = jnp.concatenate(
            [
                jnp.where(lower, need[:, 1:2], need[:, 0:1]),
                jnp.broadcast_to(ids_here[0:blocks, 0:1], (blocks, width)),
                jnp.broadcast_to(ids_here[0:blocks, 1:2], (blocks, width)),
            ],
            axis=0,
        )
        for q in range(owners // per_tile):
            ids = jnp.zeros((8, width), jnp.float32)
            for d in range(per_tile):
                tile = jnp.where(low, band_first[q * per_tile + d, tall:, :], 0.0)
                twice = tile + pltpu.roll(tile, slots, 1)
                ids = ids + (pltpu.roll(twice, tall * d, 1) if d else twice)
            id_row = jnp.broadcast_to(ids[blocks : blocks + 1, :], (all_rows, width))
            bottom = (lanes % tall) // slots == 1
            good = (wanted == id_row) & (id_row > 0.0) & (bottom != second)
            pick_rows[:, q * width : (q + 1) * width] = jnp.where(good, 1.0, 0.0)
        ids = jnp.zeros((8, width), jnp.float32)
        for d in range(8):
            tile = jnp.where(low, side_first[d, slots:, :], 0.0)
            ids = ids + (pltpu.roll(tile, slots * d, 1) if d else tile)
        id_row = jnp.broadcast_to(ids[blocks : blocks + 1, :], (all_rows, width))
        western = lanes >= 4 * slots
        for i, (east_of, west_of) in enumerate(((2, 3), (4, 5), (6, 7))):
            wanted = jnp.concatenate(
                [
                    jnp.where(
                        lower, need[:, west_of : west_of + 1], need[:, east_of : east_of + 1]
                    ),
                    jnp.broadcast_to(ids_here[0:blocks, east_of : east_of + 1], (blocks, width)),
                    jnp.broadcast_to(ids_here[0:blocks, west_of : west_of + 1], (blocks, width)),
                ],
                axis=0,
            )
            good = (wanted == id_row) & (id_row > 0.0) & (western == second)
            pick_cols[all_rows * i : all_rows * (i + 1), :] = jnp.where(good, 1.0, 0.0)

    def take_edges(k):
        all_rows = tall + 2 * blocks
        take(rows_landed(k), row_recv.at[k])
        take(cols_landed(k), col_recv.at[k])
        if k == 0:
            build_picks()
        per_tile = width // tall
        got = jnp.zeros((all_rows, width), jnp.float32)
        for q in range(owners // per_tile):
            part = pl.ds(q * per_tile, per_tile)
            edges = band_first[part, 0:tall, :] if k == 0 else band_rows[k - 1, part]
            got = got + jnp.dot(
                pick_rows[:, q * width : (q + 1) * width],
                edges.reshape(width, width),
                precision=EXACT,
                preferred_element_type=jnp.float32,
            )
        count = 8 * slots
        edges = side_first[:, 0:slots, :] if k == 0 else side_cols[k - 1]
        cols = jnp.dot(
            pick_cols[:, 0:count],
            edges.reshape(count, width),
            precision=EXACT,
            preferred_element_type=jnp.float32,
        )
        lanes = lax.broadcasted_iota(jnp.int32, (all_rows, width), 1)
        straight = cols[0:all_rows]
        above = jnp.where(lanes == width - 1, cols[all_rows : 2 * all_rows], straight)
        below = jnp.where(lanes == 0, cols[2 * all_rows : 3 * all_rows], straight)
        slanted = pltpu.roll(above, 1, 1) + pltpu.roll(below, width - 1, 1)
        return got, straight, slanted

    def put_halo(k, got, straight, slanted):
        now = k % 2
        if k < SWEEPS - 1:
            for s in range(slots):
                field[now, s, PAD - 1 : PAD, :] = got[s : s + 1, :]
                field[now, s, PAD + height : PAD + height + 1, :] = got[
                    slots + s : slots + s + 1, :
                ]
        new_top[k] = got[tall:]
        for i, tile in enumerate((straight, slanted)):
            for h in range(2):
                filled[pl.ds(tall * i + h, slots, stride=2), :] = tile[slots * h : slots * (h + 1)]
                filled[pl.ds(2 * tall + 2 * blocks * i + h, blocks, stride=2), :] = tile[
                    tall + blocks * h : tall + blocks * (h + 1)
                ]
        halo_cols[k] = filled[...].T

    def ring(k, got, straight, slanted):
        now = k % 2
        lanes = lax.broadcasted_iota(jnp.int32, (tall, width), 1)
        start = lanes == 0
        end = lanes == width - 1
        got, straight, slanted = got[0:tall], straight[0:tall], slanted[0:tall]

        def stencil(coefs, center, level, vertical, slant):
            cx, cy, cd, inv, src = (coefs[i] for i in range(5))
            slant = 0.125 * slant
            left = src - cd * center + cx * (level + slant) + cy * (vertical + slant)
            return left if k == SWEEPS - 1 else left * inv

        def spread(value, before, after):
            left = jnp.where(start, before, pltpu.roll(value, 1, 1))
            return left + jnp.where(end, after, pltpu.roll(value, width - 1, 1))

        def ends(tile, at):
            part = tile[at : at + slots]
            return jnp.concatenate([part[:, 0:1], part[:, width - 1 : width]], axis=0)

        def sides(at, deep):
            part = got[at : at + slots]
            last = width - 1 - deep
            return jnp.concatenate([part[:, last : last + 1], part[:, deep : deep + 1]], axis=0)

        center = edge_cols[k]
        inside = inner_cols[...]
        level = inside + straight
        vertical = spread(center, sides(0, 0), sides(slots, 0))
        slant = slanted + spread(inside, sides(0, 1), sides(slots, 1))
        coefs = [col_coefs[i * tall : (i + 1) * tall, :] for i in range(5)]
        left = stencil(coefs, center, level, vertical, slant)
        if k == SWEEPS - 1:
            fix_source[slots:, :] = left
        else:
            weight, keep = weights[k]
            change = weight * left + keep * col_coefs[5 * tall : 6 * tall, :]
            col_coefs[5 * tall : 6 * tall, :] = change
            edge_cols[k + 1] = center + change
            send_cols(k + 1)

        center = edge_rows[k]
        inside = jnp.concatenate(
            [field[now, s, PAD + 1 : PAD + 2, :] for s in range(slots)]
            + [field[now, s, PAD + height - 2 : PAD + height - 1, :] for s in range(slots)],
            axis=0,
        )
        vertical = inside + got
        level = spread(center, ends(straight, slots), ends(straight, 0))
        slant = spread(vertical, ends(slanted, slots), ends(slanted, 0))
        left = stencil([row_coefs[i] for i in range(5)], center, level, vertical, slant)
        if k == SWEEPS - 1:
            fix_source[0:slots, :] = left[slots:]
        else:
            change = weight * left + keep * row_coefs[5]
            row_coefs[5] = change
            edge_rows[k + 1] = center + change
            send_rows(k + 1)

    def around(value, halo):
        at = lax.broadcasted_iota(jnp.int32, value.shape, 1)
        left = jnp.where(at == 0, halo, pltpu.roll(value, 1, 1))
        right = jnp.where(at == width - 1, halo, pltpu.roll(value, width - 1, 1))
        return left + right

    def sweep(k, starts):
        now = k % 2
        weight, keep = weights[k]

        def one(s, carry):
            for r0 in starts:
                rows = pl.ds(r0, CHUNK)
                center = field[now, s, pl.ds(PAD + r0, CHUNK), :]
                north = field[now, s, pl.ds(PAD + r0 - 1, CHUNK), :]
                south = field[now, s, pl.ds(PAD + r0 + 1, CHUNK), :]
                vertical = north + south
                cols = halo_cols[k, rows, :]
                level = around(center, pltpu.roll(cols, width - 1 - 2 * s, 1))
                slant = around(vertical, pltpu.roll(cols, width - 1 - tall - 2 * s, 1))
                slant = 0.125 * slant
                left = (
                    source[s, rows, :]
                    - coef_d[s, rows, :] * center
                    + coef_x[s, rows, :] * (level + slant)
                    + coef_y[s, rows, :] * (vertical + slant)
                )
                change = weight * left * inv_d[s, rows, :] + keep * update[s, rows, :]
                update[s, rows, :] = change
                fresh = center + change
                field[1 - now, s, pl.ds(PAD + r0, CHUNK), :] = fresh
                put_columns(0, s, r0, fresh, 1)
            return carry

        lax.fori_loop(0, slots, one, 0)

    last = (SWEEPS - 1) % 2

    def remainder(r0):
        def one(s, carry):
            rows = pl.ds(r0, CHUNK)
            center = field[last, s, pl.ds(PAD + r0, CHUNK), :]
            vertical = (
                field[last, s, pl.ds(PAD + r0 - 1, CHUNK), :]
                + field[last, s, pl.ds(PAD + r0 + 1, CHUNK), :]
            )
            level = pltpu.roll(center, 1, 1) + pltpu.roll(center, width - 1, 1)
            slant = pltpu.roll(vertical, 1, 1) + pltpu.roll(vertical, width - 1, 1)
            slant = 0.125 * slant
            resid[s, rows, :] = (
                source[s, rows, :]
                - coef_d[s, rows, :] * center
                + coef_x[s, rows, :] * (level + slant)
                + coef_y[s, rows, :] * (vertical + slant)
            )
            return carry

        lax.fori_loop(0, slots, one, 0)

    def send_to(src, dst, sends, recvs, at, device):
        pltpu.make_async_remote_copy(
            src_ref=src,
            dst_ref=dst,
            send_sem=sends.at[at],
            recv_sem=recvs.at[at],
            device_id=(device, band),
            device_id_type=MESH,
        ).start()

    early = (coef_x, coef_y, coef_d, source)

    def early_start(w):
        rows = pl.ds(PART * w, PART)

        def fill(i, carry):
            for t in range(2):
                at = (1 + 2 * t) * blocks + i
                slot, live = find[at], have[at]
                for f, ref in enumerate(early):
                    near_out[w, f, t * blocks + i] = ref[slot, rows, :] * live
            return carry

        lax.fori_loop(0, blocks, fill, 0)
        send_to(near_out.at[w], near_in.at[w], early_send, early_recv, w, sibling)

    def early_cross(w):
        rows = pl.ds(PART * w, PART)
        take(near_in.at[w], early_recv.at[w])

        def fill(i, carry):
            at = 2 * blocks + i
            slot, live = find[at], have[at]
            for f, ref in enumerate(early):
                far_out[w, f, i] = ref[slot, rows, :] * live + near_in[w, f, blocks + i]
            return carry

        lax.fori_loop(0, blocks, fill, 0)
        send_to(far_out.at[w], far_in.at[w], early_send, early_recv, WINDOWS + w, across)

    def early_finish(w):
        rows = pl.ds(PART * w, PART)
        take(far_in.at[w], early_recv.at[WINDOWS + w])

        def fill(i, carry):
            slot, live = find[i], have[i]
            for f, ref in enumerate(early):
                new_coefs[f, i, rows, :] = (
                    ref[slot, rows, :] * live + near_in[w, f, i] + far_in[w, f, i]
                )
            inv = 1.0 / new_coefs[2, i, rows, :]
            new_inv[i, rows, :] = inv
            start = new_coefs[3, i, rows, :] * (inv * (1.0 / gamma))
            new_update[i, rows, :] = start
            new_field[0, i, pl.ds(PAD + PART * w, PART), :] = start
            return carry

        lax.fori_loop(0, blocks, fill, 0)

    def new_sweep(k):
        now = k % 2
        size = DEEP // 2
        for i in range(blocks):
            new_field[now, i, PAD - 1 : PAD, :] = new_top[k, i : i + 1, :]

        def one(i, carry):
            for r0 in range(0, DEEP, size):
                rows = pl.ds(r0, size)
                center = new_field[now, i, pl.ds(PAD + r0, size), :]
                vertical = (
                    new_field[now, i, pl.ds(PAD + r0 - 1, size), :]
                    + new_field[now, i, pl.ds(PAD + r0 + 1, size), :]
                )
                cols = halo_cols[k, rows, :]
                level = around(center, pltpu.roll(cols, width - 1 - 2 * tall - 2 * i, 1))
                slant = around(
                    vertical, pltpu.roll(cols, width - 1 - 2 * tall - 2 * blocks - 2 * i, 1)
                )
                slant = 0.125 * slant
                left = (
                    new_coefs[3, i, rows, :]
                    - new_coefs[2, i, rows, :] * center
                    + new_coefs[0, i, rows, :] * (level + slant)
                    + new_coefs[1, i, rows, :] * (vertical + slant)
                )
                kept = min(size, TOP - r0)
                if k == SWEEPS - 1:
                    res_out[i, pl.ds(r0, kept), :] = left[0:kept]
                else:
                    weight, keep = weights[k]
                    change = weight * left * new_inv[i, rows, :] + keep * new_update[i, rows, :]
                    new_update[i, rows, :] = change
                    fresh = center + change
                    new_field[1 - now, i, pl.ds(PAD + r0, size), :] = fresh
                    if k == SWEEPS - 2:
                        sol_out[i, pl.ds(r0, kept), :] = fresh[0:kept]
            return carry

        lax.fori_loop(0, blocks, one, 0)

    def rows_of(f, slot, r0, count):
        if f == 0:
            return field[last, slot, pl.ds(PAD + r0, count), :]
        return resid[slot, pl.ds(r0, count), :]

    def late_start(f, c):
        r0, count = LATE[c]

        def fill(i, carry):
            for t in range(2):
                at = (1 + 2 * t) * blocks + i
                late_out[c][f, t * blocks + i] = rows_of(f, find[at], r0, count) * have[at]
            return carry

        lax.fori_loop(0, blocks, fill, 0)
        at = f * len(LATE) + c
        send_to(late_out[c].at[f], late_in[c].at[f], late_send, late_recv, at, sibling)

    def late_cross(f, c):
        r0, count = LATE[c]
        at = f * len(LATE) + c
        take(late_in[c].at[f], late_recv.at[at])

        def fill(i, carry):
            at = 2 * blocks + i
            cross_out[c][f, i] = (
                rows_of(f, find[at], r0, count) * have[at] + late_in[c][f, blocks + i]
            )
            return carry

        lax.fori_loop(0, blocks, fill, 0)
        at = at + 2 * len(LATE)
        send_to(cross_out[c].at[f], cross_in[c].at[f], late_send, late_recv, at, across)

    def late_near(f, c, out):
        r0, count = LATE[c]

        def fill(i, carry):
            out[i, pl.ds(r0, count), :] = (
                rows_of(f, find[i], r0, count) * have[i] + late_in[c][f, i]
            )
            return carry

        lax.fori_loop(0, blocks, fill, 0)

    def late_far(f, c, out):
        r0, count = LATE[c]
        take(cross_in[c].at[f], late_recv.at[(2 + f) * len(LATE) + c])

        def fill(i, carry):
            rows = pl.ds(r0, count)
            out[i, rows, :] = out[i, rows, :] + cross_in[c][f, i]
            return carry

        lax.fori_loop(0, blocks, fill, 0)

    def send_fix():
        order = (me, sibling, across, base + (sibling % 4 + 2) % 4)
        fix_out[...] = jnp.zeros_like(fix_out)
        for t in range(4):
            for i in range(blocks):
                slot, live = find[t * blocks + i], have[t * blocks + i]
                east = fix_source[pl.ds(slots + slot, 1), :] * live
                west = fix_source[pl.ds(tall + slot, 1), :] * live
                south = fix_source[pl.ds(slot, 1), :] * live
                fix_out[t, 2 * i : 2 * i + 1, :] = east
                fix_out[t, 2 * i + 1 : 2 * i + 2, :] = west
                fix_out[t, 2 * blocks + i : 2 * blocks + i + 1, :] = south
        for t in range(1, 4):
            send_to(fix_out.at[t], fix_in.at[t - 1], fix_send, fix_recv, t - 1, order[t])

    def put_fix():
        for t in range(3):
            take(fix_in.at[t], fix_recv.at[t])
        total = fix_out[0] + fix_in[0] + fix_in[1] + fix_in[2]
        filled[0 : 4 * blocks, :] = total
        halo_cols[0] = filled[...].T
        count = height - TOP
        rows = pl.ds(TOP, count)
        for i in range(blocks):
            cols = pltpu.roll(halo_cols[0, rows, :], width - 1 - 2 * i, 1)
            at = lax.broadcasted_iota(jnp.int32, (count, width), 1)
            edge = (at == 0) | (at == width - 1)
            res_out[i, rows, :] = jnp.where(edge, cols, res_out[i, rows, :])
            res_out[i, height - 1 : height, :] = total[2 * blocks + i : 2 * blocks + i + 1, :]

    for f in range(2):
        new_field[f] = jnp.zeros(new_field.shape[1:], jnp.float32)

    pl.semaphore_wait(barrier, owners - 1 + 8)
    send_cols(0)
    send_rows(0)
    for w in range(WINDOWS):
        early_start(w)
    early_cross(0)
    whole = tuple(range(0, height, CHUNK))
    for k in range(SWEEPS - 2):
        halo = take_edges(k)
        ring(k, *halo)
        early_cross(k + 1)
        put_halo(k, *halo)
        sweep(k, whole)
        inner_cols[...] = col_tile[...].T[0:tall]
    k = SWEEPS - 2
    halo = take_edges(k)
    ring(k, *halo)
    put_halo(k, *halo)
    steps = len(LATE)
    for c in range(steps):
        sweep(k, (32 * (c + 1),))
        late_start(0, c)
        if c:
            late_cross(0, c - 1)
    inner_cols[...] = col_tile[...].T[0:tall]
    for c in range(steps):
        remainder(32 * (c + 1))
        late_start(1, c)
        if c:
            late_cross(1, c - 1)
        else:
            late_cross(0, steps - 1)
    late_cross(1, steps - 1)
    for w in range(WINDOWS):
        early_finish(w)
    for k in range(SWEEPS - 1):
        new_sweep(k)
    k = SWEEPS - 1
    halo = take_edges(k)
    ring(k, *halo)
    send_fix()
    put_halo(k, *halo)
    new_sweep(k)
    for f, out in enumerate((sol_out, res_out)):
        for c in range(steps):
            late_near(f, c, out)
    for f, out in enumerate((sol_out, res_out)):
        for c in range(steps):
            late_far(f, c, out)
    put_fix()

    for k in range(SWEEPS):
        take(rows_landed(k), row_send.at[k])
        take(cols_landed(k), col_send.at[k])
    for w in range(WINDOWS):
        take(near_out.at[w], early_send.at[w])
        take(far_out.at[w], early_send.at[WINDOWS + w])
    for f in range(2):
        for c in range(steps):
            take(late_out[c].at[f], late_send.at[f * steps + c])
            take(cross_out[c].at[f], late_send.at[(2 + f) * steps + c])
    for t in range(3):
        take(fix_in.at[t], fix_send.at[t])


def per_device(
    owners, bands, depth, cell_dx, cell_dy, forcing, land_mask, dest_block, source_slot, neighbours
):
    slots, height, width = depth.shape
    blocks = source_slot.shape[0]
    tall = 2 * slots
    f32 = jnp.float32
    hbm = pl.BlockSpec(memory_space=pl.ANY)
    vmem = pl.BlockSpec(memory_space=pltpu.VMEM)
    whole = pltpu.VMEM((slots, height, width), f32)
    dma = pltpu.SemaphoreType.DMA

    def tiles(*shape):
        return pltpu.VMEM((*shape, width), f32)

    out = tiles(blocks, height)
    return pl.pallas_call(
        functools.partial(kernel, owners, bands),
        out_shape=(out, out),
        in_specs=[hbm] * 5 + [pl.BlockSpec(memory_space=pltpu.SMEM), vmem, vmem],
        out_specs=(vmem, vmem),
        scratch_shapes=[
            whole,
            whole,
            whole,
            whole,
            pltpu.VMEM((slots, height, width), jnp.int32),
            whole,
            whole,
            whole,
            whole,
            whole,
            whole,
            tiles(2, slots, height + 2 * PAD),
            whole,
            pltpu.VMEM((tall + 2 * blocks, owners * tall), f32),
            tiles(3 * (tall + 2 * blocks)),
            tiles(tall + 8),
            tiles(2, slots + 8),
            tiles(owners, tall + 8),
            tiles(8, slots + 8),
            tiles(SWEEPS, tall),
            tiles(SWEEPS, tall),
            tiles(SWEEPS - 1, owners, tall),
            tiles(SWEEPS - 1, 8, slots),
            tiles(height),
            tiles(6, tall),
            pltpu.VMEM((width, height), f32),
            tiles(tall),
            pltpu.VMEM((width, height), f32),
            tiles(SWEEPS, height),
            tiles(SWEEPS, 2 * blocks),
            tiles(4, blocks, DEEP),
            tiles(blocks, DEEP),
            tiles(blocks, DEEP),
            tiles(2, blocks, DEEP + 2 * PAD),
            tiles(3 * slots),
            tiles(4, 4 * blocks),
            tiles(3, 4 * blocks),
            pltpu.SMEM((4 * blocks,), jnp.int32),
            pltpu.SMEM((4 * blocks,), f32),
            tiles(WINDOWS, 4, 2 * blocks, PART),
            tiles(WINDOWS, 4, 2 * blocks, PART),
            tiles(WINDOWS, 4, blocks, PART),
            tiles(WINDOWS, 4, blocks, PART),
            [tiles(2, 2 * blocks, count) for _, count in LATE],
            [tiles(2, 2 * blocks, count) for _, count in LATE],
            [tiles(2, blocks, count) for _, count in LATE],
            [tiles(2, blocks, count) for _, count in LATE],
            dma((5,)),
            dma((SWEEPS,)),
            dma((SWEEPS,)),
            dma((SWEEPS,)),
            dma((SWEEPS,)),
            dma((2 * WINDOWS,)),
            dma((2 * WINDOWS,)),
            dma((4 * len(LATE),)),
            dma((4 * len(LATE),)),
            dma((3,)),
            dma((3,)),
        ],
        compiler_params=pltpu.CompilerParams(
            collective_id=0, has_side_effects=True, vmem_limit_bytes=56 * 1024 * 1024
        ),
        name="barotropic_solve",
    )(
        depth,
        cell_dx,
        cell_dy,
        forcing,
        land_mask,
        dest_block,
        dest_block.reshape(1, slots),
        neighbours,
    )


def solution(mesh):
    blocks3 = P(("blk", "grp"), None, None)
    flat = P(("blk", "grp"))
    in_specs = (blocks3,) * 5 + (flat, flat, P(("blk", "grp"), None))
    return jax.shard_map(
        functools.partial(per_device, mesh.shape["blk"], mesh.shape["grp"]),
        mesh=mesh,
        in_specs=in_specs,
        out_specs=(blocks3, blocks3),
        check_vma=False,
    )
```

```python
import functools

import jax
import jax.numpy as jnp
from jax import lax
from jax.experimental import pallas as pl
from jax.experimental.pallas import tpu as pltpu
from jax.sharding import PartitionSpec as P

SWEEPS = 4
TAU_MASS = 6.0
LOW_BOUND = 0.2
HIGH_BOUND = 1.9
CHUNK = 32
PAD = 8
GATHER = 16
PAIR = 4
TOP = 40
DEEP = TOP + 8
WINDOWS = 3
PART = DEEP // WINDOWS
LATE = ((40, 24), (64, 32), (96, 32))
MESH = pl.DeviceIdType.MESH
EXACT = lax.Precision.HIGHEST


def relax_weights():
    alpha = 2.0 / (HIGH_BOUND - LOW_BOUND)
    beta = (HIGH_BOUND + LOW_BOUND) / (HIGH_BOUND - LOW_BOUND)
    gamma = beta / alpha
    weight = 2.0 / gamma
    weights = []
    for _ in range(SWEEPS - 1):
        weight = 1.0 / (gamma - weight / (4.0 * alpha**2))
        weights.append((weight, gamma * weight - 1.0))
    return gamma, weights


def kernel(
    owners,
    bands,
    depth_hbm,
    dx_hbm,
    dy_hbm,
    forcing_hbm,
    mask_hbm,
    dest_smem,
    dest_row,
    neigh,
    sol_out,
    res_out,
    depth_v,
    dx_v,
    dy_v,
    forcing_v,
    mask_v,
    coef_x,
    coef_y,
    coef_d,
    inv_d,
    source,
    update,
    field,
    resid,
    pick_rows,
    pick_cols,
    first_rows,
    first_cols,
    band_first,
    side_first,
    edge_rows,
    edge_cols,
    band_rows,
    side_cols,
    col_tile,
    col_turned,
    row_raw,
    row_coefs,
    col_coefs,
    inner_cols,
    filled,
    halo_cols,
    new_top,
    new_coefs,
    new_inv,
    new_update,
    new_field,
    fix_source,
    fix_out,
    fix_in,
    find,
    have,
    near_out,
    near_in,
    far_out,
    far_in,
    late_out,
    late_in,
    cross_out,
    cross_in,
    load_sems,
    row_send,
    row_recv,
    col_send,
    col_recv,
    early_send,
    early_recv,
    late_send,
    late_recv,
    fix_send,
    fix_recv,
):
    slots, height, width = depth_v.shape
    blocks = neigh.shape[0]
    tall = 2 * slots
    me = lax.axis_index("blk")
    band = lax.axis_index("grp")
    core = me % 2
    sibling = me + 1 - 2 * core
    base = me - me % 4
    inner = me % 4
    across = base + (inner + 2) % 4
    east_band = (band + 1) % bands
    west_band = (band + bands - 1) % bands

    loads = [
        pltpu.make_async_copy(src, dst, load_sems.at[i])
        for i, (src, dst) in enumerate(
            (
                (dx_hbm, dx_v),
                (dy_hbm, dy_v),
                (depth_hbm, depth_v),
                (mask_hbm, mask_v),
                (forcing_hbm, forcing_v),
            )
        )
    ]
    for load in loads:
        load.start()

    barrier = pltpu.get_barrier_semaphore()
    for step in range(4):
        for side in (east_band, west_band):
            pl.semaphore_signal(
                barrier,
                inc=1,
                device_id=(base + (inner + step) % 4, side),
                device_id_type=MESH,
            )
    for step in range(1, owners):
        pl.semaphore_signal(
            barrier, inc=1, device_id=((me + step) % owners, band), device_id_type=MESH
        )

    first_rows[tall:, :] = jnp.zeros((8, width), jnp.float32)
    first_rows[tall : tall + blocks, 0:8] = (neigh[...] + 1).astype(jnp.float32)
    first_rows[tall + blocks : tall + blocks + 1, 0:slots] = (dest_row[...] + 1).astype(
        jnp.float32
    )
    table = first_rows[tall:, :]
    first_cols[0, slots:, :] = table
    first_cols[1, slots:, :] = table

    targets = (me, sibling, across, base + (sibling % 4 + 2) % 4)
    for t, target in enumerate(targets):
        for j in range(blocks):
            wanted = (target * bands + band) * blocks + j
            place = jnp.int32(0)
            count = jnp.int32(0)
            for s in range(slots):
                hit = dest_smem[s] == wanted
                place = jnp.where(hit, s, place)
                count = jnp.where(hit, 1, count)
            find[t * blocks + j] = place
            have[t * blocks + j] = count.astype(jnp.float32)

    gamma, weights = relax_weights()

    def coefficients(dx, dy, deep, src):
        area = dx * dy
        scaled = deep / area
        cx = scaled * (dy * dy)
        cy = scaled * (dx * dx)
        cd = 2.5 * (cx + cy) + TAU_MASS * area
        inv = 1.0 / cd
        return cx, cy, cd, inv, src, src * (inv * (1.0 / gamma))

    for load in loads:
        load.wait()

    def gather(r, carry):
        rows = pl.ds(pl.multiple_of(r * GATHER, GATHER), GATHER)
        quad = lax.broadcasted_iota(jnp.int32, (GATHER, width), 1) // 4
        tile = jnp.zeros((GATHER, width), jnp.float32)
        for s in range(slots):
            ocean = mask_v[s, rows, :].astype(jnp.float32)
            parts = (
                dx_v[s, rows, :],
                dy_v[s, rows, :],
                depth_v[s, rows, :] * ocean,
                forcing_v[s, rows, :] * ocean,
            )
            for i, part in enumerate(parts):
                at = i * slots + s
                tile = jnp.where(quad == at, pltpu.roll(part, 2 + 4 * at, 1), tile)
        col_tile[rows, :] = tile
        return carry

    lax.fori_loop(0, height // GATHER, gather, 0)
    col_turned[...] = col_tile[...].T
    for i, ref in enumerate((dx_v, dy_v, depth_v, forcing_v, mask_v)):
        for s in range(slots):
            for at, row in ((s, 0), (slots + s, height - 1)):
                value = ref[s, row : row + 1, :]
                row_raw[i, at : at + 1, :] = value.astype(jnp.float32)
    sides_of = [
        [col_turned[pl.ds(4 * slots * i + c, slots, stride=4), :] for i in range(4)]
        for c in range(4)
    ]
    for i, part in enumerate(
        coefficients(*(jnp.concatenate([e, w], axis=0) for e, w in zip(sides_of[1], sides_of[2])))
    ):
        col_coefs[i * tall : (i + 1) * tall, :] = part
    start = coefficients(
        *(jnp.concatenate([e, w], axis=0) for e, w in zip(sides_of[0], sides_of[3]))
    )[5]
    inner_cols[...] = start
    ocean = row_raw[4]
    for i, part in enumerate(
        coefficients(row_raw[0], row_raw[1], row_raw[2] * ocean, row_raw[3] * ocean)
    ):
        row_coefs[i] = part
    edge_rows[0] = row_coefs[5]
    edge_cols[0] = col_coefs[5 * tall : 6 * tall, :]
    first_rows[0:tall, :] = row_coefs[5]
    first_cols[0, 0:slots, :] = col_coefs[5 * tall + slots : 6 * tall, :]
    first_cols[1, 0:slots, :] = col_coefs[5 * tall : 5 * tall + slots, :]

    def prepare(r0):
        rows = pl.ds(r0, CHUNK)

        def one(s, carry):
            ocean = mask_v[s, rows, :].astype(jnp.float32)
            parts = coefficients(
                dx_v[s, rows, :],
                dy_v[s, rows, :],
                depth_v[s, rows, :] * ocean,
                forcing_v[s, rows, :] * ocean,
            )
            for ref, part in zip((coef_x, coef_y, coef_d, inv_d, source, update), parts):
                ref[s, rows, :] = part
            field[0, s, pl.ds(PAD + r0, CHUNK), :] = parts[5]
            return carry

        lax.fori_loop(0, slots, one, 0)

    def send_cols(k):
        for step in range(4):
            for slot, part, side in ((step, 0, west_band), (4 + step, 1, east_band)):
                if k == 0:
                    src, dst = first_cols.at[part], side_first.at[slot]
                else:
                    src = edge_cols.at[k, pl.ds((1 - part) * slots, slots)]
                    dst = side_cols.at[k - 1, slot]
                pltpu.make_async_remote_copy(
                    src_ref=src,
                    dst_ref=dst,
                    send_sem=col_send.at[k],
                    recv_sem=col_recv.at[k],
                    device_id=(base + (inner + step) % 4, side),
                    device_id_type=MESH,
                ).start()

    def send_rows(k):
        for step in range(1, owners):
            if k == 0:
                src, dst = first_rows, band_first.at[owners - step]
            else:
                src, dst = edge_rows.at[k], band_rows.at[k - 1, owners - step]
            pltpu.make_async_remote_copy(
                src_ref=src,
                dst_ref=dst,
                send_sem=row_send.at[k],
                recv_sem=row_recv.at[k],
                device_id=((me + step) % owners, band),
                device_id_type=MESH,
            ).start()
        if k == 0:
            band_first[0] = first_rows[...]
        else:
            band_rows[k - 1, 0] = edge_rows[k]

    def take(ref, sem):
        pltpu.make_async_copy(ref, ref, sem).wait()

    def rows_landed(k):
        return (band_first if k == 0 else band_rows.at[k - 1]).at[pl.ds(1, owners - 1)]

    def cols_landed(k):
        return side_first if k == 0 else side_cols.at[k - 1]

    def build_picks():
        lanes = lax.broadcasted_iota(jnp.int32, (tall, width), 1)
        rows = lax.broadcasted_iota(jnp.int32, (tall, width), 0)
        ids_here = first_rows[tall:, :]
        mine = jnp.broadcast_to(ids_here[blocks : blocks + 1, :], (tall, width))
        own = jnp.sum(jnp.where(lanes == rows % slots, mine, 0.0), axis=1, keepdims=True)
        group_ids = ((base + lanes // 8) * bands + band) * blocks + lanes % 8 + 1
        known = (lanes % 8 < blocks) & (lanes < 32)
        match = jnp.where(known & (own == group_ids.astype(jnp.float32)), 1.0, 0.0)
        listed = jnp.concatenate(
            [band_first[(base + g - me + owners) % owners, tall:, :] for g in range(4)], axis=0
        )
        need = jnp.dot(
            match[:, :32], listed, precision=EXACT, preferred_element_type=jnp.float32
        )
        all_rows = tall + 2 * blocks
        lanes = lax.broadcasted_iota(jnp.int32, (all_rows, width), 1)
        rows = lax.broadcasted_iota(jnp.int32, (all_rows, width), 0)
        second = ((rows >= slots) & (rows < tall)) | (rows >= tall + blocks)
        lower = rows[0:tall] >= slots
        low = lax.broadcasted_iota(jnp.int32, (8, width), 1) < slots
        per_tile = width // tall
        wanted = jnp.concatenate(
            [
                jnp.where(lower, need[:, 1:2], need[:, 0:1]),
                jnp.broadcast_to(ids_here[0:blocks, 0:1], (blocks, width)),
                jnp.broadcast_to(ids_here[0:blocks, 1:2], (blocks, width)),
            ],
            axis=0,
        )
        for q in range(owners // per_tile):
            ids = jnp.zeros((8, width), jnp.float32)
            for d in range(per_tile):
                tile = jnp.where(low, band_first[q * per_tile + d, tall:, :], 0.0)
                twice = tile + pltpu.roll(tile, slots, 1)
                ids = ids + (pltpu.roll(twice, tall * d, 1) if d else twice)
            id_row = jnp.broadcast_to(ids[blocks : blocks + 1, :], (all_rows, width))
            bottom = (lanes % tall) // slots == 1
            good = (wanted == id_row) & (id_row > 0.0) & (bottom != second)
            pick_rows[:, q * width : (q + 1) * width] = jnp.where(good, 1.0, 0.0)
        ids = jnp.zeros((8, width), jnp.float32)
        for d in range(8):
            tile = jnp.where(low, side_first[d, slots:, :], 0.0)
            ids = ids + (pltpu.roll(tile, slots * d, 1) if d else tile)
        id_row = jnp.broadcast_to(ids[blocks : blocks + 1, :], (all_rows, width))
        western = lanes >= 4 * slots
        for i, (east_of, west_of) in enumerate(((2, 3), (4, 5), (6, 7))):
            wanted = jnp.concatenate(
                [
                    jnp.where(
                        lower, need[:, west_of : west_of + 1], need[:, east_of : east_of + 1]
                    ),
                    jnp.broadcast_to(ids_here[0:blocks, east_of : east_of + 1], (blocks, width)),
                    jnp.broadcast_to(ids_here[0:blocks, west_of : west_of + 1], (blocks, width)),
                ],
                axis=0,
            )
            good = (wanted == id_row) & (id_row > 0.0) & (western == second)
            pick_cols[all_rows * i : all_rows * (i + 1), :] = jnp.where(good, 1.0, 0.0)

    def take_edges(k):
        all_rows = tall + 2 * blocks
        take(rows_landed(k), row_recv.at[k])
        take(cols_landed(k), col_recv.at[k])
        if k == 0:
            build_picks()
        per_tile = width // tall
        got = jnp.zeros((all_rows, width), jnp.float32)
        for q in range(owners // per_tile):
            part = pl.ds(q * per_tile, per_tile)
            edges = band_first[part, 0:tall, :] if k == 0 else band_rows[k - 1, part]
            got = got + jnp.dot(
                pick_rows[:, q * width : (q + 1) * width],
                edges.reshape(width, width),
                precision=EXACT,
                preferred_element_type=jnp.float32,
            )
        count = 8 * slots
        edges = side_first[:, 0:slots, :] if k == 0 else side_cols[k - 1]
        cols = jnp.dot(
            pick_cols[:, 0:count],
            edges.reshape(count, width),
            precision=EXACT,
            preferred_element_type=jnp.float32,
        )
        lanes = lax.broadcasted_iota(jnp.int32, (all_rows, width), 1)
        straight = cols[0:all_rows]
        above = jnp.where(lanes == width - 1, cols[all_rows : 2 * all_rows], straight)
        below = jnp.where(lanes == 0, cols[2 * all_rows : 3 * all_rows], straight)
        slanted = pltpu.roll(above, 1, 1) + pltpu.roll(below, width - 1, 1)
        return got, straight, slanted

    def put_halo(k, got, straight, slanted):
        now = k % 2
        if k < SWEEPS - 1:
            for s in range(slots):
                field[now, s, PAD - 1 : PAD, :] = got[s : s + 1, :]
                field[now, s, PAD + height : PAD + height + 1, :] = got[
                    slots + s : slots + s + 1, :
                ]
        new_top[k] = got[tall:]
        for i, tile in enumerate((straight, slanted)):
            for h in range(2):
                filled[pl.ds(tall * i + h, slots, stride=2), :] = tile[slots * h : slots * (h + 1)]
                filled[pl.ds(2 * tall + 2 * blocks * i + h, blocks, stride=2), :] = tile[
                    tall + blocks * h : tall + blocks * (h + 1)
                ]
        halo_cols[k] = filled[...].T

    def ring(k, got, straight, slanted):
        now = k % 2
        lanes = lax.broadcasted_iota(jnp.int32, (tall, width), 1)
        start = lanes == 0
        end = lanes == width - 1
        got, straight, slanted = got[0:tall], straight[0:tall], slanted[0:tall]

        def stencil(coefs, center, level, vertical, slant):
            cx, cy, cd, inv, src = (coefs[i] for i in range(5))
            slant = 0.125 * slant
            left = src - cd * center + cx * (level + slant) + cy * (vertical + slant)
            return left if k == SWEEPS - 1 else left * inv

        def spread(value, before, after):
            left = jnp.where(start, before, pltpu.roll(value, 1, 1))
            return left + jnp.where(end, after, pltpu.roll(value, width - 1, 1))

        def ends(tile, at):
            part = tile[at : at + slots]
            return jnp.concatenate([part[:, 0:1], part[:, width - 1 : width]], axis=0)

        def sides(at, deep):
            part = got[at : at + slots]
            last = width - 1 - deep
            return jnp.concatenate([part[:, last : last + 1], part[:, deep : deep + 1]], axis=0)

        center = edge_cols[k]
        inside = inner_cols[...]
        level = inside + straight
        vertical = spread(center, sides(0, 0), sides(slots, 0))
        slant = slanted + spread(inside, sides(0, 1), sides(slots, 1))
        coefs = [col_coefs[i * tall : (i + 1) * tall, :] for i in range(5)]
        left = stencil(coefs, center, level, vertical, slant)
        if k == SWEEPS - 1:
            fix_source[slots:, :] = left
        else:
            weight, keep = weights[k]
            change = weight * left + keep * col_coefs[5 * tall : 6 * tall, :]
            col_coefs[5 * tall : 6 * tall, :] = change
            edge_cols[k + 1] = center + change
            send_cols(k + 1)

        center = edge_rows[k]
        inside = jnp.concatenate(
            [field[now, s, PAD + 1 : PAD + 2, :] for s in range(slots)]
            + [field[now, s, PAD + height - 2 : PAD + height - 1, :] for s in range(slots)],
            axis=0,
        )
        vertical = inside + got
        level = spread(center, ends(straight, slots), ends(straight, 0))
        slant = spread(vertical, ends(slanted, slots), ends(slanted, 0))
        left = stencil([row_coefs[i] for i in range(5)], center, level, vertical, slant)
        if k == SWEEPS - 1:
            fix_source[0:slots, :] = left[slots:]
        else:
            change = weight * left + keep * row_coefs[5]
            row_coefs[5] = change
            edge_rows[k + 1] = center + change
            send_rows(k + 1)

    def around(value, halo):
        at = lax.broadcasted_iota(jnp.int32, value.shape, 1)
        left = jnp.where(at == 0, halo, pltpu.roll(value, 1, 1))
        right = jnp.where(at == width - 1, halo, pltpu.roll(value, width - 1, 1))
        return left + right

    def balance(f, s, r0, level, vertical, slant):
        rows = pl.ds(r0, CHUNK)
        slant = 0.125 * slant
        return (
            source[s, rows, :]
            - coef_d[s, rows, :] * field[f, s, pl.ds(PAD + r0, CHUNK), :]
            + coef_x[s, rows, :] * (level + slant)
            + coef_y[s, rows, :] * (vertical + slant)
        )

    def columns(f, s, r0):
        center = field[f, s, pl.ds(PAD + r0, CHUNK), :]
        north = field[f, s, pl.ds(PAD + r0 - 1, CHUNK), :]
        south = field[f, s, pl.ds(PAD + r0 + 1, CHUNK), :]
        return center, north + south

    def sweep(k, starts, group):
        now = k % 2
        weight, keep = weights[k]
        quad = lax.broadcasted_iota(jnp.int32, (CHUNK, width), 1) // 4

        def some(g, carry):
            for r0 in starts:
                rows = pl.ds(r0, CHUNK)
                cols = halo_cols[k, rows, :]
                tile = col_tile[rows, :]
                done = []
                for j in range(group):
                    s = g * group + j
                    center, vertical = columns(now, s, r0)
                    level = around(center, pltpu.roll(cols, width - 1 - 2 * s, 1))
                    slant = around(vertical, pltpu.roll(cols, width - 1 - tall - 2 * s, 1))
                    left = balance(now, s, r0, level, vertical, slant)
                    change = weight * left * inv_d[s, rows, :] + keep * update[s, rows, :]
                    fresh = center + change
                    tile = jnp.where(quad == s, pltpu.roll(fresh, 2 + 4 * s, 1), tile)
                    done.append((s, change, fresh))
                for s, change, fresh in done:
                    update[s, rows, :] = change
                    field[1 - now, s, pl.ds(PAD + r0, CHUNK), :] = fresh
                col_tile[rows, :] = tile
            return carry

        lax.fori_loop(0, slots // group, some, 0)

    def turn_columns():
        col_turned[...] = col_tile[...].T
        for h in range(2):
            inner_cols[slots * h : slots * (h + 1), :] = col_turned[
                pl.ds(3 * h, slots, stride=4), :
            ]

    last = (SWEEPS - 1) % 2

    def remainder(r0, group):
        def some(g, carry):
            done = []
            for j in range(group):
                s = g * group + j
                center, vertical = columns(last, s, r0)
                level = pltpu.roll(center, 1, 1) + pltpu.roll(center, width - 1, 1)
                slant = pltpu.roll(vertical, 1, 1) + pltpu.roll(vertical, width - 1, 1)
                done.append((s, balance(last, s, r0, level, vertical, slant)))
            for s, left in done:
                resid[s, pl.ds(r0, CHUNK), :] = left
            return carry

        lax.fori_loop(0, slots // group, some, 0)

    def send_to(src, dst, sends, recvs, at, device):
        pltpu.make_async_remote_copy(
            src_ref=src,
            dst_ref=dst,
            send_sem=sends.at[at],
            recv_sem=recvs.at[at],
            device_id=(device, band),
            device_id_type=MESH,
        ).start()

    early = (coef_x, coef_y, coef_d, source)

    def early_start(w):
        rows = pl.ds(PART * w, PART)

        def fill(i, carry):
            for t in range(2):
                at = (1 + 2 * t) * blocks + i
                slot, live = find[at], have[at]
                for f, ref in enumerate(early):
                    near_out[w, f, t * blocks + i] = ref[slot, rows, :] * live
            return carry

        lax.fori_loop(0, blocks, fill, 0)
        send_to(near_out.at[w], near_in.at[w], early_send, early_recv, w, sibling)

    def early_cross(w):
        rows = pl.ds(PART * w, PART)
        take(near_in.at[w], early_recv.at[w])

        def fill(i, carry):
            at = 2 * blocks + i
            slot, live = find[at], have[at]
            for f, ref in enumerate(early):
                far_out[w, f, i] = ref[slot, rows, :] * live + near_in[w, f, blocks + i]
            return carry

        lax.fori_loop(0, blocks, fill, 0)
        send_to(far_out.at[w], far_in.at[w], early_send, early_recv, WINDOWS + w, across)

    def early_finish(w):
        rows = pl.ds(PART * w, PART)
        take(far_in.at[w], early_recv.at[WINDOWS + w])

        def fill(i, carry):
            slot, live = find[i], have[i]
            for f, ref in enumerate(early):
                new_coefs[f, i, rows, :] = (
                    ref[slot, rows, :] * live + near_in[w, f, i] + far_in[w, f, i]
                )
            inv = 1.0 / new_coefs[2, i, rows, :]
            new_inv[i, rows, :] = inv
            start = new_coefs[3, i, rows, :] * (inv * (1.0 / gamma))
            new_update[i, rows, :] = start
            new_field[0, i, pl.ds(PAD + PART * w, PART), :] = start
            return carry

        lax.fori_loop(0, blocks, fill, 0)

    def new_sweep(k):
        now = k % 2
        size = DEEP // 2
        for i in range(blocks):
            new_field[now, i, PAD - 1 : PAD, :] = new_top[k, i : i + 1, :]

        def one(i, carry):
            for r0 in range(0, DEEP, size):
                rows = pl.ds(r0, size)
                center = new_field[now, i, pl.ds(PAD + r0, size), :]
                vertical = (
                    new_field[now, i, pl.ds(PAD + r0 - 1, size), :]
                    + new_field[now, i, pl.ds(PAD + r0 + 1, size), :]
                )
                cols = halo_cols[k, rows, :]
                level = around(center, pltpu.roll(cols, width - 1 - 2 * tall - 2 * i, 1))
                slant = around(
                    vertical, pltpu.roll(cols, width - 1 - 2 * tall - 2 * blocks - 2 * i, 1)
                )
                slant = 0.125 * slant
                left = (
                    new_coefs[3, i, rows, :]
                    - new_coefs[2, i, rows, :] * center
                    + new_coefs[0, i, rows, :] * (level + slant)
                    + new_coefs[1, i, rows, :] * (vertical + slant)
                )
                kept = min(size, TOP - r0)
                if k == SWEEPS - 1:
                    res_out[i, pl.ds(r0, kept), :] = left[0:kept]
                else:
                    weight, keep = weights[k]
                    change = weight * left * new_inv[i, rows, :] + keep * new_update[i, rows, :]
                    new_update[i, rows, :] = change
                    fresh = center + change
                    new_field[1 - now, i, pl.ds(PAD + r0, size), :] = fresh
                    if k == SWEEPS - 2:
                        sol_out[i, pl.ds(r0, kept), :] = fresh[0:kept]
            return carry

        lax.fori_loop(0, blocks, one, 0)

    def rows_of(f, slot, r0, count):
        if f == 0:
            return field[last, slot, pl.ds(PAD + r0, count), :]
        return resid[slot, pl.ds(r0, count), :]

    def late_start(f, c):
        r0, count = LATE[c]

        def fill(i, carry):
            for t in range(2):
                at = (1 + 2 * t) * blocks + i
                late_out[c][f, t * blocks + i] = rows_of(f, find[at], r0, count) * have[at]
            return carry

        lax.fori_loop(0, blocks, fill, 0)
        at = f * len(LATE) + c
        send_to(late_out[c].at[f], late_in[c].at[f], late_send, late_recv, at, sibling)

    def late_cross(f, c):
        r0, count = LATE[c]
        at = f * len(LATE) + c
        take(late_in[c].at[f], late_recv.at[at])

        def fill(i, carry):
            at = 2 * blocks + i
            cross_out[c][f, i] = (
                rows_of(f, find[at], r0, count) * have[at] + late_in[c][f, blocks + i]
            )
            return carry

        lax.fori_loop(0, blocks, fill, 0)
        at = at + 2 * len(LATE)
        send_to(cross_out[c].at[f], cross_in[c].at[f], late_send, late_recv, at, across)

    def late_near(f, c, out):
        r0, count = LATE[c]

        def fill(i, carry):
            out[i, pl.ds(r0, count), :] = (
                rows_of(f, find[i], r0, count) * have[i] + late_in[c][f, i]
            )
            return carry

        lax.fori_loop(0, blocks, fill, 0)

    def late_far(f, c, out):
        r0, count = LATE[c]
        take(cross_in[c].at[f], late_recv.at[(2 + f) * len(LATE) + c])

        def fill(i, carry):
            rows = pl.ds(r0, count)
            out[i, rows, :] = out[i, rows, :] + cross_in[c][f, i]
            return carry

        lax.fori_loop(0, blocks, fill, 0)

    def send_fix():
        order = (me, sibling, across, base + (sibling % 4 + 2) % 4)
        fix_out[...] = jnp.zeros_like(fix_out)
        for t in range(4):
            for i in range(blocks):
                slot, live = find[t * blocks + i], have[t * blocks + i]
                east = fix_source[pl.ds(slots + slot, 1), :] * live
                west = fix_source[pl.ds(tall + slot, 1), :] * live
                south = fix_source[pl.ds(slot, 1), :] * live
                fix_out[t, 2 * i : 2 * i + 1, :] = east
                fix_out[t, 2 * i + 1 : 2 * i + 2, :] = west
                fix_out[t, 2 * blocks + i : 2 * blocks + i + 1, :] = south
        for t in range(1, 4):
            send_to(fix_out.at[t], fix_in.at[t - 1], fix_send, fix_recv, t - 1, order[t])

    def put_fix():
        for t in range(3):
            take(fix_in.at[t], fix_recv.at[t])
        total = fix_out[0] + fix_in[0] + fix_in[1] + fix_in[2]
        filled[0 : 4 * blocks, :] = total
        halo_cols[0] = filled[...].T
        count = height - TOP
        rows = pl.ds(TOP, count)
        for i in range(blocks):
            cols = pltpu.roll(halo_cols[0, rows, :], width - 1 - 2 * i, 1)
            at = lax.broadcasted_iota(jnp.int32, (count, width), 1)
            edge = (at == 0) | (at == width - 1)
            res_out[i, rows, :] = jnp.where(edge, cols, res_out[i, rows, :])
            res_out[i, height - 1 : height, :] = total[2 * blocks + i : 2 * blocks + i + 1, :]

    for f in range(2):
        new_field[f] = jnp.zeros(new_field.shape[1:], jnp.float32)

    filled[...] = jnp.zeros_like(filled)
    pl.semaphore_wait(barrier, owners - 1 + 8)
    send_cols(0)
    send_rows(0)
    whole = tuple(range(0, height, CHUNK))
    prepare(whole[0])
    early_start(0)
    prepare(whole[1])
    early_start(1)
    early_start(2)
    early_cross(0)
    for r0 in whole[2:]:
        prepare(r0)
    for k in range(SWEEPS - 2):
        halo = take_edges(k)
        ring(k, *halo)
        early_cross(k + 1)
        put_halo(k, *halo)
        sweep(k, whole, PAIR)
        turn_columns()
    k = SWEEPS - 2
    halo = take_edges(k)
    ring(k, *halo)
    put_halo(k, *halo)
    steps = len(LATE)
    for c in range(steps):
        sweep(k, (32 * (c + 1),), PAIR)
        late_start(0, c)
        if c:
            late_cross(0, c - 1)
    turn_columns()
    for c in range(steps):
        remainder(32 * (c + 1), PAIR)
        late_start(1, c)
        if c:
            late_cross(1, c - 1)
        else:
            late_cross(0, steps - 1)
    late_cross(1, steps - 1)
    for w in range(WINDOWS):
        early_finish(w)
    for k in range(SWEEPS - 1):
        new_sweep(k)
    k = SWEEPS - 1
    halo = take_edges(k)
    ring(k, *halo)
    send_fix()
    put_halo(k, *halo)
    new_sweep(k)
    for f, out in enumerate((sol_out, res_out)):
        for c in range(steps):
            late_near(f, c, out)
    for f, out in enumerate((sol_out, res_out)):
        for c in range(steps):
            late_far(f, c, out)
    put_fix()

    for k in range(SWEEPS):
        take(rows_landed(k), row_send.at[k])
        take(cols_landed(k), col_send.at[k])
    for w in range(WINDOWS):
        take(near_out.at[w], early_send.at[w])
        take(far_out.at[w], early_send.at[WINDOWS + w])
    for f in range(2):
        for c in range(steps):
            take(late_out[c].at[f], late_send.at[f * steps + c])
            take(cross_out[c].at[f], late_send.at[(2 + f) * steps + c])
    for t in range(3):
        take(fix_in.at[t], fix_send.at[t])


def per_device(
    owners, bands, depth, cell_dx, cell_dy, forcing, land_mask, dest_block, source_slot, neighbours
):
    slots, height, width = depth.shape
    blocks = source_slot.shape[0]
    tall = 2 * slots
    f32 = jnp.float32
    hbm = pl.BlockSpec(memory_space=pl.ANY)
    vmem = pl.BlockSpec(memory_space=pltpu.VMEM)
    whole = pltpu.VMEM((slots, height, width), f32)
    dma = pltpu.SemaphoreType.DMA

    def tiles(*shape):
        return pltpu.VMEM((*shape, width), f32)

    out = tiles(blocks, height)
    return pl.pallas_call(
        functools.partial(kernel, owners, bands),
        out_shape=(out, out),
        in_specs=[hbm] * 5 + [pl.BlockSpec(memory_space=pltpu.SMEM), vmem, vmem],
        out_specs=(vmem, vmem),
        scratch_shapes=[
            whole,
            whole,
            whole,
            whole,
            pltpu.VMEM((slots, height, width), jnp.int32),
            whole,
            whole,
            whole,
            whole,
            whole,
            whole,
            tiles(2, slots, height + 2 * PAD),
            whole,
            pltpu.VMEM((tall + 2 * blocks, owners * tall), f32),
            tiles(3 * (tall + 2 * blocks)),
            tiles(tall + 8),
            tiles(2, slots + 8),
            tiles(owners, tall + 8),
            tiles(8, slots + 8),
            tiles(SWEEPS, tall),
            tiles(SWEEPS, tall),
            tiles(SWEEPS - 1, owners, tall),
            tiles(SWEEPS - 1, 8, slots),
            tiles(height),
            pltpu.VMEM((width, height), f32),
            tiles(5, tall),
            tiles(6, tall),
            pltpu.VMEM((width, height), f32),
            tiles(tall),
            pltpu.VMEM((width, height), f32),
            tiles(SWEEPS, height),
            tiles(SWEEPS, 2 * blocks),
            tiles(4, blocks, DEEP),
            tiles(blocks, DEEP),
            tiles(blocks, DEEP),
            tiles(2, blocks, DEEP + 2 * PAD),
            tiles(3 * slots),
            tiles(4, 4 * blocks),
            tiles(3, 4 * blocks),
            pltpu.SMEM((4 * blocks,), jnp.int32),
            pltpu.SMEM((4 * blocks,), f32),
            tiles(WINDOWS, 4, 2 * blocks, PART),
            tiles(WINDOWS, 4, 2 * blocks, PART),
            tiles(WINDOWS, 4, blocks, PART),
            tiles(WINDOWS, 4, blocks, PART),
            [tiles(2, 2 * blocks, count) for _, count in LATE],
            [tiles(2, 2 * blocks, count) for _, count in LATE],
            [tiles(2, blocks, count) for _, count in LATE],
            [tiles(2, blocks, count) for _, count in LATE],
            dma((5,)),
            dma((SWEEPS,)),
            dma((SWEEPS,)),
            dma((SWEEPS,)),
            dma((SWEEPS,)),
            dma((2 * WINDOWS,)),
            dma((2 * WINDOWS,)),
            dma((4 * len(LATE),)),
            dma((4 * len(LATE),)),
            dma((3,)),
            dma((3,)),
        ],
        compiler_params=pltpu.CompilerParams(
            collective_id=0, has_side_effects=True, vmem_limit_bytes=56 * 1024 * 1024
        ),
        name="barotropic_solve",
    )(
        depth,
        cell_dx,
        cell_dy,
        forcing,
        land_mask,
        dest_block,
        dest_block.reshape(1, slots),
        neighbours,
    )


def solution(mesh):
    blocks3 = P(("blk", "grp"), None, None)
    flat = P(("blk", "grp"))
    in_specs = (blocks3,) * 5 + (flat, flat, P(("blk", "grp"), None))
    return jax.shard_map(
        functools.partial(per_device, mesh.shape["blk"], mesh.shape["grp"]),
        mesh=mesh,
        in_specs=in_specs,
        out_specs=(blocks3, blocks3),
        check_vma=False,
    )
```

```python
import functools

import jax
import jax.numpy as jnp
from jax import lax
from jax.experimental import pallas as pl
from jax.experimental.pallas import tpu as pltpu
from jax.sharding import PartitionSpec as P

SWEEPS = 4
TAU_MASS = 6.0
LOW_BOUND = 0.2
HIGH_BOUND = 1.9
CHUNK = 32
PAD = 8
GATHER = 16
PAIR = 4
EARLY = ((0, 16), (16, 16), (32, 24))
DEEP = 56
TOP = DEEP - 8
NEW = ((0, 32), (32, 24))
LATE = ((48, 24), (72, 24), (96, 32))
WINDOWS = len(EARLY)
STEPS = ((40, 32), (72, 24), (96, 32))
MESH = pl.DeviceIdType.MESH
EXACT = lax.Precision.HIGHEST


def relax_weights():
    alpha = 2.0 / (HIGH_BOUND - LOW_BOUND)
    beta = (HIGH_BOUND + LOW_BOUND) / (HIGH_BOUND - LOW_BOUND)
    gamma = beta / alpha
    weight = 2.0 / gamma
    weights = []
    for _ in range(SWEEPS - 1):
        weight = 1.0 / (gamma - weight / (4.0 * alpha**2))
        weights.append((weight, gamma * weight - 1.0))
    return gamma, weights


def kernel(
    owners,
    bands,
    depth_hbm,
    dx_hbm,
    dy_hbm,
    forcing_hbm,
    mask_hbm,
    dest_smem,
    dest_row,
    neigh,
    sol_out,
    res_out,
    fix_cols,
    fix_rows,
    cross_in,
    depth_v,
    dx_v,
    dy_v,
    forcing_v,
    mask_v,
    coef_x,
    coef_y,
    coef_d,
    inv_d,
    source,
    update,
    field,
    resid,
    pick_rows,
    pick_cols,
    first_rows,
    first_cols,
    band_first,
    side_first,
    edge_rows,
    edge_cols,
    band_rows,
    side_cols,
    col_tile,
    col_turned,
    row_raw,
    row_coefs,
    col_coefs,
    inner_cols,
    filled,
    halo_cols,
    new_top,
    new_coefs,
    new_inv,
    new_update,
    new_field,
    fix_source,
    fix_out,
    fix_in,
    find,
    have,
    near_out,
    near_in,
    far_out,
    far_in,
    late_out,
    late_in,
    cross_out,
    load_sems,
    row_send,
    row_recv,
    col_send,
    col_recv,
    early_send,
    early_recv,
    late_send,
    late_recv,
    fix_send,
    fix_recv,
):
    slots, height, width = depth_v.shape
    blocks = neigh.shape[0]
    tall = 2 * slots
    me = lax.axis_index("blk")
    band = lax.axis_index("grp")
    core = me % 2
    sibling = me + 1 - 2 * core
    base = me - me % 4
    inner = me % 4
    across = base + (inner + 2) % 4
    east_band = (band + 1) % bands
    west_band = (band + bands - 1) % bands

    loads = [
        pltpu.make_async_copy(src, dst, load_sems.at[i])
        for i, (src, dst) in enumerate(
            (
                (dx_hbm, dx_v),
                (dy_hbm, dy_v),
                (depth_hbm, depth_v),
                (mask_hbm, mask_v),
                (forcing_hbm, forcing_v),
            )
        )
    ]
    for load in loads:
        load.start()

    barrier = pltpu.get_barrier_semaphore()
    for step in range(4):
        for side in (east_band, west_band):
            pl.semaphore_signal(
                barrier,
                inc=1,
                device_id=(base + (inner + step) % 4, side),
                device_id_type=MESH,
            )
    for step in range(1, owners):
        pl.semaphore_signal(
            barrier, inc=1, device_id=((me + step) % owners, band), device_id_type=MESH
        )

    first_rows[tall:, :] = jnp.zeros((8, width), jnp.float32)
    first_rows[tall : tall + blocks, 0:8] = (neigh[...] + 1).astype(jnp.float32)
    first_rows[tall + blocks : tall + blocks + 1, 0:slots] = (dest_row[...] + 1).astype(
        jnp.float32
    )
    table = first_rows[tall:, :]
    first_cols[0, slots:, :] = table
    first_cols[1, slots:, :] = table

    targets = (me, sibling, across, base + (sibling % 4 + 2) % 4)
    for t, target in enumerate(targets):
        for j in range(blocks):
            wanted = (target * bands + band) * blocks + j
            place = jnp.int32(0)
            count = jnp.int32(0)
            for s in range(slots):
                hit = dest_smem[s] == wanted
                place = jnp.where(hit, s, place)
                count = jnp.where(hit, 1, count)
            find[t * blocks + j] = place
            have[t * blocks + j] = count.astype(jnp.float32)

    gamma, weights = relax_weights()

    def coefficients(dx, dy, deep, src):
        area = dx * dy
        scaled = deep / area
        cx = scaled * (dy * dy)
        cy = scaled * (dx * dx)
        cd = 2.5 * (cx + cy) + TAU_MASS * area
        inv = 1.0 / cd
        return cx, cy, cd, inv, src, src * (inv * (1.0 / gamma))

    for load in loads:
        load.wait()

    def gather(r, carry):
        rows = pl.ds(pl.multiple_of(r * GATHER, GATHER), GATHER)
        quad = lax.broadcasted_iota(jnp.int32, (GATHER, width), 1) // 4
        tile = jnp.zeros((GATHER, width), jnp.float32)
        for s in range(slots):
            ocean = mask_v[s, rows, :].astype(jnp.float32)
            parts = (
                dx_v[s, rows, :],
                dy_v[s, rows, :],
                depth_v[s, rows, :] * ocean,
                forcing_v[s, rows, :] * ocean,
            )
            for i, part in enumerate(parts):
                at = i * slots + s
                tile = jnp.where(quad == at, pltpu.roll(part, 2 + 4 * at, 1), tile)
        col_tile[rows, :] = tile
        return carry

    lax.fori_loop(0, height // GATHER, gather, 0)
    col_turned[...] = col_tile[...].T
    for i, ref in enumerate((dx_v, dy_v, depth_v, forcing_v, mask_v)):
        for s in range(slots):
            for at, row in ((s, 0), (slots + s, height - 1)):
                value = ref[s, row : row + 1, :]
                row_raw[i, at : at + 1, :] = value.astype(jnp.float32)
    sides_of = [
        [col_turned[pl.ds(4 * slots * i + c, slots, stride=4), :] for i in range(4)]
        for c in range(4)
    ]
    for i, part in enumerate(
        coefficients(*(jnp.concatenate([e, w], axis=0) for e, w in zip(sides_of[1], sides_of[2])))
    ):
        col_coefs[i * tall : (i + 1) * tall, :] = part
    start = coefficients(
        *(jnp.concatenate([e, w], axis=0) for e, w in zip(sides_of[0], sides_of[3]))
    )[5]
    inner_cols[...] = start
    ocean = row_raw[4]
    for i, part in enumerate(
        coefficients(row_raw[0], row_raw[1], row_raw[2] * ocean, row_raw[3] * ocean)
    ):
        row_coefs[i] = part
    edge_rows[0] = row_coefs[5]
    edge_cols[0] = col_coefs[5 * tall : 6 * tall, :].reshape(2, slots, width)
    first_rows[0:tall, :] = row_coefs[5]
    first_cols[0, 0:slots, :] = col_coefs[5 * tall + slots : 6 * tall, :]
    first_cols[1, 0:slots, :] = col_coefs[5 * tall : 5 * tall + slots, :]

    def prepare(r0):
        rows = pl.ds(r0, CHUNK)

        def one(s, carry):
            ocean = mask_v[s, rows, :].astype(jnp.float32)
            parts = coefficients(
                dx_v[s, rows, :],
                dy_v[s, rows, :],
                depth_v[s, rows, :] * ocean,
                forcing_v[s, rows, :] * ocean,
            )
            for ref, part in zip((coef_x, coef_y, coef_d, inv_d, source, update), parts):
                ref[s, rows, :] = part
            field[0, s, pl.ds(PAD + r0, CHUNK), :] = parts[5]
            return carry

        lax.fori_loop(0, slots, one, 0)

    def send_cols(k):
        wrap = (band == 0).astype(jnp.int32)
        sides = ((wrap, west_band * wrap + east_band * (1 - wrap)),)
        sides = sides + ((1 - wrap, east_band * wrap + west_band * (1 - wrap)),)
        for to_west, side in sides:
            for step in (2, 3, 1, 0):
                slot = step + 4 * (1 - to_west)
                if k == 0:
                    src, dst = first_cols.at[1 - to_west], side_first.at[slot]
                else:
                    src, dst = edge_cols.at[k, to_west], side_cols.at[k - 1, slot]
                pltpu.make_async_remote_copy(
                    src_ref=src,
                    dst_ref=dst,
                    send_sem=col_send.at[k],
                    recv_sem=col_recv.at[k],
                    device_id=(base + (inner + step) % 4, side),
                    device_id_type=MESH,
                ).start()

    def send_rows(k):
        for step in range(1, owners):
            if k == 0:
                src, dst = first_rows, band_first.at[owners - step]
            else:
                src, dst = edge_rows.at[k], band_rows.at[k - 1, owners - step]
            pltpu.make_async_remote_copy(
                src_ref=src,
                dst_ref=dst,
                send_sem=row_send.at[k],
                recv_sem=row_recv.at[k],
                device_id=((me + step) % owners, band),
                device_id_type=MESH,
            ).start()
        if k == 0:
            band_first[0] = first_rows[...]
        else:
            band_rows[k - 1, 0] = edge_rows[k]

    def take(ref, sem):
        pltpu.make_async_copy(ref, ref, sem).wait()

    def rows_landed(k):
        return (band_first if k == 0 else band_rows.at[k - 1]).at[pl.ds(1, owners - 1)]

    def cols_landed(k):
        return side_first if k == 0 else side_cols.at[k - 1]

    def build_picks():
        lanes = lax.broadcasted_iota(jnp.int32, (tall, width), 1)
        rows = lax.broadcasted_iota(jnp.int32, (tall, width), 0)
        ids_here = first_rows[tall:, :]
        mine = jnp.broadcast_to(ids_here[blocks : blocks + 1, :], (tall, width))
        own = jnp.sum(jnp.where(lanes == rows % slots, mine, 0.0), axis=1, keepdims=True)
        group_ids = ((base + lanes // 8) * bands + band) * blocks + lanes % 8 + 1
        known = (lanes % 8 < blocks) & (lanes < 32)
        match = jnp.where(known & (own == group_ids.astype(jnp.float32)), 1.0, 0.0)
        listed = jnp.concatenate(
            [band_first[(base + g - me + owners) % owners, tall:, :] for g in range(4)], axis=0
        )
        need = jnp.dot(
            match[:, :32], listed, precision=EXACT, preferred_element_type=jnp.float32
        )
        all_rows = tall + 2 * blocks
        lanes = lax.broadcasted_iota(jnp.int32, (all_rows, width), 1)
        rows = lax.broadcasted_iota(jnp.int32, (all_rows, width), 0)
        second = ((rows >= slots) & (rows < tall)) | (rows >= tall + blocks)
        lower = rows[0:tall] >= slots
        low = lax.broadcasted_iota(jnp.int32, (8, width), 1) < slots
        per_tile = width // tall
        wanted = jnp.concatenate(
            [
                jnp.where(lower, need[:, 1:2], need[:, 0:1]),
                jnp.broadcast_to(ids_here[0:blocks, 0:1], (blocks, width)),
                jnp.broadcast_to(ids_here[0:blocks, 1:2], (blocks, width)),
            ],
            axis=0,
        )
        for q in range(owners // per_tile):
            ids = jnp.zeros((8, width), jnp.float32)
            for d in range(per_tile):
                tile = jnp.where(low, band_first[q * per_tile + d, tall:, :], 0.0)
                twice = tile + pltpu.roll(tile, slots, 1)
                ids = ids + (pltpu.roll(twice, tall * d, 1) if d else twice)
            id_row = jnp.broadcast_to(ids[blocks : blocks + 1, :], (all_rows, width))
            bottom = (lanes % tall) // slots == 1
            good = (wanted == id_row) & (id_row > 0.0) & (bottom != second)
            pick_rows[:, q * width : (q + 1) * width] = jnp.where(good, 1.0, 0.0)
        ids = jnp.zeros((8, width), jnp.float32)
        for d in range(8):
            tile = jnp.where(low, side_first[d, slots:, :], 0.0)
            ids = ids + (pltpu.roll(tile, slots * d, 1) if d else tile)
        id_row = jnp.broadcast_to(ids[blocks : blocks + 1, :], (all_rows, width))
        western = lanes >= 4 * slots
        for i, (east_of, west_of) in enumerate(((2, 3), (4, 5), (6, 7))):
            wanted = jnp.concatenate(
                [
                    jnp.where(
                        lower, need[:, west_of : west_of + 1], need[:, east_of : east_of + 1]
                    ),
                    jnp.broadcast_to(ids_here[0:blocks, east_of : east_of + 1], (blocks, width)),
                    jnp.broadcast_to(ids_here[0:blocks, west_of : west_of + 1], (blocks, width)),
                ],
                axis=0,
            )
            good = (wanted == id_row) & (id_row > 0.0) & (western == second)
            pick_cols[all_rows * i : all_rows * (i + 1), :] = jnp.where(good, 1.0, 0.0)

    all_rows = tall + 2 * blocks
    lanes = lax.broadcasted_iota(jnp.int32, (tall, width), 1)
    start = lanes == 0
    end = lanes == width - 1

    def take_rows(k):
        take(rows_landed(k), row_recv.at[k])
        if k == 0:
            take(cols_landed(k), col_recv.at[k])
            build_picks()
        per_tile = width // tall
        got = jnp.zeros((all_rows, width), jnp.float32)
        for q in range(owners // per_tile):
            part = pl.ds(q * per_tile, per_tile)
            edges = band_first[part, 0:tall, :] if k == 0 else band_rows[k - 1, part]
            got = got + jnp.dot(
                pick_rows[:, q * width : (q + 1) * width],
                edges.reshape(width, width),
                precision=EXACT,
                preferred_element_type=jnp.float32,
            )
        return got

    def take_cols(k):
        if k:
            take(cols_landed(k), col_recv.at[k])
        count = 8 * slots
        edges = side_first[:, 0:slots, :] if k == 0 else side_cols[k - 1]
        cols = jnp.dot(
            pick_cols[:, 0:count],
            edges.reshape(count, width),
            precision=EXACT,
            preferred_element_type=jnp.float32,
        )
        at = lax.broadcasted_iota(jnp.int32, (all_rows, width), 1)
        straight = cols[0:all_rows]
        above = jnp.where(at == width - 1, cols[all_rows : 2 * all_rows], straight)
        below = jnp.where(at == 0, cols[2 * all_rows : 3 * all_rows], straight)
        slanted = pltpu.roll(above, 1, 1) + pltpu.roll(below, width - 1, 1)
        return straight, slanted

    def put_halo(k, got, straight, slanted):
        now = k % 2
        if k < SWEEPS - 1:
            for s in range(slots):
                field[now, s, PAD - 1 : PAD, :] = got[s : s + 1, :]
                field[now, s, PAD + height : PAD + height + 1, :] = got[
                    slots + s : slots + s + 1, :
                ]
        new_top[k] = got[tall:]
        for i, tile in enumerate((straight, slanted)):
            for h in range(2):
                filled[pl.ds(tall * i + h, slots, stride=2), :] = tile[slots * h : slots * (h + 1)]
                filled[pl.ds(2 * tall + 2 * blocks * i + h, blocks, stride=2), :] = tile[
                    tall + blocks * h : tall + blocks * (h + 1)
                ]
        halo_cols[k] = filled[...].T

    def exchange(k):
        now = k % 2
        every = take_rows(k)
        got = every[0:tall]

        def spread(value, before, after):
            left = jnp.where(start, before, pltpu.roll(value, 1, 1))
            return left + jnp.where(end, after, pltpu.roll(value, width - 1, 1))

        def ends(tile, at):
            part = tile[at : at + slots]
            return jnp.concatenate([part[:, 0:1], part[:, width - 1 : width]], axis=0)

        def sides(at, deep):
            part = got[at : at + slots]
            far = width - 1 - deep
            return jnp.concatenate([part[:, far : far + 1], part[:, deep : deep + 1]], axis=0)

        def known(coefs, center, level, vertical, slant):
            cx, cy, cd, _, src = coefs
            slant = 0.125 * slant
            return src - cd * center + cx * (level + slant) + cy * (vertical + slant)

        col_now = [col_coefs[i * tall : (i + 1) * tall, :] for i in range(5)]
        center = edge_cols[k].reshape(tall, width)
        inside = inner_cols[...]
        vertical = spread(center, sides(0, 0), sides(slots, 0))
        slant = spread(inside, sides(0, 1), sides(slots, 1))
        col_part = known(col_now, center, inside, vertical, slant)
        col_slant = 0.125 * (col_now[0] + col_now[1])

        row_now = [row_coefs[i] for i in range(5)]
        row_center = edge_rows[k]
        inside = jnp.concatenate(
            [field[now, s, PAD + 1 : PAD + 2, :] for s in range(slots)]
            + [field[now, s, PAD + height - 2 : PAD + height - 1, :] for s in range(slots)],
            axis=0,
        )
        vertical = inside + got
        level = spread(row_center, 0.0, 0.0)
        slant = spread(vertical, 0.0, 0.0)
        row_part = known(row_now, row_center, level, vertical, slant)
        row_slant = 0.125 * (row_now[0] + row_now[1])
        if k < SWEEPS - 1:
            weight, keep = weights[k]
            col_scale = weight * col_now[3]
            row_scale = weight * row_now[3]
            col_keep = keep * col_coefs[5 * tall : 6 * tall, :]
            row_keep = keep * row_coefs[5]

        straights, slants = take_cols(k)
        straight, slanted = straights[0:tall], slants[0:tall]
        left = col_part + col_now[0] * straight + col_slant * slanted
        if k == SWEEPS - 1:
            fix_source[slots:, :] = left
        else:
            change = col_scale * left + col_keep
            col_coefs[5 * tall : 6 * tall, :] = change
            edge_cols[k + 1] = (center + change).reshape(2, slots, width)
            send_cols(k + 1)

        def outer(tile):
            before, after = ends(tile, slots), ends(tile, 0)
            return jnp.where(start, before, 0.0) + jnp.where(end, after, 0.0)

        left = row_part + row_now[0] * outer(straight) + row_slant * outer(slanted)
        if k == SWEEPS - 1:
            fix_source[0:slots, :] = left[slots:]
        else:
            change = row_scale * left + row_keep
            row_coefs[5] = change
            edge_rows[k + 1] = row_center + change
            send_rows(k + 1)
        return every, straights, slants

    def around(value, halo):
        at = lax.broadcasted_iota(jnp.int32, value.shape, 1)
        left = jnp.where(at == 0, halo, pltpu.roll(value, 1, 1))
        right = jnp.where(at == width - 1, halo, pltpu.roll(value, width - 1, 1))
        return left + right

    def balance(f, s, r0, size, level, vertical, slant):
        rows = pl.ds(r0, size)
        slant = 0.125 * slant
        return (
            source[s, rows, :]
            - coef_d[s, rows, :] * field[f, s, pl.ds(PAD + r0, size), :]
            + coef_x[s, rows, :] * (level + slant)
            + coef_y[s, rows, :] * (vertical + slant)
        )

    def columns(f, s, r0, size):
        center = field[f, s, pl.ds(PAD + r0, size), :]
        north = field[f, s, pl.ds(PAD + r0 - 1, size), :]
        south = field[f, s, pl.ds(PAD + r0 + 1, size), :]
        return center, north + south

    def sweep(k, pieces, group):
        now = k % 2
        weight, keep = weights[k]
        for r0, size in pieces:
            rows = pl.ds(r0, size)
            quad = lax.broadcasted_iota(jnp.int32, (size, width), 1) // 4
            cols = halo_cols[k, rows, :]
            tile = col_tile[rows, :]
            for first in range(0, slots, group):
                done = []
                for s in range(first, first + group):
                    center, vertical = columns(now, s, r0, size)
                    level = around(center, pltpu.roll(cols, width - 1 - 2 * s, 1))
                    slant = around(vertical, pltpu.roll(cols, width - 1 - tall - 2 * s, 1))
                    left = balance(now, s, r0, size, level, vertical, slant)
                    change = weight * left * inv_d[s, rows, :] + keep * update[s, rows, :]
                    fresh = center + change
                    tile = jnp.where(quad == s, pltpu.roll(fresh, 2 + 4 * s, 1), tile)
                    done.append((s, change, fresh))
                for s, change, fresh in done:
                    update[s, rows, :] = change
                    field[1 - now, s, pl.ds(PAD + r0, size), :] = fresh
            col_tile[rows, :] = tile

    def turn_columns():
        col_turned[...] = col_tile[...].T
        for h in range(2):
            inner_cols[slots * h : slots * (h + 1), :] = col_turned[
                pl.ds(3 * h, slots, stride=4), :
            ]

    last = (SWEEPS - 1) % 2

    def remainder(r0, size, group):
        for first in range(0, slots, group):
            done = []
            for s in range(first, first + group):
                center, vertical = columns(last, s, r0, size)
                level = pltpu.roll(center, 1, 1) + pltpu.roll(center, width - 1, 1)
                slant = pltpu.roll(vertical, 1, 1) + pltpu.roll(vertical, width - 1, 1)
                done.append((s, balance(last, s, r0, size, level, vertical, slant)))
            for s, left in done:
                resid[s, pl.ds(r0, size), :] = left

    def send_to(src, dst, sends, recvs, at, device):
        pltpu.make_async_remote_copy(
            src_ref=src,
            dst_ref=dst,
            send_sem=sends.at[at],
            recv_sem=recvs.at[at],
            device_id=(device, band),
            device_id_type=MESH,
        ).start()

    early = (coef_x, coef_y, coef_d, source)

    def early_start(w):
        rows = pl.ds(*EARLY[w])

        def fill(i, carry):
            for t in range(2):
                at = (1 + 2 * t) * blocks + i
                slot, live = find[at], have[at]
                for f, ref in enumerate(early):
                    near_out[w][f, t * blocks + i] = ref[slot, rows, :] * live
            return carry

        lax.fori_loop(0, blocks, fill, 0)
        send_to(near_out[w], near_in[w], early_send, early_recv, w, sibling)

    def early_cross(w):
        rows = pl.ds(*EARLY[w])
        take(near_in[w], early_recv.at[w])

        def fill(i, carry):
            at = 2 * blocks + i
            slot, live = find[at], have[at]
            for f, ref in enumerate(early):
                far_out[w][f, i] = ref[slot, rows, :] * live + near_in[w][f, blocks + i]
            return carry

        lax.fori_loop(0, blocks, fill, 0)
        send_to(far_out[w], far_in[w], early_send, early_recv, WINDOWS + w, across)

    def early_finish(w):
        rows = pl.ds(*EARLY[w])
        take(far_in[w], early_recv.at[WINDOWS + w])

        def fill(i, carry):
            slot, live = find[i], have[i]
            for f, ref in enumerate(early):
                new_coefs[f, i, rows, :] = (
                    ref[slot, rows, :] * live + near_in[w][f, i] + far_in[w][f, i]
                )
            inv = 1.0 / new_coefs[2, i, rows, :]
            new_inv[i, rows, :] = inv
            start = new_coefs[3, i, rows, :] * (inv * (1.0 / gamma))
            new_update[i, rows, :] = start
            new_field[0, i, pl.ds(PAD + EARLY[w][0], EARLY[w][1]), :] = start
            return carry

        lax.fori_loop(0, blocks, fill, 0)

    def new_sweep(k):
        now = k % 2
        for i in range(blocks):
            new_field[now, i, PAD - 1 : PAD, :] = new_top[k, i : i + 1, :]
        for r0, size in NEW:
            rows = pl.ds(r0, size)
            cols = halo_cols[k, rows, :]
            done = []
            for i in range(blocks):
                center = new_field[now, i, pl.ds(PAD + r0, size), :]
                vertical = (
                    new_field[now, i, pl.ds(PAD + r0 - 1, size), :]
                    + new_field[now, i, pl.ds(PAD + r0 + 1, size), :]
                )
                level = around(center, pltpu.roll(cols, width - 1 - 2 * tall - 2 * i, 1))
                slant = around(
                    vertical, pltpu.roll(cols, width - 1 - 2 * tall - 2 * blocks - 2 * i, 1)
                )
                slant = 0.125 * slant
                left = (
                    new_coefs[3, i, rows, :]
                    - new_coefs[2, i, rows, :] * center
                    + new_coefs[0, i, rows, :] * (level + slant)
                    + new_coefs[1, i, rows, :] * (vertical + slant)
                )
                if k == SWEEPS - 1:
                    done.append((left, None))
                else:
                    weight, keep = weights[k]
                    change = weight * left * new_inv[i, rows, :] + keep * new_update[i, rows, :]
                    done.append((center + change, change))
            kept = min(size, TOP - r0)
            for i, (fresh, change) in enumerate(done):
                if k == SWEEPS - 1:
                    res_out[i, pl.ds(r0, kept), :] = fresh[0:kept]
                else:
                    new_update[i, rows, :] = change
                    new_field[1 - now, i, pl.ds(PAD + r0, size), :] = fresh
                    if k == SWEEPS - 2:
                        sol_out[i, pl.ds(r0, kept), :] = fresh[0:kept]

    def rows_of(f, slot, r0, count):
        if f == 0:
            return field[last, slot, pl.ds(PAD + r0, count), :]
        return resid[slot, pl.ds(r0, count), :]

    def late_start(f, c):
        r0, count = LATE[c]

        def fill(i, carry):
            for t in range(2):
                at = (1 + 2 * t) * blocks + i
                late_out[c][f, t * blocks + i] = rows_of(f, find[at], r0, count) * have[at]
            return carry

        lax.fori_loop(0, blocks, fill, 0)
        at = f * len(LATE) + c
        send_to(late_out[c].at[f], late_in[c].at[f], late_send, late_recv, at, sibling)

    def late_cross(f, c):
        r0, count = LATE[c]
        at = f * len(LATE) + c
        take(late_in[c].at[f], late_recv.at[at])

        def fill(i, carry):
            at = 2 * blocks + i
            cross_out[c][f, i] = (
                rows_of(f, find[at], r0, count) * have[at] + late_in[c][f, blocks + i]
            )
            return carry

        lax.fori_loop(0, blocks, fill, 0)
        at = at + 2 * len(LATE)
        send_to(cross_out[c].at[f], cross_in[c].at[f], late_send, late_recv, at, across)

    def late_near(f, c, out):
        r0, count = LATE[c]

        def fill(i, carry):
            out[i, pl.ds(r0, count), :] = (
                rows_of(f, find[i], r0, count) * have[i] + late_in[c][f, i]
            )
            return carry

        lax.fori_loop(0, blocks, fill, 0)

    def send_fix():
        order = (me, sibling, across, base + (sibling % 4 + 2) % 4)
        fix_out[...] = jnp.zeros_like(fix_out)
        for t in range(4):
            for i in range(blocks):
                slot, live = find[t * blocks + i], have[t * blocks + i]
                east = fix_source[pl.ds(slots + slot, 1), :] * live
                west = fix_source[pl.ds(tall + slot, 1), :] * live
                south = fix_source[pl.ds(slot, 1), :] * live
                fix_out[t, 2 * i : 2 * i + 1, :] = east
                fix_out[t, 2 * i + 1 : 2 * i + 2, :] = west
                fix_out[t, 2 * blocks + i : 2 * blocks + i + 1, :] = south
        for t in range(1, 4):
            send_to(fix_out.at[t], fix_in.at[t - 1], fix_send, fix_recv, t - 1, order[t])

    def take_fix():
        for t in range(3):
            take(fix_in.at[t], fix_recv.at[t])
        total = fix_out[0] + fix_in[0] + fix_in[1] + fix_in[2]
        filled[0 : 4 * blocks, :] = total
        fix_cols[...] = filled[...].T
        fix_rows[...] = total

    for f in range(2):
        new_field[f] = jnp.zeros(new_field.shape[1:], jnp.float32)

    filled[...] = jnp.zeros_like(filled)
    pl.semaphore_wait(barrier, owners - 1 + 8)
    send_cols(0)
    send_rows(0)
    whole = tuple(range(0, height, CHUNK))
    prepare(whole[0])
    early_start(0)
    prepare(whole[1])
    for w in range(1, WINDOWS):
        early_start(w)
    early_cross(0)
    for r0 in whole[2:]:
        prepare(r0)
    for k in range(SWEEPS - 2):
        halo = exchange(k)
        early_cross(k + 1)
        put_halo(k, *halo)
        sweep(k, [(r0, CHUNK) for r0 in whole], PAIR)
        turn_columns()
    k = SWEEPS - 2
    halo = exchange(k)
    for w in range(SWEEPS - 1, WINDOWS):
        early_cross(w)
    put_halo(k, *halo)
    steps = len(LATE)
    for c in range(steps):
        sweep(k, (STEPS[c],), PAIR)
        late_start(0, c)
        if c:
            late_cross(0, c - 1)
    turn_columns()
    for c in range(steps):
        remainder(*LATE[c], PAIR)
        late_start(1, c)
        if c:
            late_cross(1, c - 1)
        else:
            late_cross(0, steps - 1)
    for w in range(WINDOWS):
        early_finish(w)
    for k in range(SWEEPS - 1):
        new_sweep(k)
    k = SWEEPS - 1
    halo = exchange(k)
    send_fix()
    late_cross(1, steps - 1)
    put_halo(k, *halo)
    new_sweep(k)
    for f, out in enumerate((sol_out, res_out)):
        for c in range(steps):
            late_near(f, c, out)
    take_fix()
    for at in range(2 * steps, 4 * steps):
        take(cross_in[at % steps].at[at // steps - 2], late_recv.at[at])

    for k in range(SWEEPS):
        take(rows_landed(k), row_send.at[k])
        take(cols_landed(k), col_send.at[k])
    for w in range(WINDOWS):
        take(near_out[w], early_send.at[w])
        take(far_out[w], early_send.at[WINDOWS + w])
    for f in range(2):
        for c in range(steps):
            take(late_out[c].at[f], late_send.at[f * steps + c])
            take(cross_out[c].at[f], late_send.at[(2 + f) * steps + c])
    for t in range(3):
        take(fix_in.at[t], fix_send.at[t])


def finish(near_sol, near_res, fix_cols, fix_rows, cross, sol_out, res_out, sol_v, res_v, sems):
    blocks, height, width = near_sol.shape
    top = pl.ds(0, TOP)
    rest = pl.ds(TOP, height - TOP)
    pairs = ((near_sol, sol_v, sol_out), (near_res, res_v, res_out))
    copies = []
    for f, (near, _, out) in enumerate(pairs):
        copies.append(
            pltpu.make_async_copy(near.at[:, top, :], out.at[:, top, :], sems.at[2 * f])
        )
        copies[-1].start()
    for f, (near, value_v, out) in enumerate(pairs):
        for c, (r0, count) in enumerate(LATE):
            rows = pl.ds(r0, count)
            at = lax.broadcasted_iota(jnp.int32, (count, width), 1)
            edge = (at == 0) | (at == width - 1)
            for i in range(blocks):
                value = near[i, rows, :] + cross[c][f, i]
                if f:
                    cols = pltpu.roll(fix_cols[rows, :], width - 1 - 2 * i, 1)
                    value = jnp.where(edge, cols, value)
                value_v[i, pl.ds(r0 - TOP, count), :] = value
        if f:
            for i in range(blocks):
                at = 2 * blocks + i
                value_v[i, height - TOP - 1 : height - TOP, :] = fix_rows[at : at + 1, :]
        copies.append(pltpu.make_async_copy(value_v, out.at[:, rest, :], sems.at[2 * f + 1]))
        copies[-1].start()
    for copy in copies:
        copy.wait()


def per_device(
    owners, bands, depth, cell_dx, cell_dy, forcing, land_mask, dest_block, source_slot, neighbours
):
    slots, height, width = depth.shape
    blocks = source_slot.shape[0]
    tall = 2 * slots
    f32 = jnp.float32
    hbm = pl.BlockSpec(memory_space=pl.ANY)
    vmem = pl.BlockSpec(memory_space=pltpu.VMEM)
    whole = pltpu.VMEM((slots, height, width), f32)
    dma = pltpu.SemaphoreType.DMA

    def tiles(*shape):
        return pltpu.VMEM((*shape, width), f32)

    out = tiles(blocks, height)
    cross = [tiles(2, blocks, count) for _, count in LATE]
    parts = pl.pallas_call(
        functools.partial(kernel, owners, bands),
        out_shape=(out, out, tiles(height), tiles(4 * blocks), cross),
        in_specs=[hbm] * 5 + [pl.BlockSpec(memory_space=pltpu.SMEM), vmem, vmem],
        out_specs=(vmem, vmem, vmem, vmem, [vmem] * len(LATE)),
        scratch_shapes=[
            whole,
            whole,
            whole,
            whole,
            pltpu.VMEM((slots, height, width), jnp.int32),
            whole,
            whole,
            whole,
            whole,
            whole,
            whole,
            tiles(2, slots, height + 2 * PAD),
            whole,
            pltpu.VMEM((tall + 2 * blocks, owners * tall), f32),
            tiles(3 * (tall + 2 * blocks)),
            tiles(tall + 8),
            tiles(2, slots + 8),
            tiles(owners, tall + 8),
            tiles(8, slots + 8),
            tiles(SWEEPS, tall),
            tiles(SWEEPS, 2, slots),
            tiles(SWEEPS - 1, owners, tall),
            tiles(SWEEPS - 1, 8, slots),
            tiles(height),
            pltpu.VMEM((width, height), f32),
            tiles(5, tall),
            tiles(6, tall),
            pltpu.VMEM((width, height), f32),
            tiles(tall),
            pltpu.VMEM((width, height), f32),
            tiles(SWEEPS, height),
            tiles(SWEEPS, 2 * blocks),
            tiles(4, blocks, DEEP),
            tiles(blocks, DEEP),
            tiles(blocks, DEEP),
            tiles(2, blocks, DEEP + 2 * PAD),
            tiles(3 * slots),
            tiles(4, 4 * blocks),
            tiles(3, 4 * blocks),
            pltpu.SMEM((4 * blocks,), jnp.int32),
            pltpu.SMEM((4 * blocks,), f32),
            [tiles(4, 2 * blocks, count) for _, count in EARLY],
            [tiles(4, 2 * blocks, count) for _, count in EARLY],
            [tiles(4, blocks, count) for _, count in EARLY],
            [tiles(4, blocks, count) for _, count in EARLY],
            [tiles(2, 2 * blocks, count) for _, count in LATE],
            [tiles(2, 2 * blocks, count) for _, count in LATE],
            [tiles(2, blocks, count) for _, count in LATE],
            dma((5,)),
            dma((SWEEPS,)),
            dma((SWEEPS,)),
            dma((SWEEPS,)),
            dma((SWEEPS,)),
            dma((2 * WINDOWS,)),
            dma((2 * WINDOWS,)),
            dma((4 * len(LATE),)),
            dma((4 * len(LATE),)),
            dma((3,)),
            dma((3,)),
        ],
        compiler_params=pltpu.CompilerParams(
            collective_id=0, has_side_effects=True, vmem_limit_bytes=56 * 1024 * 1024
        ),
        name="barotropic_solve",
    )(
        depth,
        cell_dx,
        cell_dy,
        forcing,
        land_mask,
        dest_block,
        dest_block.reshape(1, slots),
        neighbours,
    )
    whole = jax.ShapeDtypeStruct((blocks, height, width), f32)
    hbm = pl.BlockSpec(memory_space=pltpu.HBM)
    return pl.pallas_call(
        finish,
        out_shape=(whole, whole),
        in_specs=[vmem, vmem, vmem, vmem, [vmem] * len(LATE)],
        out_specs=(hbm, hbm),
        scratch_shapes=[
            tiles(blocks, height - TOP),
            tiles(blocks, height - TOP),
            dma((4,)),
        ],
        compiler_params=pltpu.CompilerParams(vmem_limit_bytes=16 * 1024 * 1024),
        name="barotropic_finish",
    )(*parts)


def solution(mesh):
    blocks3 = P(("blk", "grp"), None, None)
    flat = P(("blk", "grp"))
    in_specs = (blocks3,) * 5 + (flat, flat, P(("blk", "grp"), None))
    return jax.shard_map(
        functools.partial(per_device, mesh.shape["blk"], mesh.shape["grp"]),
        mesh=mesh,
        in_specs=in_specs,
        out_specs=(blocks3, blocks3),
        check_vma=False,
    )
```

```python
import functools

import jax
import jax.numpy as jnp
from jax import lax
from jax.experimental import pallas as pl
from jax.experimental.pallas import tpu as pltpu
from jax.sharding import PartitionSpec as P

SWEEPS = 4
TAU_MASS = 6.0
LOW_BOUND = 0.2
HIGH_BOUND = 1.9
CHUNK = 32
PAD = 8
GATHER = 16
PAIR = 4
EARLY = ((0, 16), (16, 16), (32, 24))
DEEP = 56
TOP = DEEP - 8
NEW = ((0, 32), (32, 24))
LATE = ((48, 24), (72, 24), (96, 32))
WINDOWS = len(EARLY)
STEPS = ((40, 32), (72, 24), (96, 32))
MESH = pl.DeviceIdType.MESH
EXACT = lax.Precision.HIGHEST


def pick_dot(pick, data):
    pick = pick.astype(jnp.bfloat16)
    total = None
    for _ in range(3):
        part = data.astype(jnp.bfloat16)
        data = data - part.astype(jnp.float32)
        term = jnp.dot(pick, part, preferred_element_type=jnp.float32)
        total = term if total is None else total + term
    return total


def relax_weights():
    alpha = 2.0 / (HIGH_BOUND - LOW_BOUND)
    beta = (HIGH_BOUND + LOW_BOUND) / (HIGH_BOUND - LOW_BOUND)
    gamma = beta / alpha
    weight = 2.0 / gamma
    weights = []
    for _ in range(SWEEPS - 1):
        weight = 1.0 / (gamma - weight / (4.0 * alpha**2))
        weights.append((weight, gamma * weight - 1.0))
    return gamma, weights


def kernel(
    owners,
    bands,
    depth_hbm,
    dx_hbm,
    dy_hbm,
    forcing_hbm,
    mask_hbm,
    dest_smem,
    dest_row,
    neigh,
    sol_out,
    res_out,
    fix_cols,
    fix_rows,
    cross_in,
    depth_v,
    dx_v,
    dy_v,
    forcing_v,
    mask_v,
    coef_x,
    coef_y,
    coef_d,
    inv_d,
    source,
    update,
    field,
    resid,
    pick_rows,
    pick_cols,
    first_rows,
    first_cols,
    band_first,
    side_first,
    edge_rows,
    edge_cols,
    band_rows,
    side_cols,
    col_tile,
    col_turned,
    row_raw,
    row_coefs,
    col_coefs,
    inner_cols,
    filled,
    halo_cols,
    new_top,
    new_coefs,
    new_inv,
    new_update,
    new_field,
    fix_source,
    fix_out,
    fix_in,
    find,
    have,
    near_out,
    near_in,
    far_out,
    far_in,
    late_out,
    late_in,
    cross_out,
    load_sems,
    row_send,
    row_recv,
    col_send,
    col_recv,
    early_send,
    early_recv,
    late_send,
    late_recv,
    fix_send,
    fix_recv,
):
    slots, height, width = depth_v.shape
    blocks = neigh.shape[0]
    tall = 2 * slots
    me = lax.axis_index("blk")
    band = lax.axis_index("grp")
    core = me % 2
    sibling = me + 1 - 2 * core
    base = me - me % 4
    inner = me % 4
    across = base + (inner + 2) % 4
    east_band = (band + 1) % bands
    west_band = (band + bands - 1) % bands

    loads = [
        pltpu.make_async_copy(
            src.at[:, pl.ds(h * (height // 2), height // 2), :],
            dst.at[:, pl.ds(h * (height // 2), height // 2), :],
            load_sems.at[5 * h + i],
        )
        for h in range(2)
        for i, (src, dst) in enumerate(
            (
                (dx_hbm, dx_v),
                (dy_hbm, dy_v),
                (depth_hbm, depth_v),
                (mask_hbm, mask_v),
                (forcing_hbm, forcing_v),
            )
        )
    ]
    barrier = pltpu.get_barrier_semaphore()
    wrap = (band == 0).astype(jnp.int32)
    far_band = west_band * wrap + east_band * (1 - wrap)
    other_band = east_band * wrap + west_band * (1 - wrap)
    for side in (far_band, other_band):
        for step in (2, 3, 1, 0):
            pl.semaphore_signal(
                barrier,
                inc=1,
                device_id=(base + (inner + step) % 4, side),
                device_id_type=MESH,
            )
    for step in range(1, owners):
        pl.semaphore_signal(
            barrier, inc=1, device_id=((me + step) % owners, band), device_id_type=MESH
        )

    for load in loads:
        load.start()

    first_rows[tall:, :] = jnp.zeros((8, width), jnp.float32)
    first_rows[tall : tall + blocks, 0:8] = (neigh[...] + 1).astype(jnp.float32)
    first_rows[tall + blocks : tall + blocks + 1, 0:slots] = (dest_row[...] + 1).astype(
        jnp.float32
    )
    table = first_rows[tall:, :]
    first_cols[0, slots:, :] = table
    first_cols[1, slots:, :] = table

    targets = (me, sibling, across, base + (sibling % 4 + 2) % 4)
    for t, target in enumerate(targets):
        for j in range(blocks):
            wanted = (target * bands + band) * blocks + j
            place = jnp.int32(0)
            count = jnp.int32(0)
            for s in range(slots):
                hit = dest_smem[s] == wanted
                place = jnp.where(hit, s, place)
                count = jnp.where(hit, 1, count)
            find[t * blocks + j] = place
            have[t * blocks + j] = count.astype(jnp.float32)

    gamma, weights = relax_weights()

    def coefficients(dx, dy, deep, src):
        area = dx * dy
        scaled = deep / area
        cx = scaled * (dy * dy)
        cy = scaled * (dx * dx)
        cd = 2.5 * (cx + cy) + TAU_MASS * area
        inv = 1.0 / cd
        return cx, cy, cd, inv, src, src * (inv * (1.0 / gamma))

    def gather(r, carry):
        rows = pl.ds(pl.multiple_of(r * GATHER, GATHER), GATHER)
        quad = lax.broadcasted_iota(jnp.int32, (GATHER, width), 1) // 4
        tile = jnp.zeros((GATHER, width), jnp.float32)
        for s in range(slots):
            ocean = mask_v[s, rows, :].astype(jnp.float32)
            parts = (
                dx_v[s, rows, :],
                dy_v[s, rows, :],
                depth_v[s, rows, :] * ocean,
                forcing_v[s, rows, :] * ocean,
            )
            for i, part in enumerate(parts):
                at = i * slots + s
                tile = jnp.where(quad == at, pltpu.roll(part, 2 + 4 * at, 1), tile)
        col_tile[rows, :] = tile
        return carry

    part = height // GATHER // 2
    for h in range(2):
        for load in loads[5 * h : 5 * h + 5]:
            load.wait()
        lax.fori_loop(h * part, (h + 1) * part, gather, 0)
    col_turned[...] = col_tile[...].T
    for i, ref in enumerate((dx_v, dy_v, depth_v, forcing_v, mask_v)):
        for s in range(slots):
            for at, row in ((s, 0), (slots + s, height - 1)):
                value = ref[s, row : row + 1, :]
                row_raw[i, at : at + 1, :] = value.astype(jnp.float32)
    sides_of = [
        [col_turned[pl.ds(4 * slots * i + c, slots, stride=4), :] for i in range(4)]
        for c in range(4)
    ]
    for i, part in enumerate(
        coefficients(*(jnp.concatenate([e, w], axis=0) for e, w in zip(sides_of[1], sides_of[2])))
    ):
        col_coefs[i * tall : (i + 1) * tall, :] = part
    start = coefficients(
        *(jnp.concatenate([e, w], axis=0) for e, w in zip(sides_of[0], sides_of[3]))
    )[5]
    inner_cols[...] = start
    ocean = row_raw[4]
    for i, part in enumerate(
        coefficients(row_raw[0], row_raw[1], row_raw[2] * ocean, row_raw[3] * ocean)
    ):
        row_coefs[i] = part
    edge_rows[0] = row_coefs[5]
    edge_cols[0] = col_coefs[5 * tall : 6 * tall, :].reshape(2, slots, width)
    first_rows[0:tall, :] = row_coefs[5]
    first_cols[0, 0:slots, :] = col_coefs[5 * tall + slots : 6 * tall, :]
    first_cols[1, 0:slots, :] = col_coefs[5 * tall : 5 * tall + slots, :]

    def prepare(r0):
        rows = pl.ds(r0, CHUNK)

        def one(s, carry):
            ocean = mask_v[s, rows, :].astype(jnp.float32)
            parts = coefficients(
                dx_v[s, rows, :],
                dy_v[s, rows, :],
                depth_v[s, rows, :] * ocean,
                forcing_v[s, rows, :] * ocean,
            )
            for ref, part in zip((coef_x, coef_y, coef_d, inv_d, source, update), parts):
                ref[s, rows, :] = part
            field[0, s, pl.ds(PAD + r0, CHUNK), :] = parts[5]
            return carry

        lax.fori_loop(0, slots, one, 0)

    def send_cols(k):
        wrap = (band == 0).astype(jnp.int32)
        sides = ((wrap, west_band * wrap + east_band * (1 - wrap)),)
        sides = sides + ((1 - wrap, east_band * wrap + west_band * (1 - wrap)),)
        for to_west, side in sides:
            for step in (2, 3, 1, 0):
                slot = step + 4 * (1 - to_west)
                if k == 0:
                    src, dst = first_cols.at[1 - to_west], side_first.at[slot]
                else:
                    src, dst = edge_cols.at[k, to_west], side_cols.at[k - 1, slot]
                pltpu.make_async_remote_copy(
                    src_ref=src,
                    dst_ref=dst,
                    send_sem=col_send.at[k],
                    recv_sem=col_recv.at[k],
                    device_id=(base + (inner + step) % 4, side),
                    device_id_type=MESH,
                ).start()

    def send_rows(k):
        for step in range(1, owners):
            if k == 0:
                src, dst = first_rows, band_first.at[owners - step]
            else:
                src, dst = edge_rows.at[k], band_rows.at[k - 1, owners - step]
            pltpu.make_async_remote_copy(
                src_ref=src,
                dst_ref=dst,
                send_sem=row_send.at[k],
                recv_sem=row_recv.at[k],
                device_id=((me + step) % owners, band),
                device_id_type=MESH,
            ).start()
        if k == 0:
            band_first[0] = first_rows[...]
        else:
            band_rows[k - 1, 0] = edge_rows[k]

    def take(ref, sem):
        pltpu.make_async_copy(ref, ref, sem).wait()

    def rows_landed(k):
        return (band_first if k == 0 else band_rows.at[k - 1]).at[pl.ds(1, owners - 1)]

    def cols_landed(k):
        return side_first if k == 0 else side_cols.at[k - 1]

    def build_picks():
        lanes = lax.broadcasted_iota(jnp.int32, (tall, width), 1)
        rows = lax.broadcasted_iota(jnp.int32, (tall, width), 0)
        ids_here = first_rows[tall:, :]
        mine = jnp.broadcast_to(ids_here[blocks : blocks + 1, :], (tall, width))
        own = jnp.sum(jnp.where(lanes == rows % slots, mine, 0.0), axis=1, keepdims=True)
        group_ids = ((base + lanes // 8) * bands + band) * blocks + lanes % 8 + 1
        known = (lanes % 8 < blocks) & (lanes < 32)
        match = jnp.where(known & (own == group_ids.astype(jnp.float32)), 1.0, 0.0)
        listed = jnp.concatenate(
            [band_first[(base + g - me + owners) % owners, tall:, :] for g in range(4)], axis=0
        )
        need = jnp.dot(
            match[:, :32], listed, precision=EXACT, preferred_element_type=jnp.float32
        )
        all_rows = tall + 2 * blocks
        lanes = lax.broadcasted_iota(jnp.int32, (all_rows, width), 1)
        rows = lax.broadcasted_iota(jnp.int32, (all_rows, width), 0)
        second = ((rows >= slots) & (rows < tall)) | (rows >= tall + blocks)
        lower = rows[0:tall] >= slots
        low = lax.broadcasted_iota(jnp.int32, (8, width), 1) < slots
        per_tile = width // tall
        wanted = jnp.concatenate(
            [
                jnp.where(lower, need[:, 1:2], need[:, 0:1]),
                jnp.broadcast_to(ids_here[0:blocks, 0:1], (blocks, width)),
                jnp.broadcast_to(ids_here[0:blocks, 1:2], (blocks, width)),
            ],
            axis=0,
        )
        for q in range(owners // per_tile):
            ids = jnp.zeros((8, width), jnp.float32)
            for d in range(per_tile):
                tile = jnp.where(low, band_first[q * per_tile + d, tall:, :], 0.0)
                twice = tile + pltpu.roll(tile, slots, 1)
                ids = ids + (pltpu.roll(twice, tall * d, 1) if d else twice)
            id_row = jnp.broadcast_to(ids[blocks : blocks + 1, :], (all_rows, width))
            bottom = (lanes % tall) // slots == 1
            good = (wanted == id_row) & (id_row > 0.0) & (bottom != second)
            pick_rows[:, q * width : (q + 1) * width] = jnp.where(good, 1.0, 0.0)
        ids = jnp.zeros((8, width), jnp.float32)
        for d in range(8):
            tile = jnp.where(low, side_first[d, slots:, :], 0.0)
            ids = ids + (pltpu.roll(tile, slots * d, 1) if d else tile)
        id_row = jnp.broadcast_to(ids[blocks : blocks + 1, :], (all_rows, width))
        western = lanes >= 4 * slots
        for i, (east_of, west_of) in enumerate(((2, 3), (4, 5), (6, 7))):
            wanted = jnp.concatenate(
                [
                    jnp.where(
                        lower, need[:, west_of : west_of + 1], need[:, east_of : east_of + 1]
                    ),
                    jnp.broadcast_to(ids_here[0:blocks, east_of : east_of + 1], (blocks, width)),
                    jnp.broadcast_to(ids_here[0:blocks, west_of : west_of + 1], (blocks, width)),
                ],
                axis=0,
            )
            good = (wanted == id_row) & (id_row > 0.0) & (western == second)
            pick_cols[all_rows * i : all_rows * (i + 1), :] = jnp.where(good, 1.0, 0.0)

    all_rows = tall + 2 * blocks
    lanes = lax.broadcasted_iota(jnp.int32, (tall, width), 1)
    start = lanes == 0
    end = lanes == width - 1

    def take_rows(k):
        take(rows_landed(k), row_recv.at[k])
        if k == 0:
            take(cols_landed(k), col_recv.at[k])
            build_picks()
        per_tile = width // tall
        got = jnp.zeros((all_rows, width), jnp.float32)
        for q in range(owners // per_tile):
            part = pl.ds(q * per_tile, per_tile)
            edges = band_first[part, 0:tall, :] if k == 0 else band_rows[k - 1, part]
            got = got + pick_dot(
                pick_rows[:, q * width : (q + 1) * width], edges.reshape(width, width)
            )
        return got

    def take_cols(k):
        if k:
            take(cols_landed(k), col_recv.at[k])
        count = 8 * slots
        edges = side_first[:, 0:slots, :] if k == 0 else side_cols[k - 1]
        cols = pick_dot(pick_cols[:, 0:count], edges.reshape(count, width))
        at = lax.broadcasted_iota(jnp.int32, (all_rows, width), 1)
        straight = cols[0:all_rows]
        above = jnp.where(at == width - 1, cols[all_rows : 2 * all_rows], straight)
        below = jnp.where(at == 0, cols[2 * all_rows : 3 * all_rows], straight)
        slanted = pltpu.roll(above, 1, 1) + pltpu.roll(below, width - 1, 1)
        return straight, slanted

    def put_halo(k, got, straight, slanted):
        now = k % 2
        if k < SWEEPS - 1:
            for s in range(slots):
                field[now, s, PAD - 1 : PAD, :] = got[s : s + 1, :]
                field[now, s, PAD + height : PAD + height + 1, :] = got[
                    slots + s : slots + s + 1, :
                ]
        new_top[k] = got[tall:]
        for i, tile in enumerate((straight, slanted)):
            for h in range(2):
                filled[pl.ds(tall * i + h, slots, stride=2), :] = tile[slots * h : slots * (h + 1)]
                filled[pl.ds(2 * tall + 2 * blocks * i + h, blocks, stride=2), :] = tile[
                    tall + blocks * h : tall + blocks * (h + 1)
                ]
        halo_cols[k] = filled[...].T

    def exchange(k):
        now = k % 2
        every = take_rows(k)
        got = every[0:tall]

        def spread(value, before, after):
            left = jnp.where(start, before, pltpu.roll(value, 1, 1))
            return left + jnp.where(end, after, pltpu.roll(value, width - 1, 1))

        def ends(tile, at):
            part = tile[at : at + slots]
            return jnp.concatenate([part[:, 0:1], part[:, width - 1 : width]], axis=0)

        def sides(at, deep):
            part = got[at : at + slots]
            far = width - 1 - deep
            return jnp.concatenate([part[:, far : far + 1], part[:, deep : deep + 1]], axis=0)

        def known(coefs, center, level, vertical, slant):
            cx, cy, cd, _, src = coefs
            slant = 0.125 * slant
            return src - cd * center + cx * (level + slant) + cy * (vertical + slant)

        col_now = [col_coefs[i * tall : (i + 1) * tall, :] for i in range(5)]
        center = edge_cols[k].reshape(tall, width)
        inside = inner_cols[...]
        vertical = spread(center, sides(0, 0), sides(slots, 0))
        slant = spread(inside, sides(0, 1), sides(slots, 1))
        col_part = known(col_now, center, inside, vertical, slant)
        col_slant = 0.125 * (col_now[0] + col_now[1])

        row_now = [row_coefs[i] for i in range(5)]
        row_center = edge_rows[k]
        inside = jnp.concatenate(
            [field[now, s, PAD + 1 : PAD + 2, :] for s in range(slots)]
            + [field[now, s, PAD + height - 2 : PAD + height - 1, :] for s in range(slots)],
            axis=0,
        )
        vertical = inside + got
        level = spread(row_center, 0.0, 0.0)
        slant = spread(vertical, 0.0, 0.0)
        row_part = known(row_now, row_center, level, vertical, slant)
        row_slant = 0.125 * (row_now[0] + row_now[1])
        if k < SWEEPS - 1:
            weight, keep = weights[k]
            col_scale = weight * col_now[3]
            row_scale = weight * row_now[3]
            col_keep = keep * col_coefs[5 * tall : 6 * tall, :]
            row_keep = keep * row_coefs[5]

        straights, slants = take_cols(k)
        straight, slanted = straights[0:tall], slants[0:tall]
        left = col_part + col_now[0] * straight + col_slant * slanted
        if k == SWEEPS - 1:
            fix_source[slots:, :] = left
        else:
            change = col_scale * left + col_keep
            col_coefs[5 * tall : 6 * tall, :] = change
            edge_cols[k + 1] = (center + change).reshape(2, slots, width)
            send_cols(k + 1)

        def outer(tile):
            before, after = ends(tile, slots), ends(tile, 0)
            return jnp.where(start, before, 0.0) + jnp.where(end, after, 0.0)

        left = row_part + row_now[0] * outer(straight) + row_slant * outer(slanted)
        if k == SWEEPS - 1:
            fix_source[0:slots, :] = left[slots:]
        else:
            change = row_scale * left + row_keep
            row_coefs[5] = change
            edge_rows[k + 1] = row_center + change
            send_rows(k + 1)
        return every, straights, slants

    def around(value, halo):
        at = lax.broadcasted_iota(jnp.int32, value.shape, 1)
        left = jnp.where(at == 0, halo, pltpu.roll(value, 1, 1))
        right = jnp.where(at == width - 1, halo, pltpu.roll(value, width - 1, 1))
        return left + right

    def balance(f, s, r0, size, level, vertical, slant):
        rows = pl.ds(r0, size)
        slant = 0.125 * slant
        return (
            source[s, rows, :]
            - coef_d[s, rows, :] * field[f, s, pl.ds(PAD + r0, size), :]
            + coef_x[s, rows, :] * (level + slant)
            + coef_y[s, rows, :] * (vertical + slant)
        )

    def columns(f, s, r0, size):
        center = field[f, s, pl.ds(PAD + r0, size), :]
        north = field[f, s, pl.ds(PAD + r0 - 1, size), :]
        south = field[f, s, pl.ds(PAD + r0 + 1, size), :]
        return center, north + south

    def sweep(k, pieces, group, closed=True):
        now = k % 2
        weight, keep = weights[k]
        for r0, size in pieces:
            rows = pl.ds(r0, size)
            cols = halo_cols[k, rows, :] if closed else None
            for first in range(0, slots, group):
                done = []
                for s in range(first, first + group):
                    center, vertical = columns(now, s, r0, size)
                    if closed:
                        level = around(center, pltpu.roll(cols, width - 1 - 2 * s, 1))
                        slant = around(vertical, pltpu.roll(cols, width - 1 - tall - 2 * s, 1))
                    else:
                        level, slant = beside(center), beside(vertical)
                    left = balance(now, s, r0, size, level, vertical, slant)
                    change = weight * left * inv_d[s, rows, :] + keep * update[s, rows, :]
                    done.append((s, change, center + change))
                for s, change, fresh in done:
                    update[s, rows, :] = change
                    field[1 - now, s, pl.ds(PAD + r0, size), :] = fresh

    def beside(value):
        return pltpu.roll(value, 1, 1) + pltpu.roll(value, width - 1, 1)

    def capture(first, load):
        quad = lax.broadcasted_iota(jnp.int32, (CHUNK, width), 1) // 4
        for r0 in range(first, height, CHUNK):
            tile = jnp.zeros((CHUNK, width), jnp.float32)
            for s in range(slots):
                tile = jnp.where(quad == s, pltpu.roll(load(s, r0), 2 + 4 * s, 1), tile)
            col_tile[pl.ds(r0, CHUNK), :] = tile
        col_turned[...] = col_tile[...].T

    def turn_columns(f, first=0):
        capture(first, lambda s, r0: field[f, s, pl.ds(PAD + r0, CHUNK), :])
        for h in range(2):
            inner_cols[slots * h : slots * (h + 1), :] = col_turned[
                pl.ds(3 * h, slots, stride=4), :
            ]

    last = (SWEEPS - 1) % 2

    def remainder(r0, size, group):
        for first in range(0, slots, group):
            done = []
            for s in range(first, first + group):
                center, vertical = columns(last, s, r0, size)
                level, slant = beside(center), beside(vertical)
                done.append((s, balance(last, s, r0, size, level, vertical, slant)))
            for s, left in done:
                resid[s, pl.ds(r0, size), :] = left

    def send_to(src, dst, sends, recvs, at, device):
        pltpu.make_async_remote_copy(
            src_ref=src,
            dst_ref=dst,
            send_sem=sends.at[at],
            recv_sem=recvs.at[at],
            device_id=(device, band),
            device_id_type=MESH,
        ).start()

    early = (coef_x, coef_y, coef_d, source)

    def early_start(w):
        rows = pl.ds(*EARLY[w])

        def fill(i, carry):
            for t in range(2):
                at = (1 + 2 * t) * blocks + i
                slot, live = find[at], have[at]
                for f, ref in enumerate(early):
                    near_out[w][f, t * blocks + i] = ref[slot, rows, :] * live
            return carry

        lax.fori_loop(0, blocks, fill, 0)
        send_to(near_out[w], near_in[w], early_send, early_recv, w, sibling)

    def early_cross(w):
        rows = pl.ds(*EARLY[w])
        take(near_in[w], early_recv.at[w])

        def fill(i, carry):
            at = 2 * blocks + i
            slot, live = find[at], have[at]
            for f, ref in enumerate(early):
                far_out[w][f, i] = ref[slot, rows, :] * live + near_in[w][f, blocks + i]
            return carry

        lax.fori_loop(0, blocks, fill, 0)
        send_to(far_out[w], far_in[w], early_send, early_recv, WINDOWS + w, across)

    def early_finish(w):
        rows = pl.ds(*EARLY[w])
        take(far_in[w], early_recv.at[WINDOWS + w])

        def fill(i, carry):
            slot, live = find[i], have[i]
            for f, ref in enumerate(early):
                new_coefs[f, i, rows, :] = (
                    ref[slot, rows, :] * live + near_in[w][f, i] + far_in[w][f, i]
                )
            inv = 1.0 / new_coefs[2, i, rows, :]
            new_inv[i, rows, :] = inv
            start = new_coefs[3, i, rows, :] * (inv * (1.0 / gamma))
            new_update[i, rows, :] = start
            new_field[0, i, pl.ds(PAD + EARLY[w][0], EARLY[w][1]), :] = start
            return carry

        lax.fori_loop(0, blocks, fill, 0)

    def new_sweep(k):
        now = k % 2
        for i in range(blocks):
            new_field[now, i, PAD - 1 : PAD, :] = new_top[k, i : i + 1, :]
        for r0, size in NEW:
            rows = pl.ds(r0, size)
            cols = halo_cols[k, rows, :]
            done = []
            for i in range(blocks):
                center = new_field[now, i, pl.ds(PAD + r0, size), :]
                vertical = (
                    new_field[now, i, pl.ds(PAD + r0 - 1, size), :]
                    + new_field[now, i, pl.ds(PAD + r0 + 1, size), :]
                )
                level = around(center, pltpu.roll(cols, width - 1 - 2 * tall - 2 * i, 1))
                slant = around(
                    vertical, pltpu.roll(cols, width - 1 - 2 * tall - 2 * blocks - 2 * i, 1)
                )
                slant = 0.125 * slant
                left = (
                    new_coefs[3, i, rows, :]
                    - new_coefs[2, i, rows, :] * center
                    + new_coefs[0, i, rows, :] * (level + slant)
                    + new_coefs[1, i, rows, :] * (vertical + slant)
                )
                if k == SWEEPS - 1:
                    done.append((left, None))
                else:
                    weight, keep = weights[k]
                    change = weight * left * new_inv[i, rows, :] + keep * new_update[i, rows, :]
                    done.append((center + change, change))
            kept = min(size, TOP - r0)
            for i, (fresh, change) in enumerate(done):
                if k == SWEEPS - 1:
                    res_out[i, pl.ds(r0, kept), :] = fresh[0:kept]
                else:
                    new_update[i, rows, :] = change
                    new_field[1 - now, i, pl.ds(PAD + r0, size), :] = fresh
                    if k == SWEEPS - 2:
                        sol_out[i, pl.ds(r0, kept), :] = fresh[0:kept]

    def rows_of(f, slot, r0, count):
        if f == 0:
            return field[last, slot, pl.ds(PAD + r0, count), :]
        return resid[slot, pl.ds(r0, count), :]

    def late_start(f, c):
        r0, count = LATE[c]

        def fill(i, carry):
            for t in range(2):
                at = (1 + 2 * t) * blocks + i
                late_out[c][f, t * blocks + i] = rows_of(f, find[at], r0, count) * have[at]
            return carry

        lax.fori_loop(0, blocks, fill, 0)
        at = f * len(LATE) + c
        send_to(late_out[c].at[f], late_in[c].at[f], late_send, late_recv, at, sibling)

    def late_cross(f, c):
        r0, count = LATE[c]
        at = f * len(LATE) + c
        take(late_in[c].at[f], late_recv.at[at])

        def fill(i, carry):
            at = 2 * blocks + i
            cross_out[c][f, i] = (
                rows_of(f, find[at], r0, count) * have[at] + late_in[c][f, blocks + i]
            )
            return carry

        lax.fori_loop(0, blocks, fill, 0)
        at = at + 2 * len(LATE)
        send_to(cross_out[c].at[f], cross_in[c].at[f], late_send, late_recv, at, across)

    def late_near(f, c, out):
        r0, count = LATE[c]

        def fill(i, carry):
            out[i, pl.ds(r0, count), :] = (
                rows_of(f, find[i], r0, count) * have[i] + late_in[c][f, i]
            )
            return carry

        lax.fori_loop(0, blocks, fill, 0)

    def send_fix():
        order = (me, sibling, across, base + (sibling % 4 + 2) % 4)
        fix_out[...] = jnp.zeros_like(fix_out)
        for t in range(4):
            for i in range(blocks):
                slot, live = find[t * blocks + i], have[t * blocks + i]
                east = fix_source[pl.ds(slots + slot, 1), :] * live
                west = fix_source[pl.ds(tall + slot, 1), :] * live
                south = fix_source[pl.ds(slot, 1), :] * live
                fix_out[t, 2 * i : 2 * i + 1, :] = east
                fix_out[t, 2 * i + 1 : 2 * i + 2, :] = west
                fix_out[t, 2 * blocks + i : 2 * blocks + i + 1, :] = south
        for t in range(1, 4):
            send_to(fix_out.at[t], fix_in.at[t - 1], fix_send, fix_recv, t - 1, order[t])

    def take_fix():
        for t in range(3):
            take(fix_in.at[t], fix_recv.at[t])
        total = fix_out[0] + fix_in[0] + fix_in[1] + fix_in[2]
        filled[0 : 4 * blocks, :] = total
        fix_cols[...] = filled[...].T
        fix_rows[...] = total

    for f in range(2):
        new_field[f] = jnp.zeros(new_field.shape[1:], jnp.float32)

    filled[...] = jnp.zeros_like(filled)
    pl.semaphore_wait(barrier, owners - 1 + 8)
    send_cols(0)
    send_rows(0)
    whole = tuple(range(0, height, CHUNK))
    prepare(whole[0])
    early_start(0)
    prepare(whole[1])
    for w in range(1, WINDOWS):
        early_start(w)
    early_cross(0)
    for r0 in whole[2:]:
        prepare(r0)
    for k in range(SWEEPS - 2):
        halo = exchange(k)
        early_cross(k + 1)
        put_halo(k, *halo)
        sweep(k, [(r0, CHUNK) for r0 in whole], PAIR)
        turn_columns(1 - k % 2)
    k = SWEEPS - 2
    halo = exchange(k)
    for w in range(SWEEPS - 1, WINDOWS):
        early_cross(w)
    put_halo(k, *halo)
    steps = len(LATE)
    for c in range(steps):
        sweep(k, (STEPS[c],), PAIR)
        late_start(0, c)
        if c:
            late_cross(0, c - 1)
    turn_columns(last)
    for c in range(steps):
        remainder(*LATE[c], PAIR)
        late_start(1, c)
        if c:
            late_cross(1, c - 1)
        else:
            late_cross(0, steps - 1)
    for w in range(WINDOWS):
        early_finish(w)
    for k in range(SWEEPS - 1):
        new_sweep(k)
    k = SWEEPS - 1
    halo = exchange(k)
    send_fix()
    late_cross(1, steps - 1)
    put_halo(k, *halo)
    new_sweep(k)
    for f, out in enumerate((sol_out, res_out)):
        for c in range(steps):
            late_near(f, c, out)
    take_fix()
    for at in range(2 * steps, 4 * steps):
        take(cross_in[at % steps].at[at // steps - 2], late_recv.at[at])

    for k in range(SWEEPS):
        take(rows_landed(k), row_send.at[k])
        take(cols_landed(k), col_send.at[k])
    for w in range(WINDOWS):
        take(near_out[w], early_send.at[w])
        take(far_out[w], early_send.at[WINDOWS + w])
    for f in range(2):
        for c in range(steps):
            take(late_out[c].at[f], late_send.at[f * steps + c])
            take(cross_out[c].at[f], late_send.at[(2 + f) * steps + c])
    for t in range(3):
        take(fix_in.at[t], fix_send.at[t])


def finish(near_sol, near_res, fix_cols, fix_rows, cross, sol_out, res_out, sol_v, res_v, sems):
    blocks, height, width = near_sol.shape
    top = pl.ds(0, TOP)
    rest = pl.ds(TOP, height - TOP)
    pairs = ((near_sol, sol_v, sol_out), (near_res, res_v, res_out))
    copies = []
    for f, (near, _, out) in enumerate(pairs):
        copies.append(
            pltpu.make_async_copy(near.at[:, top, :], out.at[:, top, :], sems.at[2 * f])
        )
        copies[-1].start()
    for f, (near, value_v, out) in enumerate(pairs):
        for c, (r0, count) in enumerate(LATE):
            rows = pl.ds(r0, count)
            at = lax.broadcasted_iota(jnp.int32, (count, width), 1)
            edge = (at == 0) | (at == width - 1)
            for i in range(blocks):
                value = near[i, rows, :] + cross[c][f, i]
                if f:
                    cols = pltpu.roll(fix_cols[rows, :], width - 1 - 2 * i, 1)
                    value = jnp.where(edge, cols, value)
                value_v[i, pl.ds(r0 - TOP, count), :] = value
        if f:
            for i in range(blocks):
                at = 2 * blocks + i
                value_v[i, height - TOP - 1 : height - TOP, :] = fix_rows[at : at + 1, :]
        copies.append(pltpu.make_async_copy(value_v, out.at[:, rest, :], sems.at[2 * f + 1]))
        copies[-1].start()
    for copy in copies:
        copy.wait()


def per_device(
    owners, bands, depth, cell_dx, cell_dy, forcing, land_mask, dest_block, source_slot, neighbours
):
    slots, height, width = depth.shape
    blocks = source_slot.shape[0]
    tall = 2 * slots
    f32 = jnp.float32
    hbm = pl.BlockSpec(memory_space=pl.ANY)
    vmem = pl.BlockSpec(memory_space=pltpu.VMEM)
    whole = pltpu.VMEM((slots, height, width), f32)
    dma = pltpu.SemaphoreType.DMA

    def tiles(*shape):
        return pltpu.VMEM((*shape, width), f32)

    out = tiles(blocks, height)
    cross = [tiles(2, blocks, count) for _, count in LATE]
    parts = pl.pallas_call(
        functools.partial(kernel, owners, bands),
        out_shape=(out, out, tiles(height), tiles(4 * blocks), cross),
        in_specs=[hbm] * 5 + [pl.BlockSpec(memory_space=pltpu.SMEM), vmem, vmem],
        out_specs=(vmem, vmem, vmem, vmem, [vmem] * len(LATE)),
        scratch_shapes=[
            whole,
            whole,
            whole,
            whole,
            pltpu.VMEM((slots, height, width), jnp.int32),
            whole,
            whole,
            whole,
            whole,
            whole,
            whole,
            tiles(2, slots, height + 2 * PAD),
            whole,
            pltpu.VMEM((tall + 2 * blocks, owners * tall), f32),
            tiles(3 * (tall + 2 * blocks)),
            tiles(tall + 8),
            tiles(2, slots + 8),
            tiles(owners, tall + 8),
            tiles(8, slots + 8),
            tiles(SWEEPS, tall),
            tiles(SWEEPS, 2, slots),
            tiles(SWEEPS - 1, owners, tall),
            tiles(SWEEPS - 1, 8, slots),
            tiles(height),
            pltpu.VMEM((width, height), f32),
            tiles(5, tall),
            tiles(6, tall),
            pltpu.VMEM((width, height), f32),
            tiles(tall),
            pltpu.VMEM((width, height), f32),
            tiles(SWEEPS, height),
            tiles(SWEEPS, 2 * blocks),
            tiles(4, blocks, DEEP),
            tiles(blocks, DEEP),
            tiles(blocks, DEEP),
            tiles(2, blocks, DEEP + 2 * PAD),
            tiles(3 * slots),
            tiles(4, 4 * blocks),
            tiles(3, 4 * blocks),
            pltpu.SMEM((4 * blocks,), jnp.int32),
            pltpu.SMEM((4 * blocks,), f32),
            [tiles(4, 2 * blocks, count) for _, count in EARLY],
            [tiles(4, 2 * blocks, count) for _, count in EARLY],
            [tiles(4, blocks, count) for _, count in EARLY],
            [tiles(4, blocks, count) for _, count in EARLY],
            [tiles(2, 2 * blocks, count) for _, count in LATE],
            [tiles(2, 2 * blocks, count) for _, count in LATE],
            [tiles(2, blocks, count) for _, count in LATE],
            dma((10,)),
            dma((SWEEPS,)),
            dma((SWEEPS,)),
            dma((SWEEPS,)),
            dma((SWEEPS,)),
            dma((2 * WINDOWS,)),
            dma((2 * WINDOWS,)),
            dma((4 * len(LATE),)),
            dma((4 * len(LATE),)),
            dma((3,)),
            dma((3,)),
        ],
        compiler_params=pltpu.CompilerParams(
            collective_id=0, has_side_effects=True, vmem_limit_bytes=56 * 1024 * 1024
        ),
        name="barotropic_solve",
    )(
        depth,
        cell_dx,
        cell_dy,
        forcing,
        land_mask,
        dest_block,
        dest_block.reshape(1, slots),
        neighbours,
    )
    whole = jax.ShapeDtypeStruct((blocks, height, width), f32)
    hbm = pl.BlockSpec(memory_space=pltpu.HBM)
    return pl.pallas_call(
        finish,
        out_shape=(whole, whole),
        in_specs=[vmem, vmem, vmem, vmem, [vmem] * len(LATE)],
        out_specs=(hbm, hbm),
        scratch_shapes=[
            tiles(blocks, height - TOP),
            tiles(blocks, height - TOP),
            dma((4,)),
        ],
        compiler_params=pltpu.CompilerParams(vmem_limit_bytes=16 * 1024 * 1024),
        name="barotropic_finish",
    )(*parts)


def solution(mesh):
    blocks3 = P(("blk", "grp"), None, None)
    flat = P(("blk", "grp"))
    in_specs = (blocks3,) * 5 + (flat, flat, P(("blk", "grp"), None))
    return jax.shard_map(
        functools.partial(per_device, mesh.shape["blk"], mesh.shape["grp"]),
        mesh=mesh,
        in_specs=in_specs,
        out_specs=(blocks3, blocks3),
        check_vma=False,
    )
```

```python
import functools

import jax
import jax.numpy as jnp
from jax import lax
from jax.experimental import pallas as pl
from jax.experimental.pallas import tpu as pltpu
from jax.sharding import PartitionSpec as P

SWEEPS = 4
TAU_MASS = 6.0
LOW_BOUND = 0.2
HIGH_BOUND = 1.9
CHUNK = 32
PAD = 8
GATHER = 16
PAIR = 4
EARLY = ((0, 16), (16, 16), (32, 16))
DEEP = 48
TOP = DEEP - 8
NEW = ((0, 24), (24, 24))
LATE = ((40, 32), (72, 32), (104, 24))
WINDOWS = len(EARLY)
STEPS = ((32, 40), (72, 32), (104, 24))
MESH = pl.DeviceIdType.MESH
EXACT = lax.Precision.HIGHEST


def pick_dot(pick, data):
    pick = pick.astype(jnp.bfloat16)
    total = None
    for _ in range(3):
        part = data.astype(jnp.bfloat16)
        data = data - part.astype(jnp.float32)
        term = jnp.dot(pick, part, preferred_element_type=jnp.float32)
        total = term if total is None else total + term
    return total


def relax_weights():
    alpha = 2.0 / (HIGH_BOUND - LOW_BOUND)
    beta = (HIGH_BOUND + LOW_BOUND) / (HIGH_BOUND - LOW_BOUND)
    gamma = beta / alpha
    weight = 2.0 / gamma
    weights = []
    for _ in range(SWEEPS - 1):
        weight = 1.0 / (gamma - weight / (4.0 * alpha**2))
        weights.append((weight, gamma * weight - 1.0))
    return gamma, weights


def kernel(
    owners,
    bands,
    depth_hbm,
    dx_hbm,
    dy_hbm,
    forcing_hbm,
    mask_hbm,
    dest_smem,
    dest_row,
    neigh,
    sol_out,
    res_out,
    fix_cols,
    fix_rows,
    cross_in,
    depth_v,
    dx_v,
    dy_v,
    forcing_v,
    mask_v,
    coef_x,
    coef_y,
    coef_d,
    inv_d,
    source,
    update,
    field,
    resid,
    pick_rows,
    pick_cols,
    first_rows,
    first_cols,
    band_first,
    side_first,
    edge_rows,
    edge_cols,
    band_rows,
    side_cols,
    col_tile,
    col_turned,
    row_raw,
    row_coefs,
    col_coefs,
    inner_cols,
    filled,
    halo_cols,
    new_top,
    new_coefs,
    new_inv,
    new_update,
    new_field,
    fix_source,
    fix_out,
    fix_in,
    patch_cols,
    find,
    have,
    near_out,
    near_in,
    far_out,
    far_in,
    late_out,
    late_in,
    cross_out,
    load_sems,
    row_send,
    row_recv,
    col_send,
    col_recv,
    early_send,
    early_recv,
    late_send,
    late_recv,
    fix_send,
    fix_recv,
):
    slots, height, width = depth_v.shape
    blocks = neigh.shape[0]
    tall = 2 * slots
    me = lax.axis_index("blk")
    band = lax.axis_index("grp")
    core = me % 2
    sibling = me + 1 - 2 * core
    base = me - me % 4
    inner = me % 4
    across = base + (inner + 2) % 4
    east_band = (band + 1) % bands
    west_band = (band + bands - 1) % bands

    loads = [
        pltpu.make_async_copy(
            src.at[:, pl.ds(h * (height // 2), height // 2), :],
            dst.at[:, pl.ds(h * (height // 2), height // 2), :],
            load_sems.at[5 * h + i],
        )
        for h in range(2)
        for i, (src, dst) in enumerate(
            (
                (dx_hbm, dx_v),
                (dy_hbm, dy_v),
                (depth_hbm, depth_v),
                (mask_hbm, mask_v),
                (forcing_hbm, forcing_v),
            )
        )
    ]
    barrier = pltpu.get_barrier_semaphore()
    wrap = (band == 0).astype(jnp.int32)
    far_band = west_band * wrap + east_band * (1 - wrap)
    other_band = east_band * wrap + west_band * (1 - wrap)
    for side in (far_band, other_band):
        for step in (2, 3, 1, 0):
            pl.semaphore_signal(
                barrier,
                inc=1,
                device_id=(base + (inner + step) % 4, side),
                device_id_type=MESH,
            )
    for step in range(1, owners):
        pl.semaphore_signal(
            barrier, inc=1, device_id=((me + step) % owners, band), device_id_type=MESH
        )

    for load in loads:
        load.start()

    first_rows[tall:, :] = jnp.zeros((8, width), jnp.float32)
    first_rows[tall : tall + blocks, 0:8] = (neigh[...] + 1).astype(jnp.float32)
    first_rows[tall + blocks : tall + blocks + 1, 0:slots] = (dest_row[...] + 1).astype(
        jnp.float32
    )
    table = first_rows[tall:, :]
    first_cols[0, slots:, :] = table
    first_cols[1, slots:, :] = table

    targets = (me, sibling, across, base + (sibling % 4 + 2) % 4)
    for t, target in enumerate(targets):
        for j in range(blocks):
            wanted = (target * bands + band) * blocks + j
            place = jnp.int32(0)
            count = jnp.int32(0)
            for s in range(slots):
                hit = dest_smem[s] == wanted
                place = jnp.where(hit, s, place)
                count = jnp.where(hit, 1, count)
            find[t * blocks + j] = place
            have[t * blocks + j] = count.astype(jnp.float32)

    gamma, weights = relax_weights()

    def coefficients(dx, dy, deep, src):
        area = dx * dy
        scaled = deep / area
        cx = scaled * (dy * dy)
        cy = scaled * (dx * dx)
        cd = 2.5 * (cx + cy) + TAU_MASS * area
        inv = 1.0 / cd
        return cx, cy, cd, inv, src, src * (inv * (1.0 / gamma))

    def gather(r, carry):
        rows = pl.ds(pl.multiple_of(r * GATHER, GATHER), GATHER)
        quad = lax.broadcasted_iota(jnp.int32, (GATHER, width), 1) // 4
        tile = jnp.zeros((GATHER, width), jnp.float32)
        for s in range(slots):
            ocean = mask_v[s, rows, :].astype(jnp.float32)
            parts = (
                dx_v[s, rows, :],
                dy_v[s, rows, :],
                depth_v[s, rows, :] * ocean,
                forcing_v[s, rows, :] * ocean,
            )
            for i, part in enumerate(parts):
                at = i * slots + s
                tile = jnp.where(quad == at, pltpu.roll(part, 2 + 4 * at, 1), tile)
        col_tile[rows, :] = tile
        return carry

    part = height // GATHER // 2
    for h in range(2):
        for load in loads[5 * h : 5 * h + 5]:
            load.wait()
        lax.fori_loop(h * part, (h + 1) * part, gather, 0)
    col_turned[...] = col_tile[...].T
    for i, ref in enumerate((dx_v, dy_v, depth_v, forcing_v, mask_v)):
        for s in range(slots):
            for at, row in ((s, 0), (slots + s, height - 1)):
                value = ref[s, row : row + 1, :]
                row_raw[i, at : at + 1, :] = value.astype(jnp.float32)
    sides_of = [
        [col_turned[pl.ds(4 * slots * i + c, slots, stride=4), :] for i in range(4)]
        for c in range(4)
    ]
    for i, part in enumerate(
        coefficients(*(jnp.concatenate([e, w], axis=0) for e, w in zip(sides_of[1], sides_of[2])))
    ):
        col_coefs[i * tall : (i + 1) * tall, :] = part
    start = coefficients(
        *(jnp.concatenate([e, w], axis=0) for e, w in zip(sides_of[0], sides_of[3]))
    )[5]
    inner_cols[...] = start
    ocean = row_raw[4]
    for i, part in enumerate(
        coefficients(row_raw[0], row_raw[1], row_raw[2] * ocean, row_raw[3] * ocean)
    ):
        row_coefs[i] = part
    edge_rows[0] = row_coefs[5]
    edge_cols[0] = col_coefs[5 * tall : 6 * tall, :].reshape(2, slots, width)
    first_rows[0:tall, :] = row_coefs[5]
    first_cols[0, 0:slots, :] = col_coefs[5 * tall + slots : 6 * tall, :]
    first_cols[1, 0:slots, :] = col_coefs[5 * tall : 5 * tall + slots, :]

    def prepare(r0):
        rows = pl.ds(r0, CHUNK)

        def one(s, carry):
            ocean = mask_v[s, rows, :].astype(jnp.float32)
            parts = coefficients(
                dx_v[s, rows, :],
                dy_v[s, rows, :],
                depth_v[s, rows, :] * ocean,
                forcing_v[s, rows, :] * ocean,
            )
            for ref, part in zip((coef_x, coef_y, coef_d, inv_d, source, update), parts):
                ref[s, rows, :] = part
            field[0, s, pl.ds(PAD + r0, CHUNK), :] = parts[5]
            return carry

        lax.fori_loop(0, slots, one, 0)

    def send_cols(k):
        wrap = (band == 0).astype(jnp.int32)
        sides = ((wrap, west_band * wrap + east_band * (1 - wrap)),)
        sides = sides + ((1 - wrap, east_band * wrap + west_band * (1 - wrap)),)
        for to_west, side in sides:
            for step in (2, 3, 1, 0):
                slot = step + 4 * (1 - to_west)
                if k == 0:
                    src, dst = first_cols.at[1 - to_west], side_first.at[slot]
                else:
                    src, dst = edge_cols.at[k, to_west], side_cols.at[k - 1, slot]
                pltpu.make_async_remote_copy(
                    src_ref=src,
                    dst_ref=dst,
                    send_sem=col_send.at[k],
                    recv_sem=col_recv.at[k],
                    device_id=(base + (inner + step) % 4, side),
                    device_id_type=MESH,
                ).start()

    def send_rows(k):
        for step in range(1, owners):
            if k == 0:
                src, dst = first_rows, band_first.at[owners - step]
            else:
                src, dst = edge_rows.at[k], band_rows.at[k - 1, owners - step]
            pltpu.make_async_remote_copy(
                src_ref=src,
                dst_ref=dst,
                send_sem=row_send.at[k],
                recv_sem=row_recv.at[k],
                device_id=((me + step) % owners, band),
                device_id_type=MESH,
            ).start()
        if k == 0:
            band_first[0] = first_rows[...]
        else:
            band_rows[k - 1, 0] = edge_rows[k]

    def take(ref, sem):
        pltpu.make_async_copy(ref, ref, sem).wait()

    def rows_landed(k):
        return (band_first if k == 0 else band_rows.at[k - 1]).at[pl.ds(1, owners - 1)]

    def cols_landed(k):
        return side_first if k == 0 else side_cols.at[k - 1]

    def build_picks():
        lanes = lax.broadcasted_iota(jnp.int32, (tall, width), 1)
        rows = lax.broadcasted_iota(jnp.int32, (tall, width), 0)
        ids_here = first_rows[tall:, :]
        mine = jnp.broadcast_to(ids_here[blocks : blocks + 1, :], (tall, width))
        own = jnp.sum(jnp.where(lanes == rows % slots, mine, 0.0), axis=1, keepdims=True)
        group_ids = ((base + lanes // 8) * bands + band) * blocks + lanes % 8 + 1
        known = (lanes % 8 < blocks) & (lanes < 32)
        match = jnp.where(known & (own == group_ids.astype(jnp.float32)), 1.0, 0.0)
        listed = jnp.concatenate(
            [band_first[(base + g - me + owners) % owners, tall:, :] for g in range(4)], axis=0
        )
        need = jnp.dot(
            match[:, :32], listed, precision=EXACT, preferred_element_type=jnp.float32
        )
        all_rows = tall + 2 * blocks
        lanes = lax.broadcasted_iota(jnp.int32, (all_rows, width), 1)
        rows = lax.broadcasted_iota(jnp.int32, (all_rows, width), 0)
        second = ((rows >= slots) & (rows < tall)) | (rows >= tall + blocks)
        lower = rows[0:tall] >= slots
        low = lax.broadcasted_iota(jnp.int32, (8, width), 1) < slots
        per_tile = width // tall
        wanted = jnp.concatenate(
            [
                jnp.where(lower, need[:, 1:2], need[:, 0:1]),
                jnp.broadcast_to(ids_here[0:blocks, 0:1], (blocks, width)),
                jnp.broadcast_to(ids_here[0:blocks, 1:2], (blocks, width)),
            ],
            axis=0,
        )
        for q in range(owners // per_tile):
            ids = jnp.zeros((8, width), jnp.float32)
            for d in range(per_tile):
                tile = jnp.where(low, band_first[q * per_tile + d, tall:, :], 0.0)
                twice = tile + pltpu.roll(tile, slots, 1)
                ids = ids + (pltpu.roll(twice, tall * d, 1) if d else twice)
            id_row = jnp.broadcast_to(ids[blocks : blocks + 1, :], (all_rows, width))
            bottom = (lanes % tall) // slots == 1
            good = (wanted == id_row) & (id_row > 0.0) & (bottom != second)
            pick_rows[:, q * width : (q + 1) * width] = jnp.where(good, 1.0, 0.0)
        ids = jnp.zeros((8, width), jnp.float32)
        for d in range(8):
            tile = jnp.where(low, side_first[d, slots:, :], 0.0)
            ids = ids + (pltpu.roll(tile, slots * d, 1) if d else tile)
        id_row = jnp.broadcast_to(ids[blocks : blocks + 1, :], (all_rows, width))
        western = lanes >= 4 * slots
        for i, (east_of, west_of) in enumerate(((2, 3), (4, 5), (6, 7))):
            wanted = jnp.concatenate(
                [
                    jnp.where(
                        lower, need[:, west_of : west_of + 1], need[:, east_of : east_of + 1]
                    ),
                    jnp.broadcast_to(ids_here[0:blocks, east_of : east_of + 1], (blocks, width)),
                    jnp.broadcast_to(ids_here[0:blocks, west_of : west_of + 1], (blocks, width)),
                ],
                axis=0,
            )
            good = (wanted == id_row) & (id_row > 0.0) & (western == second)
            pick_cols[all_rows * i : all_rows * (i + 1), :] = jnp.where(good, 1.0, 0.0)

    all_rows = tall + 2 * blocks
    lanes = lax.broadcasted_iota(jnp.int32, (tall, width), 1)
    start = lanes == 0
    end = lanes == width - 1

    def take_rows(k):
        take(rows_landed(k), row_recv.at[k])
        if k == 0:
            take(cols_landed(k), col_recv.at[k])
            build_picks()
        per_tile = width // tall
        got = jnp.zeros((all_rows, width), jnp.float32)
        for q in range(owners // per_tile):
            part = pl.ds(q * per_tile, per_tile)
            edges = band_first[part, 0:tall, :] if k == 0 else band_rows[k - 1, part]
            got = got + pick_dot(
                pick_rows[:, q * width : (q + 1) * width], edges.reshape(width, width)
            )
        return got

    def take_cols(k):
        if k:
            take(cols_landed(k), col_recv.at[k])
        count = 8 * slots
        edges = side_first[:, 0:slots, :] if k == 0 else side_cols[k - 1]
        cols = pick_dot(pick_cols[:, 0:count], edges.reshape(count, width))
        at = lax.broadcasted_iota(jnp.int32, (all_rows, width), 1)
        straight = cols[0:all_rows]
        above = jnp.where(at == width - 1, cols[all_rows : 2 * all_rows], straight)
        below = jnp.where(at == 0, cols[2 * all_rows : 3 * all_rows], straight)
        slanted = pltpu.roll(above, 1, 1) + pltpu.roll(below, width - 1, 1)
        return straight, slanted

    def put_halo(k, got, straight, slanted):
        now = k % 2
        if k < SWEEPS - 1:
            for s in range(slots):
                field[now, s, PAD - 1 : PAD, :] = got[s : s + 1, :]
                field[now, s, PAD + height : PAD + height + 1, :] = got[
                    slots + s : slots + s + 1, :
                ]
        new_top[k] = got[tall:]
        for i, tile in enumerate((straight, slanted)):
            for h in range(2):
                filled[pl.ds(tall * i + h, slots, stride=2), :] = tile[slots * h : slots * (h + 1)]
                filled[pl.ds(2 * tall + 2 * blocks * i + h, blocks, stride=2), :] = tile[
                    tall + blocks * h : tall + blocks * (h + 1)
                ]
        halo_cols[k] = filled[...].T

    def exchange(k):
        now = k % 2
        every = take_rows(k)
        got = every[0:tall]

        def spread(value, before, after):
            left = jnp.where(start, before, pltpu.roll(value, 1, 1))
            return left + jnp.where(end, after, pltpu.roll(value, width - 1, 1))

        def ends(tile, at):
            part = tile[at : at + slots]
            return jnp.concatenate([part[:, 0:1], part[:, width - 1 : width]], axis=0)

        def sides(at, deep):
            part = got[at : at + slots]
            far = width - 1 - deep
            return jnp.concatenate([part[:, far : far + 1], part[:, deep : deep + 1]], axis=0)

        def known(coefs, center, level, vertical, slant):
            cx, cy, cd, _, src = coefs
            slant = 0.125 * slant
            return src - cd * center + cx * (level + slant) + cy * (vertical + slant)

        col_now = [col_coefs[i * tall : (i + 1) * tall, :] for i in range(5)]
        center = edge_cols[k].reshape(tall, width)
        inside = inner_cols[...]
        vertical = spread(center, sides(0, 0), sides(slots, 0))
        slant = spread(inside, sides(0, 1), sides(slots, 1))
        col_part = known(col_now, center, inside, vertical, slant)
        col_slant = 0.125 * (col_now[0] + col_now[1])

        row_now = [row_coefs[i] for i in range(5)]
        row_center = edge_rows[k]
        inside = jnp.concatenate(
            [field[now, s, PAD + 1 : PAD + 2, :] for s in range(slots)]
            + [field[now, s, PAD + height - 2 : PAD + height - 1, :] for s in range(slots)],
            axis=0,
        )
        vertical = inside + got
        level = spread(row_center, 0.0, 0.0)
        slant = spread(vertical, 0.0, 0.0)
        row_part = known(row_now, row_center, level, vertical, slant)
        row_slant = 0.125 * (row_now[0] + row_now[1])
        if k < SWEEPS - 1:
            weight, keep = weights[k]
            col_scale = weight * col_now[3]
            row_scale = weight * row_now[3]
            col_keep = keep * col_coefs[5 * tall : 6 * tall, :]
            row_keep = keep * row_coefs[5]

        straights, slants = take_cols(k)
        straight, slanted = straights[0:tall], slants[0:tall]
        left = col_part + col_now[0] * straight + col_slant * slanted
        if k == SWEEPS - 1:
            fix_source[slots : 3 * slots, :] = left
        else:
            change = col_scale * left + col_keep
            col_coefs[5 * tall : 6 * tall, :] = change
            edge_cols[k + 1] = (center + change).reshape(2, slots, width)
            send_cols(k + 1)

        def outer(tile):
            before, after = ends(tile, slots), ends(tile, 0)
            return jnp.where(start, before, 0.0) + jnp.where(end, after, 0.0)

        left = row_part + row_now[0] * outer(straight) + row_slant * outer(slanted)
        if k == SWEEPS - 1:
            fix_source[0:slots, :] = left[slots:]
        else:
            change = row_scale * left + row_keep
            row_coefs[5] = change
            edge_rows[k + 1] = row_center + change
            send_rows(k + 1)
        return every, straights, slants

    def around(value, halo):
        at = lax.broadcasted_iota(jnp.int32, value.shape, 1)
        left = jnp.where(at == 0, halo, pltpu.roll(value, 1, 1))
        right = jnp.where(at == width - 1, halo, pltpu.roll(value, width - 1, 1))
        return left + right

    def balance(f, s, r0, size, level, vertical, slant):
        rows = pl.ds(r0, size)
        slant = 0.125 * slant
        return (
            source[s, rows, :]
            - coef_d[s, rows, :] * field[f, s, pl.ds(PAD + r0, size), :]
            + coef_x[s, rows, :] * (level + slant)
            + coef_y[s, rows, :] * (vertical + slant)
        )

    def columns(f, s, r0, size):
        center = field[f, s, pl.ds(PAD + r0, size), :]
        north = field[f, s, pl.ds(PAD + r0 - 1, size), :]
        south = field[f, s, pl.ds(PAD + r0 + 1, size), :]
        return center, north + south

    def sweep(k, pieces, group, closed=True):
        now = k % 2
        weight, keep = weights[k]
        for r0, size in pieces:
            rows = pl.ds(r0, size)
            cols = halo_cols[k, rows, :] if closed else None
            for first in range(0, slots, group):
                done = []
                for s in range(first, first + group):
                    center, vertical = columns(now, s, r0, size)
                    if closed:
                        level = around(center, pltpu.roll(cols, width - 1 - 2 * s, 1))
                        slant = around(vertical, pltpu.roll(cols, width - 1 - tall - 2 * s, 1))
                    else:
                        level, slant = beside(center), beside(vertical)
                    left = balance(now, s, r0, size, level, vertical, slant)
                    change = weight * left * inv_d[s, rows, :] + keep * update[s, rows, :]
                    done.append((s, change, center + change))
                for s, change, fresh in done:
                    update[s, rows, :] = change
                    field[1 - now, s, pl.ds(PAD + r0, size), :] = fresh

    def beside(value):
        return pltpu.roll(value, 1, 1) + pltpu.roll(value, width - 1, 1)

    def capture(first, load):
        quad = lax.broadcasted_iota(jnp.int32, (CHUNK, width), 1) // 4
        for r0 in range(first, height, CHUNK):
            tile = jnp.zeros((CHUNK, width), jnp.float32)
            for s in range(slots):
                tile = jnp.where(quad == s, pltpu.roll(load(s, r0), 2 + 4 * s, 1), tile)
            col_tile[pl.ds(r0, CHUNK), :] = tile
        col_turned[...] = col_tile[...].T

    def turn_columns(f, first=0):
        capture(first, lambda s, r0: field[f, s, pl.ds(PAD + r0, CHUNK), :])
        for h in range(2):
            inner_cols[slots * h : slots * (h + 1), :] = col_turned[
                pl.ds(3 * h, slots, stride=4), :
            ]

    last = (SWEEPS - 1) % 2

    def remainder(r0, size, group):
        for first in range(0, slots, group):
            done = []
            for s in range(first, first + group):
                center, vertical = columns(last, s, r0, size)
                level, slant = beside(center), beside(vertical)
                done.append((s, balance(last, s, r0, size, level, vertical, slant)))
            for s, left in done:
                resid[s, pl.ds(r0, size), :] = left

    def send_to(src, dst, sends, recvs, at, device):
        pltpu.make_async_remote_copy(
            src_ref=src,
            dst_ref=dst,
            send_sem=sends.at[at],
            recv_sem=recvs.at[at],
            device_id=(device, band),
            device_id_type=MESH,
        ).start()

    early = (coef_x, coef_y, coef_d, source)

    def early_start(w):
        rows = pl.ds(*EARLY[w])

        def fill(i, carry):
            for t in range(2):
                at = (1 + 2 * t) * blocks + i
                slot, live = find[at], have[at]
                for f, ref in enumerate(early):
                    near_out[w][f, t * blocks + i] = ref[slot, rows, :] * live
            return carry

        lax.fori_loop(0, blocks, fill, 0)
        send_to(near_out[w], near_in[w], early_send, early_recv, w, sibling)

    def early_cross(w):
        rows = pl.ds(*EARLY[w])
        take(near_in[w], early_recv.at[w])

        def fill(i, carry):
            at = 2 * blocks + i
            slot, live = find[at], have[at]
            for f, ref in enumerate(early):
                far_out[w][f, i] = ref[slot, rows, :] * live + near_in[w][f, blocks + i]
            return carry

        lax.fori_loop(0, blocks, fill, 0)
        send_to(far_out[w], far_in[w], early_send, early_recv, WINDOWS + w, across)

    def early_finish(w):
        rows = pl.ds(*EARLY[w])
        take(far_in[w], early_recv.at[WINDOWS + w])

        def fill(i, carry):
            slot, live = find[i], have[i]
            for f, ref in enumerate(early):
                new_coefs[f, i, rows, :] = (
                    ref[slot, rows, :] * live + near_in[w][f, i] + far_in[w][f, i]
                )
            inv = 1.0 / new_coefs[2, i, rows, :]
            new_inv[i, rows, :] = inv
            start = new_coefs[3, i, rows, :] * (inv * (1.0 / gamma))
            new_update[i, rows, :] = start
            new_field[0, i, pl.ds(PAD + EARLY[w][0], EARLY[w][1]), :] = start
            return carry

        lax.fori_loop(0, blocks, fill, 0)

    def new_sweep(k):
        now = k % 2
        for i in range(blocks):
            new_field[now, i, PAD - 1 : PAD, :] = new_top[k, i : i + 1, :]
        for r0, size in NEW:
            rows = pl.ds(r0, size)
            cols = halo_cols[k, rows, :]
            done = []
            for i in range(blocks):
                center = new_field[now, i, pl.ds(PAD + r0, size), :]
                vertical = (
                    new_field[now, i, pl.ds(PAD + r0 - 1, size), :]
                    + new_field[now, i, pl.ds(PAD + r0 + 1, size), :]
                )
                level = around(center, pltpu.roll(cols, width - 1 - 2 * tall - 2 * i, 1))
                slant = around(
                    vertical, pltpu.roll(cols, width - 1 - 2 * tall - 2 * blocks - 2 * i, 1)
                )
                slant = 0.125 * slant
                left = (
                    new_coefs[3, i, rows, :]
                    - new_coefs[2, i, rows, :] * center
                    + new_coefs[0, i, rows, :] * (level + slant)
                    + new_coefs[1, i, rows, :] * (vertical + slant)
                )
                if k == SWEEPS - 1:
                    done.append((left, None))
                else:
                    weight, keep = weights[k]
                    change = weight * left * new_inv[i, rows, :] + keep * new_update[i, rows, :]
                    done.append((center + change, change))
            kept = min(size, TOP - r0)
            for i, (fresh, change) in enumerate(done):
                if k == SWEEPS - 1:
                    res_out[i, pl.ds(r0, kept), :] = fresh[0:kept]
                else:
                    new_update[i, rows, :] = change
                    new_field[1 - now, i, pl.ds(PAD + r0, size), :] = fresh
                    if k == SWEEPS - 2:
                        sol_out[i, pl.ds(r0, kept), :] = fresh[0:kept]

    def rows_of(f, slot, r0, count):
        if f == 0:
            return field[last, slot, pl.ds(PAD + r0, count), :]
        return resid[slot, pl.ds(r0, count), :]

    def late_start(f, c):
        r0, count = LATE[c]

        def fill(i, carry):
            for t in range(2):
                at = (1 + 2 * t) * blocks + i
                late_out[c][f, t * blocks + i] = rows_of(f, find[at], r0, count) * have[at]
            return carry

        lax.fori_loop(0, blocks, fill, 0)
        at = f * len(LATE) + c
        send_to(late_out[c].at[f], late_in[c].at[f], late_send, late_recv, at, sibling)

    def late_cross(f, c):
        r0, count = LATE[c]
        at = f * len(LATE) + c
        take(late_in[c].at[f], late_recv.at[at])

        def fill(i, carry):
            at = 2 * blocks + i
            cross_out[c][f, i] = (
                rows_of(f, find[at], r0, count) * have[at] + late_in[c][f, blocks + i]
            )
            return carry

        lax.fori_loop(0, blocks, fill, 0)
        at = at + 2 * len(LATE)
        send_to(cross_out[c].at[f], cross_in[c].at[f], late_send, late_recv, at, across)

    def late_near(f, c, out):
        r0, count = LATE[c]

        def fill(i, carry):
            out[i, pl.ds(r0, count), :] = (
                rows_of(f, find[i], r0, count) * have[i] + late_in[c][f, i]
            )
            return carry

        lax.fori_loop(0, blocks, fill, 0)

    def patch():
        for h in range(2):
            filled[pl.ds(h, slots, stride=2), :] = edge_cols[SWEEPS - 1, h]
        patch_cols[...] = filled[...].T
        r0, size = STEPS[0]
        cols = patch_cols[pl.ds(r0, size), :]
        rows = pl.ds(PAD + r0, size)
        at = lax.broadcasted_iota(jnp.int32, (size, width), 1)
        edge = (at == 0) | (at == width - 1)
        for s in range(slots):
            sides = pltpu.roll(cols, width - 1 - 2 * s, 1)
            field[last, s, rows, :] = jnp.where(edge, sides, field[last, s, rows, :])

    def send_fix():
        fix_source[3 * slots :, :] = edge_cols[SWEEPS - 1].reshape(tall, width)
        fix_out[...] = jnp.zeros_like(fix_out)
        for t in range(4):
            for i in range(blocks):
                slot, live = find[t * blocks + i], have[t * blocks + i]
                places = (2 * blocks + i, 2 * i, 2 * i + 1, 3 * blocks + 2 * i, 3 * blocks + 2 * i + 1)
                for j, at in enumerate(places):
                    value = fix_source[pl.ds(slots * j + slot, 1), :]
                    fix_out[t, at : at + 1, :] = value * live
        for t in range(1, 4):
            send_to(fix_out.at[t], fix_in.at[t - 1], fix_send, fix_recv, t - 1, targets[t])

    def take_fix():
        for t in range(3):
            take(fix_in.at[t], fix_recv.at[t])
        total = fix_out[0] + fix_in[0] + fix_in[1] + fix_in[2]
        filled[0 : 6 * blocks, :] = total
        fix_cols[...] = filled[...].T
        fix_rows[...] = total

    for f in range(2):
        new_field[f] = jnp.zeros(new_field.shape[1:], jnp.float32)

    filled[...] = jnp.zeros_like(filled)
    pl.semaphore_wait(barrier, owners - 1 + 8)
    send_cols(0)
    send_rows(0)
    whole = tuple(range(0, height, CHUNK))
    prepare(whole[0])
    early_start(0)
    prepare(whole[1])
    for w in range(1, WINDOWS):
        early_start(w)
    early_cross(0)
    for r0 in whole[2:]:
        prepare(r0)
    for k in range(SWEEPS - 2):
        halo = exchange(k)
        early_cross(k + 1)
        put_halo(k, *halo)
        sweep(k, [(r0, CHUNK) for r0 in whole], PAIR)
        turn_columns(1 - k % 2)
    k = SWEEPS - 2
    steps = len(LATE)
    sweep(k, (STEPS[0],), PAIR, closed=False)
    late_start(0, 0)
    halo = exchange(k)
    for w in range(SWEEPS - 1, WINDOWS):
        early_cross(w)
    late_cross(0, 0)
    put_halo(k, *halo)
    patch()
    for c in range(1, steps):
        sweep(k, (STEPS[c],), PAIR)
        late_start(0, c)
        if c > 1:
            late_cross(0, c - 1)
    turn_columns(last)
    for c in range(steps):
        remainder(*LATE[c], PAIR)
        late_start(1, c)
        if c:
            late_cross(1, c - 1)
        else:
            late_cross(0, steps - 1)
    for w in range(WINDOWS):
        early_finish(w)
    for k in range(SWEEPS - 1):
        new_sweep(k)
    k = SWEEPS - 1
    halo = exchange(k)
    send_fix()
    late_cross(1, steps - 1)
    put_halo(k, *halo)
    new_sweep(k)
    for f, out in enumerate((sol_out, res_out)):
        for c in range(steps):
            late_near(f, c, out)
    take_fix()
    for at in range(2 * steps, 4 * steps):
        take(cross_in[at % steps].at[at // steps - 2], late_recv.at[at])

    for k in range(SWEEPS):
        take(rows_landed(k), row_send.at[k])
        take(cols_landed(k), col_send.at[k])
    for w in range(WINDOWS):
        take(near_out[w], early_send.at[w])
        take(far_out[w], early_send.at[WINDOWS + w])
    for f in range(2):
        for c in range(steps):
            take(late_out[c].at[f], late_send.at[f * steps + c])
            take(cross_out[c].at[f], late_send.at[(2 + f) * steps + c])
    for t in range(3):
        take(fix_in.at[t], fix_send.at[t])


def finish(near_sol, near_res, fix_cols, fix_rows, cross, sol_out, res_out, sol_v, res_v, sems):
    blocks, height, width = near_sol.shape
    top = pl.ds(0, TOP)
    rest = pl.ds(TOP, height - TOP)
    pairs = ((near_sol, sol_v, sol_out), (near_res, res_v, res_out))
    copies = []
    for f, (near, _, out) in enumerate(pairs):
        copies.append(
            pltpu.make_async_copy(near.at[:, top, :], out.at[:, top, :], sems.at[2 * f])
        )
        copies[-1].start()
    for f, (near, value_v, out) in enumerate(pairs):
        for c, (r0, count) in enumerate(LATE):
            rows = pl.ds(r0, count)
            at = lax.broadcasted_iota(jnp.int32, (count, width), 1)
            edge = (at == 0) | (at == width - 1)
            for i in range(blocks):
                value = near[i, rows, :] + cross[c][f, i]
                if f or not c:
                    first = 0 if f else 3 * blocks
                    cols = pltpu.roll(fix_cols[rows, :], width - 1 - first - 2 * i, 1)
                    value = jnp.where(edge, cols, value)
                value_v[i, pl.ds(r0 - TOP, count), :] = value
        if f:
            for i in range(blocks):
                at = 2 * blocks + i
                value_v[i, height - TOP - 1 : height - TOP, :] = fix_rows[at : at + 1, :]
        copies.append(pltpu.make_async_copy(value_v, out.at[:, rest, :], sems.at[2 * f + 1]))
        copies[-1].start()
    for copy in copies:
        copy.wait()


def per_device(
    owners, bands, depth, cell_dx, cell_dy, forcing, land_mask, dest_block, source_slot, neighbours
):
    slots, height, width = depth.shape
    blocks = source_slot.shape[0]
    tall = 2 * slots
    f32 = jnp.float32
    hbm = pl.BlockSpec(memory_space=pl.ANY)
    vmem = pl.BlockSpec(memory_space=pltpu.VMEM)
    whole = pltpu.VMEM((slots, height, width), f32)
    dma = pltpu.SemaphoreType.DMA

    def tiles(*shape):
        return pltpu.VMEM((*shape, width), f32)

    out = tiles(blocks, height)
    cross = [tiles(2, blocks, count) for _, count in LATE]
    parts = pl.pallas_call(
        functools.partial(kernel, owners, bands),
        out_shape=(out, out, tiles(height), tiles(6 * blocks), cross),
        in_specs=[hbm] * 5 + [pl.BlockSpec(memory_space=pltpu.SMEM), vmem, vmem],
        out_specs=(vmem, vmem, vmem, vmem, [vmem] * len(LATE)),
        scratch_shapes=[
            whole,
            whole,
            whole,
            whole,
            pltpu.VMEM((slots, height, width), jnp.int32),
            whole,
            whole,
            whole,
            whole,
            whole,
            whole,
            tiles(2, slots, height + 2 * PAD),
            whole,
            pltpu.VMEM((tall + 2 * blocks, owners * tall), f32),
            tiles(3 * (tall + 2 * blocks)),
            tiles(tall + 8),
            tiles(2, slots + 8),
            tiles(owners, tall + 8),
            tiles(8, slots + 8),
            tiles(SWEEPS, tall),
            tiles(SWEEPS, 2, slots),
            tiles(SWEEPS - 1, owners, tall),
            tiles(SWEEPS - 1, 8, slots),
            tiles(height),
            pltpu.VMEM((width, height), f32),
            tiles(5, tall),
            tiles(6, tall),
            pltpu.VMEM((width, height), f32),
            tiles(tall),
            pltpu.VMEM((width, height), f32),
            tiles(SWEEPS, height),
            tiles(SWEEPS, 2 * blocks),
            tiles(4, blocks, DEEP),
            tiles(blocks, DEEP),
            tiles(blocks, DEEP),
            tiles(2, blocks, DEEP + 2 * PAD),
            tiles(5 * slots),
            tiles(4, 6 * blocks),
            tiles(3, 6 * blocks),
            pltpu.VMEM((width, height), f32),
            pltpu.SMEM((4 * blocks,), jnp.int32),
            pltpu.SMEM((4 * blocks,), f32),
            [tiles(4, 2 * blocks, count) for _, count in EARLY],
            [tiles(4, 2 * blocks, count) for _, count in EARLY],
            [tiles(4, blocks, count) for _, count in EARLY],
            [tiles(4, blocks, count) for _, count in EARLY],
            [tiles(2, 2 * blocks, count) for _, count in LATE],
            [tiles(2, 2 * blocks, count) for _, count in LATE],
            [tiles(2, blocks, count) for _, count in LATE],
            dma((10,)),
            dma((SWEEPS,)),
            dma((SWEEPS,)),
            dma((SWEEPS,)),
            dma((SWEEPS,)),
            dma((2 * WINDOWS,)),
            dma((2 * WINDOWS,)),
            dma((4 * len(LATE),)),
            dma((4 * len(LATE),)),
            dma((3,)),
            dma((3,)),
        ],
        compiler_params=pltpu.CompilerParams(
            collective_id=0, has_side_effects=True, vmem_limit_bytes=56 * 1024 * 1024
        ),
        name="barotropic_solve",
    )(
        depth,
        cell_dx,
        cell_dy,
        forcing,
        land_mask,
        dest_block,
        dest_block.reshape(1, slots),
        neighbours,
    )
    whole = jax.ShapeDtypeStruct((blocks, height, width), f32)
    hbm = pl.BlockSpec(memory_space=pltpu.HBM)
    return pl.pallas_call(
        finish,
        out_shape=(whole, whole),
        in_specs=[vmem, vmem, vmem, vmem, [vmem] * len(LATE)],
        out_specs=(hbm, hbm),
        scratch_shapes=[
            tiles(blocks, height - TOP),
            tiles(blocks, height - TOP),
            dma((4,)),
        ],
        compiler_params=pltpu.CompilerParams(vmem_limit_bytes=16 * 1024 * 1024),
        name="barotropic_finish",
    )(*parts)


def solution(mesh):
    blocks3 = P(("blk", "grp"), None, None)
    flat = P(("blk", "grp"))
    in_specs = (blocks3,) * 5 + (flat, flat, P(("blk", "grp"), None))
    return jax.shard_map(
        functools.partial(per_device, mesh.shape["blk"], mesh.shape["grp"]),
        mesh=mesh,
        in_specs=in_specs,
        out_specs=(blocks3, blocks3),
        check_vma=False,
    )
```

```python
import functools

import jax
import jax.numpy as jnp
from jax import lax
from jax.experimental import pallas as pl
from jax.experimental.pallas import tpu as pltpu
from jax.sharding import PartitionSpec as P

SWEEPS = 4
TAU_MASS = 6.0
LOW_BOUND = 0.2
HIGH_BOUND = 1.9
CHUNK = 32
PAD = 8
GATHER = 16
PAIR = 4
EARLY = ((0, 16), (16, 16), (32, 16))
DEEP = 48
TOP = DEEP - 8
NEW = ((0, 24), (24, 24))
LATE = ((40, 32), (72, 32), (104, 24))
WINDOWS = len(EARLY)
STEPS = ((32, 40), (72, 32), (104, 24))
MESH = pl.DeviceIdType.MESH
EXACT = lax.Precision.HIGHEST


def pick_dot(pick, data):
    pick = pick.astype(jnp.bfloat16)
    total = None
    for _ in range(3):
        part = data.astype(jnp.bfloat16)
        data = data - part.astype(jnp.float32)
        term = jnp.dot(pick, part, preferred_element_type=jnp.float32)
        total = term if total is None else total + term
    return total


def relax_weights():
    alpha = 2.0 / (HIGH_BOUND - LOW_BOUND)
    beta = (HIGH_BOUND + LOW_BOUND) / (HIGH_BOUND - LOW_BOUND)
    gamma = beta / alpha
    weight = 2.0 / gamma
    weights = []
    for _ in range(SWEEPS - 1):
        weight = 1.0 / (gamma - weight / (4.0 * alpha**2))
        weights.append((weight, gamma * weight - 1.0))
    return gamma, weights


def kernel(
    owners,
    bands,
    depth_hbm,
    dx_hbm,
    dy_hbm,
    forcing_hbm,
    mask_hbm,
    dest_smem,
    dest_row,
    neigh,
    sol_out,
    res_out,
    fix_cols,
    fix_rows,
    cross_in,
    depth_v,
    dx_v,
    dy_v,
    forcing_v,
    mask_v,
    coef_x,
    coef_y,
    coef_d,
    inv_d,
    source,
    update,
    field,
    resid,
    pick_rows,
    pick_cols,
    first_rows,
    first_cols,
    band_first,
    side_first,
    edge_rows,
    edge_cols,
    band_rows,
    side_cols,
    col_tile,
    col_turned,
    row_raw,
    row_coefs,
    col_coefs,
    inner_cols,
    filled,
    halo_cols,
    new_top,
    new_coefs,
    new_inv,
    new_update,
    new_field,
    fix_source,
    fix_out,
    fix_in,
    patch_cols,
    find,
    have,
    near_out,
    near_in,
    far_out,
    far_in,
    late_out,
    late_in,
    cross_out,
    load_sems,
    row_send,
    row_recv,
    col_send,
    col_recv,
    early_send,
    early_recv,
    late_send,
    late_recv,
    fix_send,
    fix_recv,
):
    slots, height, width = depth_v.shape
    blocks = neigh.shape[0]
    tall = 2 * slots
    me = lax.axis_index("blk")
    band = lax.axis_index("grp")
    core = me % 2
    sibling = me + 1 - 2 * core
    base = me - me % 4
    inner = me % 4
    across = base + (inner + 2) % 4
    east_band = (band + 1) % bands
    west_band = (band + bands - 1) % bands

    loads = [
        pltpu.make_async_copy(
            src.at[:, pl.ds(h * (height // 2), height // 2), :],
            dst.at[:, pl.ds(h * (height // 2), height // 2), :],
            load_sems.at[5 * h + i],
        )
        for h in range(2)
        for i, (src, dst) in enumerate(
            (
                (dx_hbm, dx_v),
                (dy_hbm, dy_v),
                (depth_hbm, depth_v),
                (mask_hbm, mask_v),
                (forcing_hbm, forcing_v),
            )
        )
    ]
    barrier = pltpu.get_barrier_semaphore()
    wrap = (band == 0).astype(jnp.int32)
    far_band = west_band * wrap + east_band * (1 - wrap)
    other_band = east_band * wrap + west_band * (1 - wrap)
    for side in (far_band, other_band):
        for step in (2, 3, 1, 0):
            pl.semaphore_signal(
                barrier,
                inc=1,
                device_id=(base + (inner + step) % 4, side),
                device_id_type=MESH,
            )
    for step in range(1, owners):
        pl.semaphore_signal(
            barrier, inc=1, device_id=((me + step) % owners, band), device_id_type=MESH
        )

    for load in loads:
        load.start()

    first_rows[tall:, :] = jnp.zeros((8, width), jnp.float32)
    first_rows[tall : tall + blocks, 0:8] = (neigh[...] + 1).astype(jnp.float32)
    first_rows[tall + blocks : tall + blocks + 1, 0:slots] = (dest_row[...] + 1).astype(
        jnp.float32
    )
    table = first_rows[tall:, :]
    first_cols[0, slots:, :] = table
    first_cols[1, slots:, :] = table

    targets = (me, sibling, across, base + (sibling % 4 + 2) % 4)
    for t, target in enumerate(targets):
        for j in range(blocks):
            wanted = (target * bands + band) * blocks + j
            place = jnp.int32(0)
            count = jnp.int32(0)
            for s in range(slots):
                hit = dest_smem[s] == wanted
                place = jnp.where(hit, s, place)
                count = jnp.where(hit, 1, count)
            find[t * blocks + j] = place
            have[t * blocks + j] = count.astype(jnp.float32)

    gamma, weights = relax_weights()

    def coefficients(dx, dy, deep, src):
        area = dx * dy
        scaled = deep / area
        cx = scaled * (dy * dy)
        cy = scaled * (dx * dx)
        cd = 2.5 * (cx + cy) + TAU_MASS * area
        inv = 1.0 / cd
        return cx, cy, cd, inv, src, src * (inv * (1.0 / gamma))

    def gather(r, carry):
        rows = pl.ds(pl.multiple_of(r * GATHER, GATHER), GATHER)
        quad = lax.broadcasted_iota(jnp.int32, (GATHER, width), 1) // 4
        tile = jnp.zeros((GATHER, width), jnp.float32)
        for s in range(slots):
            ocean = mask_v[s, rows, :].astype(jnp.float32)
            parts = (
                dx_v[s, rows, :],
                dy_v[s, rows, :],
                depth_v[s, rows, :] * ocean,
                forcing_v[s, rows, :] * ocean,
            )
            for i, part in enumerate(parts):
                at = i * slots + s
                tile = jnp.where(quad == at, pltpu.roll(part, 2 + 4 * at, 1), tile)
        col_tile[rows, :] = tile
        return carry

    part = height // GATHER // 2
    for h in range(2):
        for load in loads[5 * h : 5 * h + 5]:
            load.wait()
        lax.fori_loop(h * part, (h + 1) * part, gather, 0)
    col_turned[...] = col_tile[...].T
    for i, ref in enumerate((dx_v, dy_v, depth_v, forcing_v, mask_v)):
        for s in range(slots):
            for at, row in ((s, 0), (slots + s, height - 1)):
                value = ref[s, row : row + 1, :]
                row_raw[i, at : at + 1, :] = value.astype(jnp.float32)
    sides_of = [
        [col_turned[pl.ds(4 * slots * i + c, slots, stride=4), :] for i in range(4)]
        for c in range(4)
    ]
    for i, part in enumerate(
        coefficients(*(jnp.concatenate([e, w], axis=0) for e, w in zip(sides_of[1], sides_of[2])))
    ):
        col_coefs[i * tall : (i + 1) * tall, :] = part
    start = coefficients(
        *(jnp.concatenate([e, w], axis=0) for e, w in zip(sides_of[0], sides_of[3]))
    )[5]
    inner_cols[...] = start
    ocean = row_raw[4]
    for i, part in enumerate(
        coefficients(row_raw[0], row_raw[1], row_raw[2] * ocean, row_raw[3] * ocean)
    ):
        row_coefs[i] = part
    edge_rows[0] = row_coefs[5]
    edge_cols[0] = col_coefs[5 * tall : 6 * tall, :].reshape(2, slots, width)
    first_rows[0:tall, :] = row_coefs[5]
    first_cols[0, 0:slots, :] = col_coefs[5 * tall + slots : 6 * tall, :]
    first_cols[1, 0:slots, :] = col_coefs[5 * tall : 5 * tall + slots, :]

    def prepare(r0):
        rows = pl.ds(r0, CHUNK)

        def one(s, carry):
            ocean = mask_v[s, rows, :].astype(jnp.float32)
            parts = coefficients(
                dx_v[s, rows, :],
                dy_v[s, rows, :],
                depth_v[s, rows, :] * ocean,
                forcing_v[s, rows, :] * ocean,
            )
            for ref, part in zip((coef_x, coef_y, coef_d, inv_d, source, update), parts):
                ref[s, rows, :] = part
            field[0, s, pl.ds(PAD + r0, CHUNK), :] = parts[5]
            return carry

        lax.fori_loop(0, slots, one, 0)

    def send_cols(k):
        wrap = (band == 0).astype(jnp.int32)
        sides = ((wrap, west_band * wrap + east_band * (1 - wrap)),)
        sides = sides + ((1 - wrap, east_band * wrap + west_band * (1 - wrap)),)
        for to_west, side in sides:
            for step in (2, 3, 1, 0):
                slot = step + 4 * (1 - to_west)
                if k == 0:
                    src, dst = first_cols.at[1 - to_west], side_first.at[slot]
                else:
                    src, dst = edge_cols.at[k, to_west], side_cols.at[k - 1, slot]
                pltpu.make_async_remote_copy(
                    src_ref=src,
                    dst_ref=dst,
                    send_sem=col_send.at[k],
                    recv_sem=col_recv.at[k],
                    device_id=(base + (inner + step) % 4, side),
                    device_id_type=MESH,
                ).start()

    def send_rows(k):
        for step in range(1, owners):
            if k == 0:
                src, dst = first_rows, band_first.at[owners - step]
            else:
                src, dst = edge_rows.at[k], band_rows.at[k - 1, owners - step]
            pltpu.make_async_remote_copy(
                src_ref=src,
                dst_ref=dst,
                send_sem=row_send.at[k],
                recv_sem=row_recv.at[k],
                device_id=((me + step) % owners, band),
                device_id_type=MESH,
            ).start()
        if k == 0:
            band_first[0] = first_rows[...]
        else:
            band_rows[k - 1, 0] = edge_rows[k]

    def take(ref, sem):
        pltpu.make_async_copy(ref, ref, sem).wait()

    def rows_landed(k):
        return (band_first if k == 0 else band_rows.at[k - 1]).at[pl.ds(1, owners - 1)]

    def cols_landed(k):
        return side_first if k == 0 else side_cols.at[k - 1]

    def build_picks():
        lanes = lax.broadcasted_iota(jnp.int32, (tall, width), 1)
        rows = lax.broadcasted_iota(jnp.int32, (tall, width), 0)
        ids_here = first_rows[tall:, :]
        mine = jnp.broadcast_to(ids_here[blocks : blocks + 1, :], (tall, width))
        own = jnp.sum(jnp.where(lanes == rows % slots, mine, 0.0), axis=1, keepdims=True)
        group_ids = ((base + lanes // 8) * bands + band) * blocks + lanes % 8 + 1
        known = (lanes % 8 < blocks) & (lanes < 32)
        match = jnp.where(known & (own == group_ids.astype(jnp.float32)), 1.0, 0.0)
        listed = jnp.concatenate(
            [band_first[(base + g - me + owners) % owners, tall:, :] for g in range(4)], axis=0
        )
        need = jnp.dot(
            match[:, :32], listed, precision=EXACT, preferred_element_type=jnp.float32
        )
        all_rows = tall + 2 * blocks
        lanes = lax.broadcasted_iota(jnp.int32, (all_rows, width), 1)
        rows = lax.broadcasted_iota(jnp.int32, (all_rows, width), 0)
        second = ((rows >= slots) & (rows < tall)) | (rows >= tall + blocks)
        lower = rows[0:tall] >= slots
        low = lax.broadcasted_iota(jnp.int32, (8, width), 1) < slots
        per_tile = width // tall
        wanted = jnp.concatenate(
            [
                jnp.where(lower, need[:, 1:2], need[:, 0:1]),
                jnp.broadcast_to(ids_here[0:blocks, 0:1], (blocks, width)),
                jnp.broadcast_to(ids_here[0:blocks, 1:2], (blocks, width)),
            ],
            axis=0,
        )
        for q in range(owners // per_tile):
            ids = jnp.zeros((8, width), jnp.float32)
            for d in range(per_tile):
                tile = jnp.where(low, band_first[q * per_tile + d, tall:, :], 0.0)
                twice = tile + pltpu.roll(tile, slots, 1)
                ids = ids + (pltpu.roll(twice, tall * d, 1) if d else twice)
            id_row = jnp.broadcast_to(ids[blocks : blocks + 1, :], (all_rows, width))
            bottom = (lanes % tall) // slots == 1
            good = (wanted == id_row) & (id_row > 0.0) & (bottom != second)
            pick_rows[:, q * width : (q + 1) * width] = jnp.where(good, 1.0, 0.0)
        ids = jnp.zeros((8, width), jnp.float32)
        for d in range(8):
            tile = jnp.where(low, side_first[d, slots:, :], 0.0)
            ids = ids + (pltpu.roll(tile, slots * d, 1) if d else tile)
        id_row = jnp.broadcast_to(ids[blocks : blocks + 1, :], (all_rows, width))
        western = lanes >= 4 * slots
        for i, (east_of, west_of) in enumerate(((2, 3), (4, 5), (6, 7))):
            wanted = jnp.concatenate(
                [
                    jnp.where(
                        lower, need[:, west_of : west_of + 1], need[:, east_of : east_of + 1]
                    ),
                    jnp.broadcast_to(ids_here[0:blocks, east_of : east_of + 1], (blocks, width)),
                    jnp.broadcast_to(ids_here[0:blocks, west_of : west_of + 1], (blocks, width)),
                ],
                axis=0,
            )
            good = (wanted == id_row) & (id_row > 0.0) & (western == second)
            pick_cols[all_rows * i : all_rows * (i + 1), :] = jnp.where(good, 1.0, 0.0)

    all_rows = tall + 2 * blocks
    lanes = lax.broadcasted_iota(jnp.int32, (tall, width), 1)
    start = lanes == 0
    end = lanes == width - 1

    def take_rows(k):
        take(rows_landed(k), row_recv.at[k])
        if k == 0:
            take(cols_landed(k), col_recv.at[k])
            build_picks()
        per_tile = width // tall
        got = jnp.zeros((all_rows, width), jnp.float32)
        for q in range(owners // per_tile):
            part = pl.ds(q * per_tile, per_tile)
            edges = band_first[part, 0:tall, :] if k == 0 else band_rows[k - 1, part]
            got = got + pick_dot(
                pick_rows[:, q * width : (q + 1) * width], edges.reshape(width, width)
            )
        return got

    def take_cols(k):
        if k:
            take(cols_landed(k), col_recv.at[k])
        count = 8 * slots
        edges = side_first[:, 0:slots, :] if k == 0 else side_cols[k - 1]
        cols = pick_dot(pick_cols[:, 0:count], edges.reshape(count, width))
        at = lax.broadcasted_iota(jnp.int32, (all_rows, width), 1)
        straight = cols[0:all_rows]
        above = jnp.where(at == width - 1, cols[all_rows : 2 * all_rows], straight)
        below = jnp.where(at == 0, cols[2 * all_rows : 3 * all_rows], straight)
        slanted = pltpu.roll(above, 1, 1) + pltpu.roll(below, width - 1, 1)
        return straight, slanted

    def put_halo(k, got, straight, slanted):
        now = k % 2
        if k < SWEEPS - 1:
            for s in range(slots):
                field[now, s, PAD - 1 : PAD, :] = got[s : s + 1, :]
                field[now, s, PAD + height : PAD + height + 1, :] = got[
                    slots + s : slots + s + 1, :
                ]
        new_top[k] = got[tall:]
        for i, tile in enumerate((straight, slanted)):
            for h in range(2):
                filled[pl.ds(tall * i + h, slots, stride=2), :] = tile[slots * h : slots * (h + 1)]
                filled[pl.ds(2 * tall + 2 * blocks * i + h, blocks, stride=2), :] = tile[
                    tall + blocks * h : tall + blocks * (h + 1)
                ]
        halo_cols[k] = filled[...].T

    def exchange(k):
        now = k % 2
        every = take_rows(k)
        got = every[0:tall]

        def spread(value, before, after):
            left = jnp.where(start, before, pltpu.roll(value, 1, 1))
            return left + jnp.where(end, after, pltpu.roll(value, width - 1, 1))

        def ends(tile, at):
            part = tile[at : at + slots]
            return jnp.concatenate([part[:, 0:1], part[:, width - 1 : width]], axis=0)

        def sides(at, deep):
            part = got[at : at + slots]
            far = width - 1 - deep
            return jnp.concatenate([part[:, far : far + 1], part[:, deep : deep + 1]], axis=0)

        def known(coefs, center, level, vertical, slant):
            cx, cy, cd, _, src = coefs
            slant = 0.125 * slant
            return src - cd * center + cx * (level + slant) + cy * (vertical + slant)

        col_now = [col_coefs[i * tall : (i + 1) * tall, :] for i in range(5)]
        center = edge_cols[k].reshape(tall, width)
        inside = inner_cols[...]
        vertical = spread(center, sides(0, 0), sides(slots, 0))
        slant = spread(inside, sides(0, 1), sides(slots, 1))
        col_part = known(col_now, center, inside, vertical, slant)
        col_slant = 0.125 * (col_now[0] + col_now[1])

        row_now = [row_coefs[i] for i in range(5)]
        row_center = edge_rows[k]
        inside = jnp.concatenate(
            [field[now, s, PAD + 1 : PAD + 2, :] for s in range(slots)]
            + [field[now, s, PAD + height - 2 : PAD + height - 1, :] for s in range(slots)],
            axis=0,
        )
        vertical = inside + got
        level = spread(row_center, 0.0, 0.0)
        slant = spread(vertical, 0.0, 0.0)
        row_part = known(row_now, row_center, level, vertical, slant)
        row_slant = 0.125 * (row_now[0] + row_now[1])
        if k < SWEEPS - 1:
            weight, keep = weights[k]
            col_scale = weight * col_now[3]
            row_scale = weight * row_now[3]
            col_keep = keep * col_coefs[5 * tall : 6 * tall, :]
            row_keep = keep * row_coefs[5]

        straights, slants = take_cols(k)
        straight, slanted = straights[0:tall], slants[0:tall]
        left = col_part + col_now[0] * straight + col_slant * slanted
        if k == SWEEPS - 1:
            fix_source[slots : 3 * slots, :] = left
        else:
            change = col_scale * left + col_keep
            col_coefs[5 * tall : 6 * tall, :] = change
            edge_cols[k + 1] = (center + change).reshape(2, slots, width)
            send_cols(k + 1)

        def outer(tile):
            before, after = ends(tile, slots), ends(tile, 0)
            return jnp.where(start, before, 0.0) + jnp.where(end, after, 0.0)

        left = row_part + row_now[0] * outer(straight) + row_slant * outer(slanted)
        if k == SWEEPS - 1:
            fix_source[0:slots, :] = left[slots:]
        else:
            change = row_scale * left + row_keep
            row_coefs[5] = change
            edge_rows[k + 1] = row_center + change
            send_rows(k + 1)
        return every, straights, slants

    def around(value, halo):
        at = lax.broadcasted_iota(jnp.int32, value.shape, 1)
        left = jnp.where(at == 0, halo, pltpu.roll(value, 1, 1))
        right = jnp.where(at == width - 1, halo, pltpu.roll(value, width - 1, 1))
        return left + right

    def balance(f, s, r0, size, level, vertical, slant):
        rows = pl.ds(r0, size)
        slant = 0.125 * slant
        return (
            source[s, rows, :]
            - coef_d[s, rows, :] * field[f, s, pl.ds(PAD + r0, size), :]
            + coef_x[s, rows, :] * (level + slant)
            + coef_y[s, rows, :] * (vertical + slant)
        )

    def columns(f, s, r0, size):
        center = field[f, s, pl.ds(PAD + r0, size), :]
        north = field[f, s, pl.ds(PAD + r0 - 1, size), :]
        south = field[f, s, pl.ds(PAD + r0 + 1, size), :]
        return center, north + south

    def sweep(k, pieces, group, closed=True):
        now = k % 2
        weight, keep = weights[k]
        for r0, size in pieces:
            rows = pl.ds(r0, size)
            cols = halo_cols[k, rows, :] if closed else None
            for first in range(0, slots, group):
                done = []
                for s in range(first, first + group):
                    center, vertical = columns(now, s, r0, size)
                    if closed:
                        level = around(center, pltpu.roll(cols, width - 1 - 2 * s, 1))
                        slant = around(vertical, pltpu.roll(cols, width - 1 - tall - 2 * s, 1))
                    else:
                        level, slant = beside(center), beside(vertical)
                    left = balance(now, s, r0, size, level, vertical, slant)
                    change = weight * left * inv_d[s, rows, :] + keep * update[s, rows, :]
                    done.append((s, change, center + change))
                for s, change, fresh in done:
                    update[s, rows, :] = change
                    field[1 - now, s, pl.ds(PAD + r0, size), :] = fresh

    def beside(value):
        return pltpu.roll(value, 1, 1) + pltpu.roll(value, width - 1, 1)

    def capture(first, load):
        quad = lax.broadcasted_iota(jnp.int32, (CHUNK, width), 1) // 4
        for r0 in range(first, height, CHUNK):
            tile = jnp.zeros((CHUNK, width), jnp.float32)
            for s in range(slots):
                tile = jnp.where(quad == s, pltpu.roll(load(s, r0), 2 + 4 * s, 1), tile)
            col_tile[pl.ds(r0, CHUNK), :] = tile
        col_turned[...] = col_tile[...].T

    def turn_columns(f, first=0):
        capture(first, lambda s, r0: field[f, s, pl.ds(PAD + r0, CHUNK), :])
        for h in range(2):
            inner_cols[slots * h : slots * (h + 1), :] = col_turned[
                pl.ds(3 * h, slots, stride=4), :
            ]

    last = (SWEEPS - 1) % 2

    def remainder(r0, size, group):
        for first in range(0, slots, group):
            done = []
            for s in range(first, first + group):
                center, vertical = columns(last, s, r0, size)
                level, slant = beside(center), beside(vertical)
                done.append((s, balance(last, s, r0, size, level, vertical, slant)))
            for s, left in done:
                resid[s, pl.ds(r0, size), :] = left

    def send_to(src, dst, sends, recvs, at, device):
        pltpu.make_async_remote_copy(
            src_ref=src,
            dst_ref=dst,
            send_sem=sends.at[at],
            recv_sem=recvs.at[at],
            device_id=(device, band),
            device_id_type=MESH,
        ).start()

    early = (coef_x, coef_y, coef_d, source)

    def early_start(w):
        rows = pl.ds(*EARLY[w])

        def fill(i, carry):
            for t in range(2):
                at = (1 + 2 * t) * blocks + i
                slot, live = find[at], have[at]
                for f, ref in enumerate(early):
                    near_out[w][f, t * blocks + i] = ref[slot, rows, :] * live
            return carry

        lax.fori_loop(0, blocks, fill, 0)
        send_to(near_out[w], near_in[w], early_send, early_recv, w, sibling)

    def early_cross(w):
        rows = pl.ds(*EARLY[w])
        take(near_in[w], early_recv.at[w])

        def fill(i, carry):
            at = 2 * blocks + i
            slot, live = find[at], have[at]
            for f, ref in enumerate(early):
                far_out[w][f, i] = ref[slot, rows, :] * live + near_in[w][f, blocks + i]
            return carry

        lax.fori_loop(0, blocks, fill, 0)
        send_to(far_out[w], far_in[w], early_send, early_recv, WINDOWS + w, across)

    def early_finish(w):
        rows = pl.ds(*EARLY[w])
        take(far_in[w], early_recv.at[WINDOWS + w])

        def fill(i, carry):
            slot, live = find[i], have[i]
            for f, ref in enumerate(early):
                new_coefs[f, i, rows, :] = (
                    ref[slot, rows, :] * live + near_in[w][f, i] + far_in[w][f, i]
                )
            inv = 1.0 / new_coefs[2, i, rows, :]
            new_inv[i, rows, :] = inv
            start = new_coefs[3, i, rows, :] * (inv * (1.0 / gamma))
            new_update[i, rows, :] = start
            new_field[0, i, pl.ds(PAD + EARLY[w][0], EARLY[w][1]), :] = start
            return carry

        lax.fori_loop(0, blocks, fill, 0)

    def new_sweep(k):
        now = k % 2
        for i in range(blocks):
            new_field[now, i, PAD - 1 : PAD, :] = new_top[k, i : i + 1, :]
        for r0, size in NEW:
            rows = pl.ds(r0, size)
            cols = halo_cols[k, rows, :]
            done = []
            for i in range(blocks):
                center = new_field[now, i, pl.ds(PAD + r0, size), :]
                vertical = (
                    new_field[now, i, pl.ds(PAD + r0 - 1, size), :]
                    + new_field[now, i, pl.ds(PAD + r0 + 1, size), :]
                )
                level = around(center, pltpu.roll(cols, width - 1 - 2 * tall - 2 * i, 1))
                slant = around(
                    vertical, pltpu.roll(cols, width - 1 - 2 * tall - 2 * blocks - 2 * i, 1)
                )
                slant = 0.125 * slant
                left = (
                    new_coefs[3, i, rows, :]
                    - new_coefs[2, i, rows, :] * center
                    + new_coefs[0, i, rows, :] * (level + slant)
                    + new_coefs[1, i, rows, :] * (vertical + slant)
                )
                if k == SWEEPS - 1:
                    done.append((left, None))
                else:
                    weight, keep = weights[k]
                    change = weight * left * new_inv[i, rows, :] + keep * new_update[i, rows, :]
                    done.append((center + change, change))
            kept = min(size, TOP - r0)
            for i, (fresh, change) in enumerate(done):
                if k == SWEEPS - 1:
                    res_out[i, pl.ds(r0, kept), :] = fresh[0:kept]
                else:
                    new_update[i, rows, :] = change
                    new_field[1 - now, i, pl.ds(PAD + r0, size), :] = fresh
                    if k == SWEEPS - 2:
                        sol_out[i, pl.ds(r0, kept), :] = fresh[0:kept]

    def rows_of(f, slot, r0, count):
        if f == 0:
            return field[last, slot, pl.ds(PAD + r0, count), :]
        return resid[slot, pl.ds(r0, count), :]

    def late_start(f, c):
        r0, count = LATE[c]

        def fill(i, carry):
            for t in range(2):
                at = (1 + 2 * t) * blocks + i
                late_out[c][f, t * blocks + i] = rows_of(f, find[at], r0, count) * have[at]
            return carry

        lax.fori_loop(0, blocks, fill, 0)
        at = f * len(LATE) + c
        send_to(late_out[c].at[f], late_in[c].at[f], late_send, late_recv, at, sibling)

    def late_cross(f, c):
        r0, count = LATE[c]
        at = f * len(LATE) + c
        take(late_in[c].at[f], late_recv.at[at])

        def fill(i, carry):
            at = 2 * blocks + i
            cross_out[c][f, i] = (
                rows_of(f, find[at], r0, count) * have[at] + late_in[c][f, blocks + i]
            )
            return carry

        lax.fori_loop(0, blocks, fill, 0)
        at = at + 2 * len(LATE)
        send_to(cross_out[c].at[f], cross_in[c].at[f], late_send, late_recv, at, across)

    def late_near(f, c, out):
        r0, count = LATE[c]

        def fill(i, carry):
            out[i, pl.ds(r0, count), :] = (
                rows_of(f, find[i], r0, count) * have[i] + late_in[c][f, i]
            )
            return carry

        lax.fori_loop(0, blocks, fill, 0)

    def patch():
        for h in range(2):
            filled[pl.ds(h, slots, stride=2), :] = edge_cols[SWEEPS - 1, h]
        patch_cols[...] = filled[...].T
        r0, size = STEPS[0]
        cols = patch_cols[pl.ds(r0, size), :]
        rows = pl.ds(PAD + r0, size)
        at = lax.broadcasted_iota(jnp.int32, (size, width), 1)
        edge = (at == 0) | (at == width - 1)
        for s in range(slots):
            sides = pltpu.roll(cols, width - 1 - 2 * s, 1)
            field[last, s, rows, :] = jnp.where(edge, sides, field[last, s, rows, :])

    def send_fix():
        fix_source[3 * slots :, :] = edge_cols[SWEEPS - 1].reshape(tall, width)
        fix_out[...] = jnp.zeros_like(fix_out)
        for t in range(4):
            for i in range(blocks):
                slot, live = find[t * blocks + i], have[t * blocks + i]
                places = (2 * blocks + i, 2 * i, 2 * i + 1, 3 * blocks + 2 * i, 3 * blocks + 2 * i + 1)
                for j, at in enumerate(places):
                    value = fix_source[pl.ds(slots * j + slot, 1), :]
                    fix_out[t, at : at + 1, :] = value * live
        for t in range(1, 4):
            send_to(fix_out.at[t], fix_in.at[t - 1], fix_send, fix_recv, t - 1, targets[t])

    def take_fix():
        for t in range(3):
            take(fix_in.at[t], fix_recv.at[t])
        total = fix_out[0] + fix_in[0] + fix_in[1] + fix_in[2]
        filled[0 : 6 * blocks, :] = total
        fix_cols[...] = filled[...].T
        fix_rows[...] = total

    for f in range(2):
        new_field[f] = jnp.zeros(new_field.shape[1:], jnp.float32)

    filled[...] = jnp.zeros_like(filled)
    pl.semaphore_wait(barrier, owners - 1 + 8)
    send_cols(0)
    send_rows(0)
    whole = tuple(range(0, height, CHUNK))
    prepare(whole[0])
    early_start(0)
    prepare(whole[1])
    for w in range(1, WINDOWS):
        early_start(w)
    early_cross(0)
    for r0 in whole[2:]:
        prepare(r0)
    for k in range(SWEEPS - 2):
        halo = exchange(k)
        early_cross(k + 1)
        put_halo(k, *halo)
        sweep(k, [(r0, CHUNK) for r0 in whole], PAIR)
        turn_columns(1 - k % 2)
    k = SWEEPS - 2
    steps = len(LATE)
    sweep(k, (STEPS[0],), PAIR, closed=False)
    late_start(0, 0)
    halo = exchange(k)
    for w in range(SWEEPS - 1, WINDOWS):
        early_cross(w)
    late_cross(0, 0)
    put_halo(k, *halo)
    patch()
    for c in range(1, steps):
        sweep(k, (STEPS[c],), PAIR)
        late_start(0, c)
        if c > 1:
            late_cross(0, c - 1)
    turn_columns(last)
    for c in range(steps):
        remainder(*LATE[c], PAIR)
        late_start(1, c)
        if c:
            late_cross(1, c - 1)
        else:
            late_cross(0, steps - 1)
    for w in range(WINDOWS):
        early_finish(w)
    for k in range(SWEEPS - 1):
        new_sweep(k)
    for f, out in enumerate((sol_out, res_out)):
        for c in range(steps - f):
            late_near(f, c, out)
    k = SWEEPS - 1
    halo = exchange(k)
    send_fix()
    late_cross(1, steps - 1)
    put_halo(k, *halo)
    new_sweep(k)
    late_near(1, steps - 1, res_out)
    take_fix()
    for at in range(2 * steps, 4 * steps):
        take(cross_in[at % steps].at[at // steps - 2], late_recv.at[at])

    for k in range(SWEEPS):
        take(rows_landed(k), row_send.at[k])
        take(cols_landed(k), col_send.at[k])
    for w in range(WINDOWS):
        take(near_out[w], early_send.at[w])
        take(far_out[w], early_send.at[WINDOWS + w])
    for f in range(2):
        for c in range(steps):
            take(late_out[c].at[f], late_send.at[f * steps + c])
            take(cross_out[c].at[f], late_send.at[(2 + f) * steps + c])
    for t in range(3):
        take(fix_in.at[t], fix_send.at[t])


def finish(near_sol, near_res, fix_cols, fix_rows, cross, sol_out, res_out, sol_v, res_v, sems):
    blocks, height, width = near_sol.shape
    top = pl.ds(0, TOP)
    rest = pl.ds(TOP, height - TOP)
    pairs = ((near_sol, sol_v, sol_out), (near_res, res_v, res_out))
    copies = []
    for f, (near, _, out) in enumerate(pairs):
        copies.append(
            pltpu.make_async_copy(near.at[:, top, :], out.at[:, top, :], sems.at[2 * f])
        )
        copies[-1].start()
    for f, (near, value_v, out) in enumerate(pairs):
        for c, (r0, count) in enumerate(LATE):
            rows = pl.ds(r0, count)
            at = lax.broadcasted_iota(jnp.int32, (count, width), 1)
            edge = (at == 0) | (at == width - 1)
            for i in range(blocks):
                value = near[i, rows, :] + cross[c][f, i]
                if f or not c:
                    first = 0 if f else 3 * blocks
                    cols = pltpu.roll(fix_cols[rows, :], width - 1 - first - 2 * i, 1)
                    value = jnp.where(edge, cols, value)
                value_v[i, pl.ds(r0 - TOP, count), :] = value
        if f:
            for i in range(blocks):
                at = 2 * blocks + i
                value_v[i, height - TOP - 1 : height - TOP, :] = fix_rows[at : at + 1, :]
        copies.append(pltpu.make_async_copy(value_v, out.at[:, rest, :], sems.at[2 * f + 1]))
        copies[-1].start()
    for copy in copies:
        copy.wait()


def per_device(
    owners, bands, depth, cell_dx, cell_dy, forcing, land_mask, dest_block, source_slot, neighbours
):
    slots, height, width = depth.shape
    blocks = source_slot.shape[0]
    tall = 2 * slots
    f32 = jnp.float32
    hbm = pl.BlockSpec(memory_space=pl.ANY)
    vmem = pl.BlockSpec(memory_space=pltpu.VMEM)
    whole = pltpu.VMEM((slots, height, width), f32)
    dma = pltpu.SemaphoreType.DMA

    def tiles(*shape):
        return pltpu.VMEM((*shape, width), f32)

    out = tiles(blocks, height)
    cross = [tiles(2, blocks, count) for _, count in LATE]
    parts = pl.pallas_call(
        functools.partial(kernel, owners, bands),
        out_shape=(out, out, tiles(height), tiles(6 * blocks), cross),
        in_specs=[hbm] * 5 + [pl.BlockSpec(memory_space=pltpu.SMEM), vmem, vmem],
        out_specs=(vmem, vmem, vmem, vmem, [vmem] * len(LATE)),
        scratch_shapes=[
            whole,
            whole,
            whole,
            whole,
            pltpu.VMEM((slots, height, width), jnp.int32),
            whole,
            whole,
            whole,
            whole,
            whole,
            whole,
            tiles(2, slots, height + 2 * PAD),
            whole,
            pltpu.VMEM((tall + 2 * blocks, owners * tall), f32),
            tiles(3 * (tall + 2 * blocks)),
            tiles(tall + 8),
            tiles(2, slots + 8),
            tiles(owners, tall + 8),
            tiles(8, slots + 8),
            tiles(SWEEPS, tall),
            tiles(SWEEPS, 2, slots),
            tiles(SWEEPS - 1, owners, tall),
            tiles(SWEEPS - 1, 8, slots),
            tiles(height),
            pltpu.VMEM((width, height), f32),
            tiles(5, tall),
            tiles(6, tall),
            pltpu.VMEM((width, height), f32),
            tiles(tall),
            pltpu.VMEM((width, height), f32),
            tiles(SWEEPS, height),
            tiles(SWEEPS, 2 * blocks),
            tiles(4, blocks, DEEP),
            tiles(blocks, DEEP),
            tiles(blocks, DEEP),
            tiles(2, blocks, DEEP + 2 * PAD),
            tiles(5 * slots),
            tiles(4, 6 * blocks),
            tiles(3, 6 * blocks),
            pltpu.VMEM((width, height), f32),
            pltpu.SMEM((4 * blocks,), jnp.int32),
            pltpu.SMEM((4 * blocks,), f32),
            [tiles(4, 2 * blocks, count) for _, count in EARLY],
            [tiles(4, 2 * blocks, count) for _, count in EARLY],
            [tiles(4, blocks, count) for _, count in EARLY],
            [tiles(4, blocks, count) for _, count in EARLY],
            [tiles(2, 2 * blocks, count) for _, count in LATE],
            [tiles(2, 2 * blocks, count) for _, count in LATE],
            [tiles(2, blocks, count) for _, count in LATE],
            dma((10,)),
            dma((SWEEPS,)),
            dma((SWEEPS,)),
            dma((SWEEPS,)),
            dma((SWEEPS,)),
            dma((2 * WINDOWS,)),
            dma((2 * WINDOWS,)),
            dma((4 * len(LATE),)),
            dma((4 * len(LATE),)),
            dma((3,)),
            dma((3,)),
        ],
        compiler_params=pltpu.CompilerParams(
            collective_id=0, has_side_effects=True, vmem_limit_bytes=56 * 1024 * 1024
        ),
        name="barotropic_solve",
    )(
        depth,
        cell_dx,
        cell_dy,
        forcing,
        land_mask,
        dest_block,
        dest_block.reshape(1, slots),
        neighbours,
    )
    whole = jax.ShapeDtypeStruct((blocks, height, width), f32)
    hbm = pl.BlockSpec(memory_space=pltpu.HBM)
    return pl.pallas_call(
        finish,
        out_shape=(whole, whole),
        in_specs=[vmem, vmem, vmem, vmem, [vmem] * len(LATE)],
        out_specs=(hbm, hbm),
        scratch_shapes=[
            tiles(blocks, height - TOP),
            tiles(blocks, height - TOP),
            dma((4,)),
        ],
        compiler_params=pltpu.CompilerParams(vmem_limit_bytes=16 * 1024 * 1024),
        name="barotropic_finish",
    )(*parts)


def solution(mesh):
    blocks3 = P(("blk", "grp"), None, None)
    flat = P(("blk", "grp"))
    in_specs = (blocks3,) * 5 + (flat, flat, P(("blk", "grp"), None))
    return jax.shard_map(
        functools.partial(per_device, mesh.shape["blk"], mesh.shape["grp"]),
        mesh=mesh,
        in_specs=in_specs,
        out_specs=(blocks3, blocks3),
        check_vma=False,
    )
```
